32 devices in a mesh: row: 16 (over z, y, x), col: 2 (over core).
Axes of the slice: x: 2, y: 2, z: 4, core: 2. Of those that a mesh axis runs over, the one named last changes fastest.
Arguments:
- vectors_in: bfloat16 [32768, 2048], P('row', 'col'), may hold values from -6 to 6
- panel: bfloat16 [32768, 256], P('row', 'col'), may hold values from -0.03125 to 0.03125
- factor: float32 [256, 256], replicated, may hold values from -3 to 8, as said below
- atom_basis: int32 [16, 128], P('row'), may hold values from 1 to 24, 2048 in all within a row
- proj_count: int32 [2048], P('row'), may hold values from 1 to 16
- coupling: bfloat16 [2048, 9, 384], P('row'), may hold values from -0.4375 to 0.4375
- block_present: int32 [2048, 9], P('row'), may hold values 0 or 1
- occ_mask: int32 [2048], P('col'), may hold values 0 or 1
- occ_weight: float32 [2048], P('col'), may hold values from 0.5 to 2
Outputs:
- vectors: bfloat16 [32768, 2048], P('row', 'col')
- density: float32 [2048, 256], P(('row', 'col'))
The draws below stay inside these ranges and needn't reach their ends.
Inputs may be any that keep to these rules, and one draw needn't show every extreme that they name: `factor`: zero below the diagonal; the diagonal lies in 4 to 8. `atom_basis`: each row sums to 2048, and 24 is reached in each row.
All inputs are finite; a program needn't handle non-finite values. No bound on the sum of `block_present` or of `occ_mask` on one device may be relied on, other than what follows from the above.
Results may differ from the reference program's by a relative error of at most 0.0075.
Values may be sent and summed in bfloat16 or wider, within the bound.
A program may use at most 192 MiB of HBM per device.

```python
import math
import jax
import jax.numpy as jnp
import numpy as np
from jax import lax

M_DEV = 2048
NB_DEV = 1024
NPAN = 256
NPMAX = 16
BMAX = 24
K = 9
A_DEV = 128
M = 32768
NB = 2048
ATOMS = 2048
N_ROW = 16
N_COL = 2


def draw_factor(key, part):
    key_upper, key_diagonal = jax.random.split(key, 2)
    upper = jnp.clip(jax.random.normal(key_upper, (NPAN, NPAN), jnp.float32), -6.0, 6.0) * 0.5
    diagonal = jax.random.uniform(key_diagonal, (NPAN,), jnp.float32, 4.0, 8.0)
    return jnp.triu(upper, 1) + jnp.diag(diagonal)


def place_ends(values, rng, least, high):
    longest = values.shape.index(max(values.shape))
    spots = []
    for shift in (0, 1):
        where = [jax.random.randint(jax.random.fold_in(rng, axis), (), 0, length) for axis, length in enumerate(values.shape)]
        where[longest] = (where[longest] + shift) % values.shape[longest]
        spots.append(tuple(where))
    return values.at[spots[0]].set(least).at[spots[1]].set(high)


def steps_of(key, dims, cuts, smallest, high):
    level, own = 1.0, jax.random.fold_in(key, 6)
    for axis_at, parts in cuts:
        draws = jnp.exp(jax.random.uniform(jax.random.fold_in(own, axis_at), (parts,), jnp.float32, smallest / len(cuts), high / len(cuts)))
        level = level * jnp.repeat(draws, dims[axis_at] // parts).reshape([-1 if axis == axis_at else 1 for axis in range(len(dims))])
    return level


def split_up(number_of, total, most, skew):
    weights = [(1 << 20) // math.isqrt(rank ** skew) + 1 for rank in range(2, number_of + 1)]
    spare, holding = total - most - (number_of - 1), [1] * (number_of - 1)
    while spare > 0:
        candidates = [i for i in range(number_of - 1) if holding[i] < most]
        mass, left = sum([weights[i] for i in candidates]), spare
        for i in candidates:
            extra = min(most - holding[i], max(1, left * weights[i] // mass), spare)
            holding[i] = holding[i] + extra
            spare = spare - extra
    return np.array([most] + holding)


def ragged(rng, amount, total, limit, skew):
    if amount == 2:
        one = jax.random.randint(rng, (), max(1, total - limit), min(limit, total - 1) + 1)
        return jnp.stack([one, total - one])
    tallies = jnp.asarray(split_up(amount, total, limit, skew), jnp.int32)
    pairs = (amount - 1) // 2
    source_of, receiver = tallies[1:1 + 2 * pairs:2], tallies[2:2 + 2 * pairs:2]
    slack = jnp.minimum(source_of - 1, limit - receiver)
    moved = jax.random.randint(jax.random.fold_in(rng, 1), (pairs,), 0, 1 << 20) % (slack + 1)
    tallies = tallies.at[1:1 + 2 * pairs:2].set(source_of - moved).at[2:2 + 2 * pairs:2].set(receiver + moved)
    return tallies[jax.random.permutation(jax.random.fold_in(rng, 2), amount)]


def bell_draw(rng, extent, width, reach, cuts=(), held_as=jnp.bfloat16):
    array = jax.random.normal(rng, extent, jnp.float32) * width
    if len(cuts) > 0:
        array = steps_of(rng, extent, cuts, -0.22, 0.18) * array
    return jnp.clip(array, min=-reach, max=reach).astype(held_as)


def setup_inputs(seed: int = 0) -> dict:
    splits = jax.random.split(jax.random.key(seed), 10)
    return {
        "vectors_in": bell_draw(splits[0], (M, NB), 1.0, 6.0, ((0, 16), (1, 2))),
        "panel": bell_draw(splits[1], (M, NPAN), M ** -0.5, 0.03125, ((0, 16), (1, 2))),
        "factor": draw_factor(jax.random.fold_in(splits[9], 71), 0),
        "atom_basis": jax.vmap(lambda own: ragged(own, A_DEV, M_DEV, BMAX, 0))(jax.random.split(splits[3], N_ROW)).reshape((N_ROW, A_DEV)).astype(jnp.int32),
        "proj_count": place_ends(jax.random.randint(splits[4], (ATOMS,), 1, NPMAX + 1), jax.random.fold_in(splits[4], 1), 1, NPMAX).astype(jnp.int32),
        "coupling": bell_draw(splits[5], (ATOMS, K, NPMAX * BMAX), (K * BMAX) ** -0.5, 0.4375, ((0, 16),)),
        "block_present": place_ends((jax.random.randint(splits[6], (ATOMS, K), 0, 4) < 3).astype(jnp.int32), jax.random.fold_in(splits[6], 1), 0, 1),
        "occ_mask": place_ends((jax.random.randint(splits[7], (NB,), 0, 4) < 3).astype(jnp.int32), jax.random.fold_in(splits[7], 1), 0, 1),
        "occ_weight": jnp.clip(jnp.exp(math.log(2.0) - 1.3862944 * jax.random.uniform(splits[8], (NB,), jnp.float32) ** steps_of(splits[8], (NB,), ((0, 2),), -0.2, 0.2)), 0.5, 2.0),
    }


def reference(vectors_in, panel, factor, atom_basis, proj_count, coupling, block_present, occ_mask, occ_weight):
    column_blocks = vectors_in.reshape(N_ROW, M_DEV, NB)
    panel_blocks = panel.reshape(N_ROW, M_DEV, NPAN)

    def accumulate(running, pair):
        product = lax.dot_general(pair[1], pair[0], (((0,), (0,)), ((), ())), preferred_element_type=jnp.float32)
        return running + product, None

    inner_products, leftover = lax.scan(accumulate, jnp.zeros((NPAN, NB), jnp.float32), (column_blocks, panel_blocks))
    mixing = jnp.dot(factor.T, inner_products, precision=lax.Precision.HIGHEST).astype(jnp.bfloat16)

    def rotate(pair):
        update = jnp.dot(pair[1], mixing, preferred_element_type=jnp.float32)
        return (pair[0].astype(jnp.float32) - update).astype(jnp.bfloat16)

    vectors = lax.map(rotate, (column_blocks, panel_blocks)).reshape(N_ROW * M_DEV, NB)

    counts = atom_basis.astype(jnp.int32)
    starts = jnp.cumsum(counts, axis=1).astype(jnp.int32) - counts
    starts = starts + jnp.arange(N_ROW, dtype=jnp.int32)[:, None] * M_DEV
    starts = starts.reshape(-1)
    counts_flat = counts.reshape(-1)
    slot_rank = jnp.arange(BMAX, dtype=jnp.int32)
    row_index = jnp.where(slot_rank[None, :] < counts_flat[:, None], starts[:, None] + slot_rank[None, :], N_ROW * M_DEV).astype(jnp.int32).reshape(-1)
    kept_rows = (jnp.arange(NPMAX, dtype=jnp.int32)[None, :] < proj_count[:, None]).astype(jnp.float32)
    weights = occ_mask.astype(jnp.float32) * occ_weight / NB
    rim_width = (K - 1) // 2

    def column_block(running, block_number):
        columns = lax.dynamic_slice_in_dim(vectors, block_number * NB_DEV, NB_DEV, 1)
        padded = jnp.take(columns, row_index, axis=0, mode="fill", fill_value=0).reshape(ATOMS, BMAX, NB_DEV).astype(jnp.float32)
        projections = jnp.zeros((ATOMS, NPMAX, NB_DEV), jnp.float32)
        for relative in range(K):
            blocks = coupling[:, relative].reshape(ATOMS, NPMAX, BMAX)
            blocks = jnp.where(block_present[:, relative, None, None] > 0, blocks, jnp.zeros_like(blocks)).astype(jnp.float32)
            neighbours = jnp.roll(padded, rim_width - relative, axis=0)
            projections = projections + jnp.einsum("aij,ajn->ain", blocks, neighbours, precision=lax.Precision.HIGHEST)
        rounded = (projections * kept_rows[:, :, None]).astype(jnp.bfloat16)
        local_weights = lax.dynamic_slice_in_dim(weights, block_number * NB_DEV, NB_DEV, 0)
        weighted = (rounded.astype(jnp.float32) * local_weights[None, None, :]).astype(jnp.bfloat16)
        partial_value = jnp.einsum("ain,ajn->aij", weighted.astype(jnp.float32), rounded.astype(jnp.float32), precision=lax.Precision.HIGHEST)
        return running + partial_value.reshape(ATOMS, NPMAX * NPMAX), None

    density, remains = lax.scan(column_block, jnp.zeros((ATOMS, NPMAX * NPMAX), jnp.float32), jnp.arange(N_COL, dtype=jnp.int32))
    return vectors, density
```

```python
import functools

import jax
import jax.numpy as jnp
from jax import lax
from jax.experimental import pallas as pl
from jax.experimental.pallas import tpu as pltpu
from jax.sharding import PartitionSpec as P

NPMAX = 16
BMAX = 24
K = 9
RIM = (K - 1) // 2
HALO = RIM * BMAX
GROUP = 16
WIN = -(-(GROUP + K - 1) * BMAX // 128) * 128
REACH = GROUP + K - 1
F32 = jnp.float32
BF16 = jnp.bfloat16
MESH = pl.DeviceIdType.MESH


def iota(rows, columns, axis):
    return lax.broadcasted_iota(jnp.int32, (rows, columns), axis)


def group_of(rows, columns, axis, size, most):
    small = (8, columns) if axis == 1 else (rows, 128)
    index = iota(*small, axis)
    group = jnp.zeros(small, jnp.int32)
    for edge in range(1, most):
        group = group + jnp.where(index >= edge * size, 1, 0)
    return jnp.tile(group, (rows // small[0], columns // small[1]))


def mix_kernel(n, plane, vec_hbm, panel_hbm, coupling_hbm, factor_ref, basis_ref, proj_ref, present_ref, mask_ref, occ_ref,
               vec, pan_ref, mix_ref, own_ref, got_ref,
               pan_t, part, got_first, middle, got_second, factor_hi, factor_lo, counts, limit, cm_ref, halo_ref, skew, band,
               first_ref, starts, ext, pext, padded, ppadded, base, lean, full, dens, weight,
               load_sem, own_sem, cm_sem, start_sem, pan_sems, halo_sems, count_sems, ring_sems, den_sems):
    row, col = lax.axis_index("row"), lax.axis_index("col")
    other = 1 - col
    up, down = lax.rem(row + 1, n), lax.rem(row + n - 1, n)
    rows, half = panel_hbm.shape
    chunks, wide_c, npan = part.shape
    unit = wide_c // n
    atoms, wide = cm_ref.shape[1:]
    groups = atoms // GROUP
    body = pl.ds(HALO, rows)
    q, p = n // plane, plane
    line, spot = lax.div(row, p), lax.rem(row, p)
    contract = (((0,), (0,)), ((), ()))
    across = (((1,), (1,)), ((), ()))

    def plane_peer(step):
        return line * p + lax.rem(spot + step, p)

    def line_peer(step):
        return lax.rem(line + step, q) * p + spot

    by_plane, by_line = (p, spot, plane_peer), (q, line, line_peer)
    ways = [(by_line, by_plane) if chunks > 2 and c == 0 else (by_plane, by_line) for c in range(chunks)]

    own = pltpu.make_async_copy(panel_hbm, pan_ref.at[col, body], own_sem)
    own.start()
    pieces = rows // load_sem.shape[0]
    loads = [pltpu.make_async_copy(vec_hbm.at[pl.ds(i * pieces, pieces)], vec.at[pl.ds(i * pieces, pieces)], load_sem.at[i])
             for i in range(load_sem.shape[0])]
    for load in loads:
        load.start()
    blocks = pltpu.make_async_copy(coupling_hbm, cm_ref, cm_sem)
    blocks.start()

    barrier = pltpu.get_barrier_semaphore()
    greeted = [(plane_peer(step), col) for step in range(1, p)] + [(line_peer(step), col) for step in range(1, q)]
    greeted += [(up, col), (down, col)] + [(peer, other) for peer in (row, up, down)]
    for target in greeted:
        pl.semaphore_signal(barrier, inc=1, device_id=target, device_id_type=MESH)
    high = factor_ref[...].astype(BF16)
    factor_hi[...] = high
    factor_lo[...] = (factor_ref[...] - high.astype(F32)).astype(BF16)
    weight[...] = mask_ref[...].astype(F32) * occ_ref[...] / (vec_hbm.shape[1] * lax.axis_size("col"))
    length = ext.shape[1]
    edge = rows + HALO
    ext[:, edge:, :] = jnp.zeros((ext.shape[0], length - edge, 128), F32)
    pext[:, edge:, :] = jnp.zeros((2, length - edge, half), F32)
    used = (atoms + 2 * RIM) * BMAX
    padded[used:, :] = jnp.zeros((padded.shape[0] - used, padded.shape[1]), BF16)
    ppadded[used:, :] = jnp.zeros((ppadded.shape[0] - used, ppadded.shape[1]), BF16)
    low = (GROUP - 1) * GROUP
    skew[:, 0:low, :] = jnp.zeros((skew.shape[0], low, 128), F32)
    skew[:, low + K * GROUP:, :] = jnp.zeros((skew.shape[0], low, 128), F32)
    pl.semaphore_wait(barrier, len(greeted))

    def remote(src, dst, sems, slot, target):
        return pltpu.make_async_remote_copy(
            src_ref=src, dst_ref=dst, send_sem=sems.at[(0,) + slot], recv_sem=sems.at[(1,) + slot],
            device_id=target, device_id_type=MESH)

    swap = remote(panel_hbm, pan_ref.at[col, body], pan_sems, (0,), (row, other))
    swap.start()
    count_copies = [
        remote(basis_ref, counts.at[side], count_sems, (side,), (target, col))
        for side, target in ((0, up), (1, down))
    ]
    for copy in count_copies:
        copy.start()
    pan_halos, vec_halos = [], []
    for side, target in ((0, up), (1, down)):
        src_at = rows - HALO if side == 0 else 0
        dst_at = 0 if side == 0 else HALO + rows
        for where in (0, 1):
            to = col if where == 0 else other
            pan_halos.append(remote(panel_hbm.at[pl.ds(src_at, HALO)], pan_ref.at[col, pl.ds(dst_at, HALO)],
                                    pan_sems, (1 + 2 * side + where,), (target, to)))
        vec_halos.append(remote(vec_hbm.at[pl.ds(src_at, HALO)], halo_ref.at[side], halo_sems, (side,), (target, col)))
    for copy in pan_halos:
        copy.start()

    own.wait()
    pan_t[pl.ds(pl.multiple_of(col * half, half), half), :] = pan_ref[col, body, :].T
    for load in loads:
        load.wait()

    lanes = [slice(c * 128, (c + 1) * 128) for c in range(ext.shape[0])]
    chunk_rows = rows // 8

    def widen(t, carry):
        at = pl.multiple_of(t * chunk_rows, 16)
        block = vec[pl.ds(at, chunk_rows), :].astype(F32)
        for c, span in enumerate(lanes):
            ext[c, pl.ds(HALO + at, chunk_rows), :] = block[:, span]
        return carry

    lax.fori_loop(0, 8, widen, 0)

    swap.wait_recv()
    pan_t[pl.ds(pl.multiple_of(other * half, half), half), :] = pan_ref[other, body, :].T

    def span_of(c):
        return slice(c * wide_c, (c + 1) * wide_c)

    def first_copy(c, step):
        (size, at, peer), (size_s, _, _) = ways[c]
        length = size_s * unit
        src = pl.ds(pl.multiple_of(lax.rem(at + step, size) * length, unit), length)
        return remote(part.at[c, src], got_first.at[c, step, pl.ds(0, length)], ring_sems, (c, 0, step), (peer(step), col))

    def second_copy(c, step):
        _, (size, at, peer) = ways[c]
        src = pl.ds(pl.multiple_of(lax.rem(at + step, size) * unit, unit), unit)
        return remote(middle.at[c, src], got_second.at[c, step], ring_sems, (c, 1, step), (peer(step), col))

    def own_block(c):
        (_, at, _), (size_s, _, _) = ways[c]
        return pl.multiple_of(c * wide_c + at * size_s * unit, unit)

    def third_copy(c, step):
        _, (_, at, peer) = ways[c]
        mine = pl.ds(pl.multiple_of(own_block(c) + at * unit, unit), unit)
        return remote(mix_ref.at[mine], mix_ref.at[mine], ring_sems, (c, 2, step), (peer(step), col))

    def fourth_copy(c, step):
        (_, _, peer), (size_s, _, _) = ways[c]
        mine = pl.ds(own_block(c), size_s * unit)
        return remote(mix_ref.at[mine], mix_ref.at[mine], ring_sems, (c, 3, step), (peer(step), col))

    def first_steps(c):
        return range(1, ways[c][0][0])

    def second_steps(c):
        return range(1, ways[c][1][0])

    def after_first(c):
        (_, at, _), (size_s, _, _) = ways[c]
        length = size_s * unit
        for step in first_steps(c):
            first_copy(c, step).wait_recv()
        total = part[c, pl.ds(pl.multiple_of(at * length, unit), length), :].astype(F32)
        for step in first_steps(c):
            total = total + got_first[c, step, 0:length, :].astype(F32)
        middle[c, 0:length, :] = total.astype(BF16)
        for step in second_steps(c):
            second_copy(c, step).start()

    def after_second(c):
        _, (_, at, _) = ways[c]
        for step in second_steps(c):
            second_copy(c, step).wait_recv()
        inner = middle[c, pl.ds(pl.multiple_of(at * unit, unit), unit), :].astype(F32)
        for step in second_steps(c):
            inner = inner + got_second[c, step].astype(F32)
        top = inner.astype(BF16)
        rest = (inner - top.astype(F32)).astype(BF16)
        both = jnp.dot(jnp.concatenate([top, rest], axis=0), factor_hi[...], preferred_element_type=F32)
        mixed = both[0:unit] + both[unit:] + jnp.dot(top, factor_lo[...], preferred_element_type=F32)
        mix_ref[pl.ds(pl.multiple_of(own_block(c) + at * unit, unit), unit), :] = mixed.astype(BF16)
        for step in second_steps(c):
            third_copy(c, step).start()

    def after_third(c):
        for step in second_steps(c):
            third_copy(c, step).wait_recv()
        for step in first_steps(c):
            fourth_copy(c, step).start()

    def after_fourth(c):
        for step in first_steps(c):
            fourth_copy(c, step).wait_recv()

    for c in range(chunks):
        inner = jnp.dot(pan_t[...], vec[:, span_of(c)], preferred_element_type=F32)
        part[c] = inner.T.astype(BF16)
        for step in first_steps(c):
            first_copy(c, step).start()
    for copy in vec_halos:
        copy.start()

    for which in (0, 1):
        pext[which, HALO:HALO + rows, :] = pan_ref[which, body, :].astype(F32)
    for copy in count_copies:
        copy.wait_recv()
    here = basis_ref[...].astype(F32)
    prev, post = counts[0].astype(F32), counts[1].astype(F32)
    lower = jnp.where(iota(atoms, atoms, 0) < iota(atoms, atoms, 1), 1.0, 0.0).astype(BF16)
    table = jnp.concatenate([prev, here, post, jnp.zeros((5, atoms), F32)], axis=0).astype(BF16)
    first = jnp.dot(table, lower, preferred_element_type=F32).astype(jnp.int32)
    first_ref[...] = jnp.clip(first + (HALO - rows) + rows * iota(8, atoms, 0), 0, rows + 2 * HALO)
    begin_copy = pltpu.make_async_copy(first_ref, starts, start_sem)
    begin_copy.start()
    lines = []
    at = iota(1, atoms, 1)
    for k in range(K):
        d = k - RIM
        near = here
        if d != 0:
            turn = (-d) % atoms
            inside = (at + d >= 0) & (at + d < atoms)
            near = jnp.where(inside, pltpu.roll(here, turn, 1), pltpu.roll(prev if d < 0 else post, turn, 1))
        lines.append(jnp.where(present_ref[k:k + 1, :] > 0, near, 0.0))
    lines.append(proj_ref[...].astype(F32))
    lines.append(jnp.zeros((atoms - K - 1, atoms), F32))
    limit[...] = jnp.concatenate(lines, axis=0).T
    blocks.wait()

    in_i = group_of(GROUP, wide, 1, BMAX, NPMAX)
    slot = (iota(GROUP, wide, 1) - BMAX * in_i).astype(F32)
    in_i = in_i.astype(F32)
    lane = iota(8, 128, 1)

    def band_step(t, carry):
        chunk = pl.ds(pl.multiple_of(t * GROUP, GROUP), GROUP)
        bounds = limit[chunk, :]
        valid = in_i < bounds[:, K:K + 1]
        for k in range(K):
            block = cm_ref[k, chunk, :].astype(F32)
            block = jnp.where(valid & (slot < bounds[:, k:k + 1]), block, 0.0)
            top = (GROUP + K - 2 - k) * GROUP
            for tile in range(wide // 128):
                skew[tile, top:top + GROUP, :] = block[:, tile * 128:(tile + 1) * 128]
        for i in range(NPMAX):
            sides = []
            for side in range(GROUP // 8):
                near = range(8 * side, 8 * side + 8 + K - 1)
                tiles = []
                for tile in range(WIN // 128):
                    acc, end = jnp.zeros((8, 128), F32), 0
                    for b in near:
                        to, last = max(b * BMAX, tile * 128), min((b + 1) * BMAX, (tile + 1) * 128)
                        while to < last:
                            source = i * BMAX + to - b * BMAX
                            count = min(last - to, 128 - source % 128)
                            begin = (REACH - 1 - b) * GROUP + 8 * side * (GROUP + 1)
                            piece = skew[source // 128, pl.ds(begin, 8, stride=GROUP + 1), :]
                            turn = (to - source) % 128
                            piece = piece if turn == 0 else pltpu.roll(piece, turn, 1)
                            acc = jnp.where(lane >= to % 128, piece, acc)
                            to += count
                            end = (to - 1) % 128 + 1
                    tiles.append(jnp.where(lane < end, acc, 0.0) if 0 < end < 128 else acc)
                sides.append(jnp.concatenate(tiles, axis=1))
            band[t, i * GROUP:(i + 1) * GROUP, :] = jnp.concatenate(sides, axis=0).astype(BF16)
        return carry

    def gather(t, carry):
        at = pl.multiple_of(2 * t * BMAX, 16)
        begins = []
        for e in (0, 1):
            flat = 2 * t + e + atoms - RIM
            begins.append(starts[lax.div(flat, atoms), lax.rem(flat, atoms)])
        for c, span in enumerate(lanes):
            both = [ext[c, pl.ds(begin, BMAX), :] for begin in begins]
            padded[pl.ds(at, 2 * BMAX), span] = jnp.concatenate(both, axis=0).astype(BF16)
        for c in (0, 1):
            both = [pext[c, pl.ds(begin, BMAX), :] for begin in begins]
            ppadded[pl.ds(at, 2 * BMAX), c * half:(c + 1) * half] = jnp.concatenate(both, axis=0).astype(BF16)
        return carry

    def project(g, carry):
        at = pl.ds(pl.multiple_of(g * GROUP * BMAX, 16), WIN)
        base[g] = jnp.dot(band[g], padded[at, :], preferred_element_type=F32)
        lean[g] = jnp.dot(band[g], ppadded[at, :], preferred_element_type=F32).astype(BF16)
        return carry

    lax.fori_loop(0, groups // 2, band_step, 0)
    for c in range(chunks):
        after_first(c)
    lax.fori_loop(groups // 2, groups, band_step, 0)
    for c in range(chunks):
        after_second(c)
    begin_copy.wait()
    lax.fori_loop(RIM // 2, (atoms + RIM) // 2, gather, 0)
    for c in range(chunks):
        after_third(c)
    lax.fori_loop(1, groups - 1, project, 0)

    size = GROUP * NPMAX
    same = (iota(size, size, 0) & (GROUP - 1)) == (iota(size, size, 1) & (GROUP - 1))
    expand = jnp.where(group_of(size, size, 0, GROUP, NPMAX) == (iota(size, size, 1) & (NPMAX - 1)), 1.0, 0.0).astype(BF16)
    owner = group_of(GROUP, size, 1, NPMAX, NPMAX)

    def tail(c, g):
        update = lax.dot_general(lean[g], mix_ref[span_of(c), :], across, preferred_element_type=F32)
        rounded = (base[g, :, span_of(c)] - update).astype(BF16)
        weighted = (rounded.astype(F32) * weight[:, span_of(c)]).astype(BF16)
        product = lax.dot_general(weighted, rounded, across, preferred_element_type=F32)
        full[g] = product if c == 0 else full[g] + product

    def finish(g):
        kept = jnp.where(same, full[g], 0.0)
        top = kept.astype(BF16)
        rest = (kept - top.astype(F32)).astype(BF16)
        spread = jnp.dot(top, expand, preferred_element_type=F32) + jnp.dot(rest, expand, preferred_element_type=F32)
        result = jnp.zeros((GROUP, size), F32)
        for i in range(NPMAX):
            result = jnp.where(owner == i, spread[i * GROUP:(i + 1) * GROUP, :], result)
        dens[pl.ds(pl.multiple_of(g * GROUP, GROUP), GROUP), :] = result

    for c in range(chunks):
        after_fourth(c)

        def step_of(g, carry, c=c):
            tail(c, g)
            return carry

        lax.fori_loop(1, groups - 1, step_of, 0)

    def finish_step(g, carry):
        finish(g)
        return carry

    lax.fori_loop(1, groups - 1, finish_step, 0)
    share = own_ref.shape[0]
    inside = share - GROUP

    def den_copy(start, count, slot):
        src = pl.ds(pl.multiple_of(start, GROUP), count)
        dst = pl.ds(pl.multiple_of(start - other * share, GROUP), count)
        return remote(dens.at[src], got_ref.at[dst], den_sems, (slot,), (row, other))

    sent = [den_copy(other * share + GROUP * col, inside, 0), den_copy(other * (atoms - GROUP), GROUP, 1)]
    sent[0].start()

    for copy in pan_halos + vec_halos:
        copy.wait()
    for side, at in ((0, 0), (1, HALO + rows)):
        block = halo_ref[side].astype(F32)
        for c, span in enumerate(lanes):
            ext[c, at:at + HALO, :] = block[:, span]
        for which in (0, 1):
            pext[which, at:at + HALO, :] = pan_ref[which, at:at + HALO, :].astype(F32)
    lax.fori_loop(0, RIM // 2, gather, 0)
    lax.fori_loop((atoms + RIM) // 2, (atoms + 2 * RIM) // 2, gather, 0)

    def last_group(g):
        project(g, 0)
        for c in range(chunks):
            tail(c, g)
        finish(g)

    def last_step(t, carry):
        last_group(lax.rem(other + t, 2) * (groups - 1))

        @pl.when(t == 0)
        def _():
            sent[1].start()

        return carry

    lax.fori_loop(0, 2, last_step, 0)
    own_ref[...] = dens[pl.ds(pl.multiple_of(col * share, share), share), :]

    for copy in sent:
        copy.wait()
    swap.wait_send()
    for copy in count_copies:
        copy.wait_send()
    for c in range(chunks):
        for step in first_steps(c):
            first_copy(c, step).wait_send()
            fourth_copy(c, step).wait_send()
        for step in second_steps(c):
            second_copy(c, step).wait_send()
            third_copy(c, step).wait_send()


def vector_kernel(vin_ref, pan_ref, mix_ref, own_ref, got_ref, vec_ref, den_ref, mixing):
    step = pl.program_id(0)
    tile = vec_ref.shape[0]

    @pl.when(step == 0)
    def _():
        mixing[...] = mix_ref[...].T
        den_ref[...] = own_ref[...] + got_ref[...]

    at = pl.multiple_of(step * tile, 16)
    inside = pl.ds(pl.multiple_of(HALO + at, 16), tile)
    panel = jnp.concatenate([pan_ref[0, inside, :], pan_ref[1, inside, :]], axis=1)
    update = jnp.dot(panel, mixing[...], preferred_element_type=F32)
    vec_ref[...] = (vin_ref[pl.ds(at, tile), :].astype(F32) - update).astype(BF16)


def local(vectors_in, panel, factor, atom_basis, proj_count, coupling, block_present, occ_mask, occ_weight):
    n = lax.axis_size("row")
    rows, cols = vectors_in.shape
    half = panel.shape[1]
    npan = factor.shape[0]
    atoms = atom_basis.shape[1]
    groups = atoms // GROUP
    share = atoms // lax.axis_size("col")
    wide = coupling.shape[2]
    vmem = pl.BlockSpec(memory_space=pltpu.VMEM)
    hbm = pl.BlockSpec(memory_space=pl.ANY)
    plane = max(d for d in range(1, n + 1) if n % d == 0 and d * d <= n)
    most, least = max(plane, n // plane), min(plane, n // plane)
    chunks = max(1, cols // (n * 16))
    width = cols // chunks
    unit = width // n
    ext_rows = rows + 2 * HALO
    pad_rows = (groups - 1) * GROUP * BMAX + WIN
    dma = pltpu.SemaphoreType.DMA
    operands = (vectors_in, panel, jnp.swapaxes(coupling, 0, 1), factor, atom_basis, proj_count[None, :], block_present.T)
    operands = [pltpu.with_memory_space_constraint(x, pltpu.HBM) for x in operands]
    vin, pan, mix, own, got = pl.pallas_call(
        functools.partial(mix_kernel, n, plane),
        out_shape=(
            jax.ShapeDtypeStruct((rows, cols), BF16),
            jax.ShapeDtypeStruct((2, ext_rows, half), BF16),
            jax.ShapeDtypeStruct((cols, npan), BF16),
            jax.ShapeDtypeStruct((share, NPMAX * NPMAX), F32),
            jax.ShapeDtypeStruct((share, NPMAX * NPMAX), F32),
        ),
        in_specs=[hbm] * 3 + [vmem] * 6,
        out_specs=(vmem,) * 5,
        scratch_shapes=[
            pltpu.VMEM((npan, rows), BF16),
            pltpu.VMEM((chunks, width, npan), BF16),
            pltpu.VMEM((chunks, most, width // least, npan), BF16),
            pltpu.VMEM((chunks, width // least, npan), BF16),
            pltpu.VMEM((chunks, most, unit, npan), BF16),
            pltpu.VMEM((npan, npan), BF16),
            pltpu.VMEM((npan, npan), BF16),
            pltpu.VMEM((2, 1, atoms), jnp.int32),
            pltpu.VMEM((atoms, atoms), F32),
            pltpu.VMEM((K, atoms, wide), BF16),
            pltpu.VMEM((2, HALO, cols), BF16),
            pltpu.VMEM((wide // 128, (2 * GROUP + K - 2) * GROUP, 128), F32),
            pltpu.VMEM((groups, GROUP * NPMAX, WIN), BF16),
            pltpu.VMEM((8, atoms), jnp.int32),
            pltpu.SMEM((8, atoms), jnp.int32),
            pltpu.VMEM((cols // 128, ext_rows + BMAX, 128), F32),
            pltpu.VMEM((2, ext_rows + BMAX, half), F32),
            pltpu.VMEM((pad_rows, cols), BF16),
            pltpu.VMEM((pad_rows, npan), BF16),
            pltpu.VMEM((groups, GROUP * NPMAX, cols), F32),
            pltpu.VMEM((groups, GROUP * NPMAX, npan), BF16),
            pltpu.VMEM((groups, GROUP * NPMAX, GROUP * NPMAX), F32),
            pltpu.VMEM((atoms, NPMAX * NPMAX), F32),
            pltpu.VMEM((1, cols), F32),
            dma((2,)), dma, dma, dma, dma((2, 5)), dma((2, 2)), dma((2, 2)),
            dma((2, chunks, 4, most)), dma((2, 2)),
        ],
        compiler_params=pltpu.CompilerParams(collective_id=0, has_side_effects=True, vmem_limit_bytes=48 << 20),
        cost_estimate=pl.CostEstimate(flops=8 * 10**9, bytes_accessed=10 << 20, transcendentals=0),
    )(*operands, occ_mask[None, :], occ_weight[None, :])

    tile = rows // 8
    return pl.pallas_call(
        vector_kernel,
        out_shape=(
            jax.ShapeDtypeStruct((rows, cols), BF16),
            jax.ShapeDtypeStruct((share, NPMAX * NPMAX), F32),
        ),
        grid=(rows // tile,),
        in_specs=[vmem] * 5,
        out_specs=[
            pl.BlockSpec((tile, cols), lambda s: (s, 0)),
            pl.BlockSpec((share, NPMAX * NPMAX), lambda s: (0, 0)),
        ],
        scratch_shapes=[pltpu.VMEM((npan, cols), BF16)],
        compiler_params=pltpu.CompilerParams(vmem_limit_bytes=16 << 20),
        cost_estimate=pl.CostEstimate(flops=6 * 10**9, bytes_accessed=10 << 20, transcendentals=0),
    )(vin, pan, mix, own, got)


def solution(mesh):
    placed = (
        P("row", "col"),
        P("row", "col"),
        P(),
        P("row", None),
        P("row"),
        P("row", None, None),
        P("row", None),
        P("col"),
        P("col"),
    )
    return jax.shard_map(
        local,
        mesh=mesh,
        in_specs=placed,
        out_specs=(P("row", "col"), P(("row", "col"), None)),
        check_vma=False,
    )
```

```python
import functools

import jax
import jax.numpy as jnp
from jax import lax
from jax.experimental import pallas as pl
from jax.experimental.pallas import tpu as pltpu
from jax.sharding import PartitionSpec as P

NPMAX = 16
BMAX = 24
K = 9
RIM = (K - 1) // 2
HALO = RIM * BMAX
PIECES = 3
GROUP = 16
WIN = -(-(GROUP + K - 1) * BMAX // 128) * 128
REACH = GROUP + K - 1
F32 = jnp.float32
BF16 = jnp.bfloat16
MESH = pl.DeviceIdType.MESH


def iota(rows, columns, axis):
    return lax.broadcasted_iota(jnp.int32, (rows, columns), axis)


def group_of(rows, columns, axis, size, most):
    small = (8, columns) if axis == 1 else (rows, 128)
    index = iota(*small, axis)
    group = jnp.zeros(small, jnp.int32)
    for edge in range(1, most):
        group = group + jnp.where(index >= edge * size, 1, 0)
    return jnp.tile(group, (rows // small[0], columns // small[1]))


def mix_kernel(n, plane, vec_hbm, panel_hbm, coupling_hbm, factor_hbm, basis_hbm, proj_hbm, present_hbm, mask_hbm, occ_hbm,
               vec, pan_ref, mix_ref, own_ref, got_ref,
               factor_ref, basis_ref, proj_ref, present_ref, mask_ref, occ_ref,
               pan_t, part, got_first, middle, got_second, factor_hi, factor_lo, counts, limit, cm_ref, halo_ref, skew, band,
               first_ref, starts, ext, pext, padded, ppadded, base, lean, full, dens, weight,
               load_sem, small_sem, own_sem, cm_sem, start_sem, pan_sems, halo_sems, count_sems, ring_sems, fold_sems, den_sems):
    row, col = lax.axis_index("row"), lax.axis_index("col")
    other = 1 - col
    up, down = lax.rem(row + 1, n), lax.rem(row + n - 1, n)
    rows, half = panel_hbm.shape
    chunks, wide_c, npan = part.shape
    unit = wide_c // n
    atoms, wide = cm_ref.shape[1:]
    groups = atoms // GROUP
    body = pl.ds(HALO, rows)
    q, p = n // plane, plane
    line, spot = lax.div(row, p), lax.rem(row, p)
    contract = (((0,), (0,)), ((), ()))
    across = (((1,), (1,)), ((), ()))

    def plane_peer(step):
        return line * p + lax.rem(spot + step, p)

    def line_peer(step):
        return lax.rem(line + step, q) * p + spot

    by_plane, by_line = (p, spot, plane_peer), (q, line, line_peer)
    ways = [(by_line, by_plane) if chunks == 4 and c == 2 else (by_plane, by_line) for c in range(chunks)]

    own = pltpu.make_async_copy(panel_hbm, pan_ref.at[col, body], own_sem)
    own.start()
    pieces = rows // load_sem.shape[0]
    loads = [pltpu.make_async_copy(vec_hbm.at[pl.ds(i * pieces, pieces)], vec.at[pl.ds(i * pieces, pieces)], load_sem.at[i])
             for i in range(load_sem.shape[0])]
    for load in loads:
        load.start()
    small = [pltpu.make_async_copy(src, dst, small_sem.at[i]) for i, (src, dst) in enumerate((
        (basis_hbm, basis_ref), (factor_hbm, factor_ref), (proj_hbm, proj_ref), (present_hbm, present_ref),
        (mask_hbm, mask_ref), (occ_hbm, occ_ref)))]
    for load in small:
        load.start()
    blocks = pltpu.make_async_copy(coupling_hbm, cm_ref, cm_sem)
    blocks.start()

    barrier = pltpu.get_barrier_semaphore()
    greeted = [(plane_peer(step), col) for step in range(1, p)] + [(line_peer(step), col) for step in range(1, q)]
    greeted += [(up, col), (down, col)] + [(peer, other) for peer in (row, up, down)]
    for target in greeted:
        pl.semaphore_signal(barrier, inc=1, device_id=target, device_id_type=MESH)
    length = ext.shape[1]
    edge = rows + HALO
    ext[:, edge:, :] = jnp.zeros((ext.shape[0], length - edge, 128), F32)
    pext[:, edge:, :] = jnp.zeros((2, length - edge, half), F32)
    used = (atoms + 2 * RIM) * BMAX
    padded[used:, :] = jnp.zeros((padded.shape[0] - used, padded.shape[1]), BF16)
    ppadded[used:, :] = jnp.zeros((ppadded.shape[0] - used, ppadded.shape[1]), BF16)
    low = (GROUP - 1) * GROUP
    skew[:, 0:low, :] = jnp.zeros((skew.shape[0], low, 128), F32)
    skew[:, low + K * GROUP:, :] = jnp.zeros((skew.shape[0], low, 128), F32)
    pl.semaphore_wait(barrier, len(greeted))

    def remote(src, dst, sems, slot, target):
        return pltpu.make_async_remote_copy(
            src_ref=src, dst_ref=dst, send_sem=sems.at[(0,) + slot], recv_sem=sems.at[(1,) + slot],
            device_id=target, device_id_type=MESH)

    swap = remote(panel_hbm, pan_ref.at[col, body], pan_sems, (0,), (row, other))
    swap.start()
    count_copies = [
        remote(basis_hbm, counts.at[side], count_sems, (side,), (target, col))
        for side, target in ((0, up), (1, down))
    ]
    for copy in count_copies:
        copy.start()
    pan_halos, vec_halos = [], []
    for side, target in ((0, up), (1, down)):
        src_at = rows - HALO if side == 0 else 0
        dst_at = 0 if side == 0 else HALO + rows
        for where in (0, 1):
            to = col if where == 0 else other
            pan_halos.append(remote(panel_hbm.at[pl.ds(src_at, HALO)], pan_ref.at[col, pl.ds(dst_at, HALO)],
                                    pan_sems, (1 + 2 * side + where,), (target, to)))
        for piece in range(PIECES):
            part_at = piece * (HALO // PIECES)
            vec_halos.append(remote(vec_hbm.at[pl.ds(src_at + part_at, HALO // PIECES)],
                                    halo_ref.at[side, pl.ds(part_at, HALO // PIECES)], halo_sems, (side, piece), (target, col)))
    for copy in pan_halos:
        copy.start()

    own.wait()
    pan_t[pl.ds(pl.multiple_of(col * half, half), half), :] = pan_ref[col, body, :].T
    for load in small:
        load.wait()
    high = factor_ref[...].astype(BF16)
    factor_hi[...] = high
    factor_lo[...] = (factor_ref[...] - high.astype(F32)).astype(BF16)
    weight[...] = mask_ref[...].astype(F32) * occ_ref[...] / (vec_hbm.shape[1] * lax.axis_size("col"))
    for load in loads:
        load.wait()

    lanes = [slice(c * 128, (c + 1) * 128) for c in range(ext.shape[0])]
    chunk_rows = rows // 8

    def widen(t, carry):
        at = pl.multiple_of(t * chunk_rows, 16)
        block = vec[pl.ds(at, chunk_rows), :].astype(F32)
        for c, span in enumerate(lanes):
            ext[c, pl.ds(HALO + at, chunk_rows), :] = block[:, span]
        return carry

    lax.fori_loop(0, 8, widen, 0)

    swap.wait_recv()
    pan_t[pl.ds(pl.multiple_of(other * half, half), half), :] = pan_ref[other, body, :].T

    def span_of(c):
        return slice(c * wide_c, (c + 1) * wide_c)

    def first_copy(c, step):
        (size, at, peer), (size_s, _, _) = ways[c]
        length = size_s * unit
        src = pl.ds(pl.multiple_of(lax.rem(at + step, size) * length, unit), length)
        return remote(part.at[c, src], got_first.at[c, step, pl.ds(0, length)], ring_sems, (c, 0, step), (peer(step), col))

    def rounds(c):
        return range(ways[c][1][0].bit_length() - 1)

    def fold_copy(c, turn):
        _, (size, at, peer) = ways[c]
        reach = 1 << turn
        ahead = lax.rem(lax.div(at, reach), 2)
        step = reach + ahead * (size - 2 * reach)
        length = size * unit
        return remote(middle.at[c, turn, pl.ds(0, length)], got_second.at[c, turn, pl.ds(0, length)],
                      fold_sems, (c, turn), (peer(step), col))

    def own_block(c):
        (_, at, _), (size_s, _, _) = ways[c]
        return pl.multiple_of(c * wide_c + at * size_s * unit, unit)

    def last_copy(c, step):
        (_, _, peer), (size_s, _, _) = ways[c]
        mine = pl.ds(own_block(c), size_s * unit)
        return remote(mix_ref.at[mine], mix_ref.at[mine], ring_sems, (c, 1, step), (peer(step), col))

    def first_steps(c):
        return range(1, ways[c][0][0])

    def after_first(c):
        (_, at, _), (size_s, _, _) = ways[c]
        length = size_s * unit
        for step in first_steps(c):
            first_copy(c, step).wait_recv()
        total = part[c, pl.ds(pl.multiple_of(at * length, unit), length), :].astype(F32)
        for step in first_steps(c):
            total = total + got_first[c, step, 0:length, :].astype(F32)
        middle[c, 0, 0:length, :] = total.astype(BF16)
        fold_copy(c, 0).start()

    def after_fold(c, turn):
        length = ways[c][1][0] * unit
        fold_copy(c, turn).wait_recv()
        inner = middle[c, turn, 0:length, :].astype(F32) + got_second[c, turn, 0:length, :].astype(F32)
        top = inner.astype(BF16)
        if turn + 1 < len(rounds(c)):
            middle[c, turn + 1, 0:length, :] = top
            fold_copy(c, turn + 1).start()
            return
        rest = (inner - top.astype(F32)).astype(BF16)
        both = jnp.dot(jnp.concatenate([top, rest], axis=0), factor_hi[...], preferred_element_type=F32)
        mixed = both[0:length] + both[length:] + jnp.dot(top, factor_lo[...], preferred_element_type=F32)
        mix_ref[pl.ds(own_block(c), length), :] = mixed.astype(BF16)
        for step in first_steps(c):
            last_copy(c, step).start()

    def after_last(c):
        for step in first_steps(c):
            last_copy(c, step).wait_recv()

    def start_halos(*which):
        for piece in which:
            for copy in vec_halos[piece::PIECES]:
                copy.start()

    for first_c, last_c in ([(1, 3), (0, 1), (3, 4)] if chunks == 4 else [(0, chunks)]):
        at = first_c * wide_c
        inner = jnp.dot(pan_t[...], vec[:, at:last_c * wide_c], preferred_element_type=F32).T.astype(BF16)
        for c in range(first_c, last_c):
            part[c] = inner[c * wide_c - at:(c + 1) * wide_c - at]
            for step in first_steps(c):
                first_copy(c, step).start()
    start_halos(0)

    for which in (0, 1):
        pext[which, HALO:HALO + rows, :] = pan_ref[which, body, :].astype(F32)
    for copy in count_copies:
        copy.wait_recv()
    here = basis_ref[...].astype(F32)
    prev, post = counts[0].astype(F32), counts[1].astype(F32)
    lower = jnp.where(iota(atoms, atoms, 0) < iota(atoms, atoms, 1), 1.0, 0.0).astype(BF16)
    table = jnp.concatenate([prev, here, post, jnp.zeros((5, atoms), F32)], axis=0).astype(BF16)
    first = jnp.dot(table, lower, preferred_element_type=F32).astype(jnp.int32)
    first_ref[...] = jnp.clip(first + (HALO - rows) + rows * iota(8, atoms, 0), 0, rows + 2 * HALO)
    begin_copy = pltpu.make_async_copy(first_ref, starts, start_sem)
    begin_copy.start()
    lines = []
    at = iota(1, atoms, 1)
    for k in range(K):
        d = k - RIM
        near = here
        if d != 0:
            turn = (-d) % atoms
            inside = (at + d >= 0) & (at + d < atoms)
            near = jnp.where(inside, pltpu.roll(here, turn, 1), pltpu.roll(prev if d < 0 else post, turn, 1))
        lines.append(jnp.where(present_ref[k:k + 1, :] > 0, near, 0.0))
    lines.append(proj_ref[...].astype(F32))
    lines.append(jnp.zeros((atoms - K - 1, atoms), F32))
    limit[...] = jnp.concatenate(lines, axis=0).T
    blocks.wait()

    in_i = group_of(GROUP, wide, 1, BMAX, NPMAX)
    slot = (iota(GROUP, wide, 1) - BMAX * in_i).astype(F32)
    in_i = in_i.astype(F32)
    lane = iota(8, 128, 1)

    def band_step(t, carry):
        chunk = pl.ds(pl.multiple_of(t * GROUP, GROUP), GROUP)
        bounds = limit[chunk, :]
        valid = in_i < bounds[:, K:K + 1]
        for k in range(K):
            block = cm_ref[k, chunk, :].astype(F32)
            block = jnp.where(valid & (slot < bounds[:, k:k + 1]), block, 0.0)
            top = (GROUP + K - 2 - k) * GROUP
            for tile in range(wide // 128):
                skew[tile, top:top + GROUP, :] = block[:, tile * 128:(tile + 1) * 128]
        for i in range(NPMAX):
            sides = []
            for side in range(GROUP // 8):
                near = range(8 * side, 8 * side + 8 + K - 1)
                tiles = []
                for tile in range(WIN // 128):
                    acc, end = jnp.zeros((8, 128), F32), 0
                    for b in near:
                        to, last = max(b * BMAX, tile * 128), min((b + 1) * BMAX, (tile + 1) * 128)
                        while to < last:
                            source = i * BMAX + to - b * BMAX
                            count = min(last - to, 128 - source % 128)
                            begin = (REACH - 1 - b) * GROUP + 8 * side * (GROUP + 1)
                            piece = skew[source // 128, pl.ds(begin, 8, stride=GROUP + 1), :]
                            turn = (to - source) % 128
                            piece = piece if turn == 0 else pltpu.roll(piece, turn, 1)
                            acc = jnp.where(lane >= to % 128, piece, acc)
                            to += count
                            end = (to - 1) % 128 + 1
                    tiles.append(jnp.where(lane < end, acc, 0.0) if 0 < end < 128 else acc)
                sides.append(jnp.concatenate(tiles, axis=1))
            band[t, i * GROUP:(i + 1) * GROUP, :] = jnp.concatenate(sides, axis=0).astype(BF16)
        return carry

    def gather(t, carry):
        at = pl.multiple_of(2 * t * BMAX, 16)
        begins = []
        for e in (0, 1):
            flat = 2 * t + e + atoms - RIM
            begins.append(starts[lax.div(flat, atoms), lax.rem(flat, atoms)])
        for c, span in enumerate(lanes):
            both = [ext[c, pl.ds(begin, BMAX), :] for begin in begins]
            padded[pl.ds(at, 2 * BMAX), span] = jnp.concatenate(both, axis=0).astype(BF16)
        for c in (0, 1):
            both = [pext[c, pl.ds(begin, BMAX), :] for begin in begins]
            ppadded[pl.ds(at, 2 * BMAX), c * half:(c + 1) * half] = jnp.concatenate(both, axis=0).astype(BF16)
        return carry

    def project(g, carry):
        at = pl.ds(pl.multiple_of(g * GROUP * BMAX, 16), WIN)
        base[g] = jnp.dot(band[g], padded[at, :], preferred_element_type=F32)
        lean[g] = jnp.dot(band[g], ppadded[at, :], preferred_element_type=F32).astype(BF16)
        return carry

    def bands(low, high):
        lax.fori_loop(low, high, band_step, 0)

    def gathers(low, high):
        lax.fori_loop(low, high, gather, 0)

    def projects(low, high):
        lax.fori_loop(low, high, project, 0)

    begin_copy.wait()
    inside_from, inside_to = RIM // 2, (atoms + RIM) // 2
    inside_mid = (inside_from + inside_to) // 2
    eighth = groups // 4
    works = [functools.partial(bands, t * eighth, (t + 1) * eighth) for t in range(4)]
    works += [functools.partial(gathers, inside_from, inside_mid), functools.partial(gathers, inside_mid, inside_to)]
    works += [functools.partial(projects, g, g + 1) for g in range(1, groups - 1)]
    if chunks == 4:
        order = [
            [],
            [(after_first, 1)],
            [(after_first, 0)],
            [(after_fold, 1, 0)],
            [(after_first, 2), (after_first, 3), (after_fold, 0, 0)],
            [],
            [(after_fold, 2, 0), (after_fold, 1, 1), (after_fold, 3, 0)],
            [],
            [(after_fold, 0, 1), (after_fold, 2, 1)],
            [],
            [(after_fold, 3, 1), (start_halos, 1, 2)],
            [],
        ]
    else:
        every = range(chunks)
        order = [[], [(after_first, c) for c in every] + [(start_halos, 1, 2)]]
        order += [[(after_fold, c, turn) for c in every] for turn in range(len(rounds(0)))]
        order += [[] for _ in works[len(order):]]
    for work, events in zip(works, order, strict=True):
        work()
        for event in events:
            event[0](*event[1:])

    size = GROUP * NPMAX
    same = (iota(size, size, 0) & (GROUP - 1)) == (iota(size, size, 1) & (GROUP - 1))
    expand = jnp.where(group_of(size, size, 0, GROUP, NPMAX) == (iota(size, size, 1) & (NPMAX - 1)), 1.0, 0.0).astype(BF16)
    owner = group_of(GROUP, size, 1, NPMAX, NPMAX)

    def tail(span, g):
        update = lax.dot_general(lean[g], mix_ref[span, :], across, preferred_element_type=F32)
        rounded = (base[g, :, span] - update).astype(BF16)
        weighted = (rounded.astype(F32) * weight[:, span]).astype(BF16)
        return lax.dot_general(weighted, rounded, across, preferred_element_type=F32)

    def finish(product, g):
        kept = jnp.where(same, product, 0.0)
        top = kept.astype(BF16)
        rest = (kept - top.astype(F32)).astype(BF16)
        spread = jnp.dot(top, expand, preferred_element_type=F32) + jnp.dot(rest, expand, preferred_element_type=F32)
        result = jnp.zeros((GROUP, size), F32)
        for i in range(NPMAX):
            result = jnp.where(owner == i, spread[i * GROUP:(i + 1) * GROUP, :], result)
        dens[pl.ds(pl.multiple_of(g * GROUP, GROUP), GROUP), :] = result

    cut = vec.shape[1] // 2
    first_half, second_half = slice(0, cut), slice(cut, 2 * cut)
    batch = max(d for d in (3, 2, 1) if (groups - 2) % d == 0)

    def tail_first(t, carry):
        for e in range(batch):
            g = 1 + t * batch + e
            full[g] = tail(first_half, g)
        return carry

    def tail_second(t, carry):
        products = [full[1 + t * batch + e] + tail(second_half, 1 + t * batch + e) for e in range(batch)]
        for e, product in enumerate(products):
            finish(product, 1 + t * batch + e)
        return carry

    for c in range(0, max(1, chunks // 2)):
        after_last(c)
    lax.fori_loop(0, (groups - 2) // batch, tail_first, 0)
    for c in range(max(1, chunks // 2), chunks):
        after_last(c)
    lax.fori_loop(0, (groups - 2) // batch, tail_second, 0)
    share = own_ref.shape[0]
    inside = share - GROUP

    def den_copy(start, count, slot):
        src = pl.ds(pl.multiple_of(start, GROUP), count)
        dst = pl.ds(pl.multiple_of(start - other * share, GROUP), count)
        return remote(dens.at[src], got_ref.at[dst], den_sems, (slot,), (row, other))

    sent = [den_copy(other * share + GROUP * col, inside, 0), den_copy(other * (atoms - GROUP), GROUP, 1)]
    sent[0].start()

    for copy in pan_halos + vec_halos:
        copy.wait()
    for side, at in ((0, 0), (1, HALO + rows)):
        block = halo_ref[side].astype(F32)
        for c, span in enumerate(lanes):
            ext[c, at:at + HALO, :] = block[:, span]
        for which in (0, 1):
            pext[which, at:at + HALO, :] = pan_ref[which, at:at + HALO, :].astype(F32)
    lax.fori_loop(0, RIM // 2, gather, 0)
    lax.fori_loop((atoms + RIM) // 2, (atoms + 2 * RIM) // 2, gather, 0)

    every = slice(0, 2 * cut)
    theirs, ours = other * (groups - 1), col * (groups - 1)
    project(theirs, 0)
    product = tail(every, theirs)
    project(ours, 0)
    finish(product, theirs)
    sent[1].start()
    finish(tail(every, ours), ours)
    own_ref[...] = dens[pl.ds(pl.multiple_of(col * share, share), share), :]

    for copy in sent:
        copy.wait()
    swap.wait_send()
    for copy in count_copies:
        copy.wait_send()
    for c in range(chunks):
        for step in first_steps(c):
            first_copy(c, step).wait_send()
            last_copy(c, step).wait_send()
        for turn in rounds(c):
            fold_copy(c, turn).wait_send()


def vector_kernel(vin_ref, pan_ref, mix_ref, own_ref, got_ref, vec_hbm, den_ref, done, sems):
    tiles = sems.shape[0]
    tile = vin_ref.shape[0] // tiles
    den_ref[...] = own_ref[...] + got_ref[...]
    copies = []
    for t in range(tiles):
        at = slice(t * tile, (t + 1) * tile)
        inside = slice(HALO + t * tile, HALO + (t + 1) * tile)
        panel = jnp.concatenate([pan_ref[0, inside, :], pan_ref[1, inside, :]], axis=1)
        update = lax.dot_general(panel, mix_ref[...], (((1,), (1,)), ((), ())), preferred_element_type=F32)
        done[at, :] = (vin_ref[at, :].astype(F32) - update).astype(BF16)
        copies.append(pltpu.make_async_copy(done.at[at], vec_hbm.at[at], sems.at[t]))
        copies[-1].start()
    for copy in copies:
        copy.wait()


def local(vectors_in, panel, factor, atom_basis, proj_count, coupling, block_present, occ_mask, occ_weight):
    n = lax.axis_size("row")
    rows, cols = vectors_in.shape
    half = panel.shape[1]
    npan = factor.shape[0]
    atoms = atom_basis.shape[1]
    groups = atoms // GROUP
    share = atoms // lax.axis_size("col")
    wide = coupling.shape[2]
    vmem = pl.BlockSpec(memory_space=pltpu.VMEM)
    hbm = pl.BlockSpec(memory_space=pl.ANY)
    plane = max(d for d in range(1, n + 1) if n % d == 0 and d * d <= n)
    most, least = max(plane, n // plane), min(plane, n // plane)
    chunks = max(1, cols // (n * 16))
    width = cols // chunks
    unit = width // n
    turns = most.bit_length() - 1
    ext_rows = rows + 2 * HALO
    pad_rows = (groups - 1) * GROUP * BMAX + WIN
    dma = pltpu.SemaphoreType.DMA
    operands = (vectors_in, panel, jnp.swapaxes(coupling, 0, 1), factor, atom_basis, proj_count[None, :], block_present.T,
                occ_mask[None, :], occ_weight[None, :])
    operands = [pltpu.with_memory_space_constraint(x, pltpu.HBM) for x in operands]
    vin, pan, mix, own, got = pl.pallas_call(
        functools.partial(mix_kernel, n, plane),
        out_shape=(
            jax.ShapeDtypeStruct((rows, cols), BF16),
            jax.ShapeDtypeStruct((2, ext_rows, half), BF16),
            jax.ShapeDtypeStruct((cols, npan), BF16),
            jax.ShapeDtypeStruct((share, NPMAX * NPMAX), F32),
            jax.ShapeDtypeStruct((share, NPMAX * NPMAX), F32),
        ),
        in_specs=[hbm] * 9,
        out_specs=(vmem,) * 5,
        scratch_shapes=[
            *[pltpu.VMEM(x.shape, x.dtype) for x in operands[3:]],
            pltpu.VMEM((npan, rows), BF16),
            pltpu.VMEM((chunks, width, npan), BF16),
            pltpu.VMEM((chunks, most, width // least, npan), BF16),
            pltpu.VMEM((chunks, turns, width // least, npan), BF16),
            pltpu.VMEM((chunks, turns, width // least, npan), BF16),
            pltpu.VMEM((npan, npan), BF16),
            pltpu.VMEM((npan, npan), BF16),
            pltpu.VMEM((2, 1, atoms), jnp.int32),
            pltpu.VMEM((atoms, atoms), F32),
            pltpu.VMEM((K, atoms, wide), BF16),
            pltpu.VMEM((2, HALO, cols), BF16),
            pltpu.VMEM((wide // 128, (2 * GROUP + K - 2) * GROUP, 128), F32),
            pltpu.VMEM((groups, GROUP * NPMAX, WIN), BF16),
            pltpu.VMEM((8, atoms), jnp.int32),
            pltpu.SMEM((8, atoms), jnp.int32),
            pltpu.VMEM((cols // 128, ext_rows + BMAX, 128), F32),
            pltpu.VMEM((2, ext_rows + BMAX, half), F32),
            pltpu.VMEM((pad_rows, cols), BF16),
            pltpu.VMEM((pad_rows, npan), BF16),
            pltpu.VMEM((groups, GROUP * NPMAX, cols), F32),
            pltpu.VMEM((groups, GROUP * NPMAX, npan), BF16),
            pltpu.VMEM((groups, GROUP * NPMAX, GROUP * NPMAX), F32),
            pltpu.VMEM((atoms, NPMAX * NPMAX), F32),
            pltpu.VMEM((1, cols), F32),
            dma((2,)), dma((6,)), dma, dma, dma, dma((2, 5)), dma((2, 2, PIECES)), dma((2, 2)),
            dma((2, chunks, 2, most)), dma((2, chunks, turns)), dma((2, 2)),
        ],
        compiler_params=pltpu.CompilerParams(collective_id=0, has_side_effects=True, vmem_limit_bytes=48 << 20),
        cost_estimate=pl.CostEstimate(flops=8 * 10**9, bytes_accessed=10 << 20, transcendentals=0),
    )(*operands)

    return pl.pallas_call(
        vector_kernel,
        out_shape=(
            jax.ShapeDtypeStruct((rows, cols), BF16),
            jax.ShapeDtypeStruct((share, NPMAX * NPMAX), F32),
        ),
        in_specs=[vmem] * 5,
        out_specs=[hbm, vmem],
        scratch_shapes=[pltpu.VMEM((rows, cols), BF16), dma((8,))],
        compiler_params=pltpu.CompilerParams(vmem_limit_bytes=16 << 20),
        cost_estimate=pl.CostEstimate(flops=6 * 10**9, bytes_accessed=10 << 20, transcendentals=0),
    )(vin, pan, mix, own, got)


def solution(mesh):
    placed = (
        P("row", "col"),
        P("row", "col"),
        P(),
        P("row", None),
        P("row"),
        P("row", None, None),
        P("row", None),
        P("col"),
        P("col"),
    )
    return jax.shard_map(
        local,
        mesh=mesh,
        in_specs=placed,
        out_specs=(P("row", "col"), P(("row", "col"), None)),
        check_vma=False,
    )
```

```python
import functools

import jax
import jax.numpy as jnp
from jax import lax
from jax.experimental import pallas as pl
from jax.experimental.pallas import tpu as pltpu
from jax.sharding import PartitionSpec as P

NPMAX = 16
BMAX = 24
K = 9
RIM = (K - 1) // 2
HALO = RIM * BMAX
PIECES = 6
GROUP = 16
SUB = 8
WIN = -(-(SUB + K - 1) * BMAX // 128) * 128
REACH = SUB + K - 1
F32 = jnp.float32
BF16 = jnp.bfloat16
MESH = pl.DeviceIdType.MESH


def iota(rows, columns, axis):
    return lax.broadcasted_iota(jnp.int32, (rows, columns), axis)


def group_of(rows, columns, axis, size, most):
    small = (8, columns) if axis == 1 else (rows, 128)
    index = iota(*small, axis)
    group = jnp.zeros(small, jnp.int32)
    for edge in range(1, most):
        group = group + jnp.where(index >= edge * size, 1, 0)
    return jnp.tile(group, (rows // small[0], columns // small[1]))


def mix_kernel(n, plane, vec_hbm, panel_hbm, coupling_hbm, factor_hbm, basis_hbm, proj_hbm, present_hbm, mask_hbm, occ_hbm,
               vec, pan_ref, mix_ref, own_ref, got_ref,
               factor_ref, basis_ref, proj_ref, present_ref, mask_ref, occ_ref,
               pan_t, part, got_first, middle, got_second, factor_hi, factor_lo, counts, limit, cm_ref, halo_ref, skew, band,
               first_ref, starts, ext, pext, padded, ppadded, base, lean, full, dens, weight,
               load_sem, small_sem, own_sem, cm_sem, start_sem, pan_sems, halo_sems, count_sems, ring_sems, fold_sems, den_sems):
    row, col = lax.axis_index("row"), lax.axis_index("col")
    other = 1 - col
    up, down = lax.rem(row + 1, n), lax.rem(row + n - 1, n)
    rows, half = panel_hbm.shape
    chunks, wide_c, npan = part.shape
    unit = wide_c // n
    atoms, wide = cm_ref.shape[1:]
    groups = atoms // GROUP
    body = pl.ds(HALO, rows)
    q, p = n // plane, plane
    line, spot = lax.div(row, p), lax.rem(row, p)
    contract = (((0,), (0,)), ((), ()))
    across = (((1,), (1,)), ((), ()))

    def plane_peer(step):
        return line * p + lax.rem(spot + step, p)

    def line_peer(step):
        return lax.rem(line + step, q) * p + spot

    by_plane, by_line = (p, spot, plane_peer), (q, line, line_peer)
    ways = [(by_line, by_plane) if chunks == 4 and c == 2 else (by_plane, by_line) for c in range(chunks)]

    own = pltpu.make_async_copy(panel_hbm, pan_ref.at[col, body], own_sem)
    own.start()
    pieces = rows // load_sem.shape[0]
    loads = [pltpu.make_async_copy(vec_hbm.at[pl.ds(i * pieces, pieces)], vec.at[pl.ds(i * pieces, pieces)], load_sem.at[i])
             for i in range(load_sem.shape[0])]
    for load in loads:
        load.start()
    small = [pltpu.make_async_copy(src, dst, small_sem.at[i]) for i, (src, dst) in enumerate((
        (basis_hbm, basis_ref), (factor_hbm, factor_ref), (proj_hbm, proj_ref), (present_hbm, present_ref),
        (mask_hbm, mask_ref), (occ_hbm, occ_ref)))]
    for load in small:
        load.start()
    blocks = pltpu.make_async_copy(coupling_hbm, cm_ref, cm_sem)

    barrier = pltpu.get_barrier_semaphore()
    greeted = [(plane_peer(step), col) for step in range(1, p)] + [(line_peer(step), col) for step in range(1, q)]
    greeted += [(row, other)]
    for target in greeted:
        pl.semaphore_signal(barrier, inc=1, device_id=target, device_id_type=MESH)
    length = ext.shape[1]
    edge = rows + HALO
    ext[:, edge:, :] = jnp.zeros((ext.shape[0], length - edge, 128), F32)
    pext[:, edge:, :] = jnp.zeros((2, length - edge, half), F32)
    low = (SUB - 1) * SUB
    skew[:, :, 0:low, :] = jnp.zeros((*skew.shape[:2], low, 128), F32)
    skew[:, :, low + K * SUB:, :] = jnp.zeros((*skew.shape[:2], low, 128), F32)
    pl.semaphore_wait(barrier, len(greeted))

    def remote(src, dst, sems, slot, target):
        return pltpu.make_async_remote_copy(
            src_ref=src, dst_ref=dst, send_sem=sems.at[(0,) + slot], recv_sem=sems.at[(1,) + slot],
            device_id=target, device_id_type=MESH)

    swap = remote(panel_hbm, pan_ref.at[col, body], pan_sems, (0,), (row, other))
    swap.start()
    count_copies = [
        remote(basis_hbm, counts.at[side], count_sems, (side,), (target, col))
        for side, target in ((0, up), (1, down))
    ]
    pan_halos, passed, vec_halos = [], [], []
    for side, target in ((0, up), (1, down)):
        src_at = rows - HALO if side == 0 else 0
        dst_at = 0 if side == 0 else HALO + rows
        pan_halos.append(remote(panel_hbm.at[pl.ds(src_at, HALO)], pan_ref.at[col, pl.ds(dst_at, HALO)],
                                pan_sems, (1 + side,), (target, col)))
        ghost = pan_ref.at[col, pl.ds(dst_at, HALO)]
        passed.append(remote(ghost, ghost, pan_sems, (3 + side,), (row, other)))
        for piece in range(PIECES):
            part_at = piece * (HALO // PIECES)
            vec_halos.append(remote(vec_hbm.at[pl.ds(src_at + part_at, HALO // PIECES)],
                                    halo_ref.at[side, pl.ds(part_at, HALO // PIECES)], halo_sems, (side, piece), (target, col)))

    own.wait()
    pan_t[pl.ds(pl.multiple_of(col * half, half), half), :] = pan_ref[col, body, :].T
    for load in small:
        load.wait()
    high = factor_ref[...].astype(BF16)
    factor_hi[...] = high
    factor_lo[...] = (factor_ref[...] - high.astype(F32)).astype(BF16)
    weight[...] = mask_ref[...].astype(F32) * occ_ref[...] / (vec_hbm.shape[1] * lax.axis_size("col"))
    for load in loads:
        load.wait()
    blocks.start()

    swap.wait_recv()
    pan_t[pl.ds(pl.multiple_of(other * half, half), half), :] = pan_ref[other, body, :].T

    def span_of(c):
        return slice(c * wide_c, (c + 1) * wide_c)

    def first_copy(c, step):
        (size, at, peer), (size_s, _, _) = ways[c]
        length = size_s * unit
        src = pl.ds(pl.multiple_of(lax.rem(at + step, size) * length, unit), length)
        return remote(part.at[c, src], got_first.at[c, step, pl.ds(0, length)], ring_sems, (c, 0, step), (peer(step), col))

    def rounds(c):
        return range(ways[c][1][0].bit_length() - 1)

    def fold_copy(c, turn):
        _, (size, at, peer) = ways[c]
        reach = 1 << turn
        ahead = lax.rem(lax.div(at, reach), 2)
        step = reach + ahead * (size - 2 * reach)
        length = size * unit
        return remote(middle.at[c, turn, pl.ds(0, length)], got_second.at[c, turn, pl.ds(0, length)],
                      fold_sems, (c, turn), (peer(step), col))

    def own_block(c):
        (_, at, _), (size_s, _, _) = ways[c]
        return pl.multiple_of(c * wide_c + at * size_s * unit, unit)

    def last_copy(c, step):
        (_, _, peer), (size_s, _, _) = ways[c]
        mine = pl.ds(own_block(c), size_s * unit)
        return remote(mix_ref.at[mine], mix_ref.at[mine], ring_sems, (c, 1, step), (peer(step), col))

    def first_steps(c):
        return range(1, ways[c][0][0])

    def after_first(c):
        (_, at, _), (size_s, _, _) = ways[c]
        length = size_s * unit
        for step in first_steps(c):
            first_copy(c, step).wait_recv()
        total = part[c, pl.ds(pl.multiple_of(at * length, unit), length), :].astype(F32)
        for step in first_steps(c):
            total = total + got_first[c, step, 0:length, :].astype(F32)
        middle[c, 0, 0:length, :] = total.astype(BF16)
        fold_copy(c, 0).start()

    def after_fold(c, turn):
        length = ways[c][1][0] * unit
        fold_copy(c, turn).wait_recv()
        inner = middle[c, turn, 0:length, :].astype(F32) + got_second[c, turn, 0:length, :].astype(F32)
        top = inner.astype(BF16)
        if turn + 1 < len(rounds(c)):
            middle[c, turn + 1, 0:length, :] = top
            fold_copy(c, turn + 1).start()
            return
        rest = (inner - top.astype(F32)).astype(BF16)
        both = jnp.dot(jnp.concatenate([top, rest], axis=0), factor_hi[...], preferred_element_type=F32)
        mixed = both[0:length] + both[length:] + jnp.dot(top, factor_lo[...], preferred_element_type=F32)
        mix_ref[pl.ds(own_block(c), length), :] = mixed.astype(BF16)
        for step in first_steps(c):
            last_copy(c, step).start()

    def after_last(c):
        for step in first_steps(c):
            last_copy(c, step).wait_recv()

    def greet_neighbours():
        for copy in count_copies + pan_halos:
            copy.start()

    def pass_on():
        for copy in pan_halos:
            copy.wait_recv()
        for copy in passed:
            copy.start()

    def start_halos(*which):
        for piece in which:
            for copy in vec_halos[piece::PIECES]:
                copy.start()

    for pair in ([(1, 2), (0, 3)] if chunks == 4 else [range(chunks)]):
        columns = jnp.concatenate([vec[:, span_of(c)] for c in pair], axis=1)
        inner = jnp.dot(pan_t[...], columns, preferred_element_type=F32).T.astype(BF16)
        for at, c in enumerate(pair):
            part[c] = inner[at * wide_c:(at + 1) * wide_c]
            for step in first_steps(c):
                first_copy(c, step).start()

    lanes = [slice(c * 128, (c + 1) * 128) for c in range(ext.shape[0])]
    chunk_rows = rows // 8

    def widen(t, carry):
        at = pl.multiple_of(t * chunk_rows, 16)
        block = vec[pl.ds(at, chunk_rows), :].astype(F32)
        for c, span in enumerate(lanes):
            ext[c, pl.ds(HALO + at, chunk_rows), :] = block[:, span]
        return carry

    lax.fori_loop(0, 8, widen, 0)

    for which in (0, 1):
        pext[which, HALO:HALO + rows, :] = pan_ref[which, body, :].astype(F32)
    here = basis_ref[...].astype(F32)
    lower = jnp.where(iota(atoms, atoms, 0) < iota(atoms, atoms, 1), 1.0, 0.0).astype(BF16)
    at = iota(1, atoms, 1)

    def tables(prev, post, which):
        table = jnp.concatenate([prev, here, post, jnp.zeros((5, atoms), F32)], axis=0).astype(BF16)
        first = jnp.dot(table, lower, preferred_element_type=F32).astype(jnp.int32)
        first_ref[which] = jnp.clip(first + (HALO - rows) + rows * iota(8, atoms, 0), 0, rows + 2 * HALO)
        copy = pltpu.make_async_copy(first_ref.at[which], starts.at[which], start_sem.at[which])
        copy.start()
        lines = []
        for k in range(K):
            d = k - RIM
            near = here
            if d != 0:
                turn = (-d) % atoms
                inside = (at + d >= 0) & (at + d < atoms)
                near = jnp.where(inside, pltpu.roll(here, turn, 1), pltpu.roll(prev if d < 0 else post, turn, 1))
            lines.append(jnp.where(present_ref[k:k + 1, :] > 0, near, 0.0))
        lines.append(proj_ref[...].astype(F32))
        lines.append(jnp.zeros((atoms - K - 1, atoms), F32))
        limit[...] = jnp.concatenate(lines, axis=0).T
        return copy

    none = jnp.zeros((1, atoms), F32)
    begin_copy = tables(none, none, 0)
    blocks.wait()

    in_i = group_of(SUB, wide, 1, BMAX, NPMAX)
    slot = (iota(SUB, wide, 1) - BMAX * in_i).astype(F32)
    in_i = in_i.astype(F32)
    lane = iota(8, 128, 1)

    def band_piece(u, i):
        tiles = []
        for tile in range(WIN // 128):
            acc = None
            for b in range(REACH):
                to, last = max(b * BMAX, tile * 128), min((b + 1) * BMAX, (tile + 1) * 128)
                while to < last:
                    source = i * BMAX + to - b * BMAX
                    count = min(last - to, 128 - source % 128)
                    piece = skew[u, source // 128, pl.ds((REACH - 1 - b) * SUB, SUB, stride=SUB + 1), :]
                    turn = (to - source) % 128
                    piece = piece if turn == 0 else pltpu.roll(piece, turn, 1)
                    acc = piece if acc is None else jnp.where(lane >= to % 128, piece, acc)
                    to += count
            tiles.append(acc)
        return jnp.concatenate(tiles, axis=1)

    def band_step(t, carry):
        chunk = pl.ds(pl.multiple_of(t * GROUP, GROUP), GROUP)
        bounds = limit[chunk, :]
        for u in range(GROUP // SUB):
            within = bounds[u * SUB:(u + 1) * SUB]
            valid = in_i < within[:, K:K + 1]
            for k in range(K):
                block = cm_ref[k, chunk, :].astype(F32)[u * SUB:(u + 1) * SUB]
                block = jnp.where(valid & (slot < within[:, k:k + 1]), block, 0.0)
                top = (REACH - 1 - k) * SUB
                for tile in range(wide // 128):
                    skew[u, tile, top:top + SUB, :] = block[:, tile * 128:(tile + 1) * 128]
        for u in range(GROUP // SUB):
            for i in range(0, NPMAX, 2):
                both = jnp.concatenate([band_piece(u, i), band_piece(u, i + 1)], axis=0)
                band[t * (GROUP // SUB) + u, i * SUB:(i + 2) * SUB, :] = both.astype(BF16)
        return carry

    def gather(t, carry, which=0):
        at = pl.multiple_of(2 * t * BMAX, 16)
        begins = []
        for e in (0, 1):
            flat = 2 * t + e + atoms - RIM
            begins.append(starts[which, lax.div(flat, atoms), lax.rem(flat, atoms)])
        for c, span in enumerate(lanes):
            both = [ext[c, pl.ds(begin, BMAX), :] for begin in begins]
            padded[pl.ds(at, 2 * BMAX), span] = jnp.concatenate(both, axis=0).astype(BF16)
        for c in (0, 1):
            both = [pext[c, pl.ds(begin, BMAX), :] for begin in begins]
            ppadded[pl.ds(at, 2 * BMAX), c * half:(c + 1) * half] = jnp.concatenate(both, axis=0).astype(BF16)
        return carry

    def project(s, carry=0):
        at = pl.ds(pl.multiple_of(s * SUB * BMAX, 16), WIN)
        base[s] = jnp.dot(band[s], padded[at, :], preferred_element_type=F32)
        lean[s] = jnp.dot(band[s], ppadded[at, :], preferred_element_type=F32).astype(BF16)
        return carry

    def bands(low, high):
        lax.fori_loop(low, high, band_step, 0)

    def gathers(low, high):
        lax.fori_loop(low, high, gather, 0)

    def projects(*which):
        for s in which:
            project(s)

    begin_copy.wait()
    inside_from, inside_to = RIM // 2, (atoms + RIM) // 2
    inside_mid = (inside_from + inside_to) // 2
    def outer_bands():
        for copy in count_copies:
            copy.wait_recv()
        tables(counts[0].astype(F32), counts[1].astype(F32), 1).wait()
        lax.fori_loop(0, 2, lambda t, carry: band_step(t * (groups - 1), carry), 0)

    third = (groups - 2) // 3
    works = [functools.partial(bands, 1 + t * third, 1 + (t + 1) * third) for t in range(3)]
    works += [functools.partial(gathers, inside_from, inside_mid), functools.partial(gathers, inside_mid, inside_to)]
    subs = atoms // SUB
    works += [functools.partial(projects, s, s + 1) for s in range(2, subs - 2, 2)]
    works += [outer_bands, functools.partial(projects, 1, subs - 2)]
    if chunks == 4:
        order = [
            [],
            [(after_first, 1), (greet_neighbours,), (start_halos, 0)],
            [(after_first, 0)],
            [(after_fold, 1, 0), (after_first, 2), (start_halos, 1, 2)],
            [(after_first, 3), (after_fold, 0, 0), (start_halos, 3)],
            [],
            [(after_fold, 2, 0)],
            [(after_fold, 1, 1)],
            [(after_fold, 3, 0)],
            [],
            [(after_fold, 0, 1), (after_fold, 2, 1)],
            [],
            [(after_fold, 3, 1), (start_halos, 4, 5), (pass_on,)],
        ]
    else:
        every = range(chunks)
        order = [[], [(after_first, c) for c in every] + [(greet_neighbours,), (start_halos, *range(PIECES))]]
        order += [[(after_fold, c, turn) for c in every] for turn in range(len(rounds(0)))]
        order += [[] for _ in works[len(order):-1]] + [[(pass_on,)]]
    for work, events in zip(works, order, strict=True):
        work()
        for event in events:
            event[0](*event[1:])

    size = GROUP * NPMAX
    part_size = SUB * NPMAX
    row_at, lane_at = iota(size, size, 0), iota(size, size, 1)
    same = ((row_at >= part_size) == (lane_at >= part_size)) & ((row_at & (SUB - 1)) == (lane_at & (SUB - 1)))
    expand = jnp.where(group_of(size, size, 0, SUB, size // SUB) - jnp.where(row_at >= part_size, NPMAX, 0)
                       == (lane_at & (NPMAX - 1)), 1.0, 0.0).astype(BF16)
    owner = group_of(GROUP, size, 1, NPMAX, NPMAX)
    pair_of = range(GROUP // SUB)

    def tail(span, g):
        lines = jnp.concatenate([lean[g * len(pair_of) + u] for u in pair_of], axis=0)
        update = lax.dot_general(lines, mix_ref[span, :], across, preferred_element_type=F32)
        plain = jnp.concatenate([base[g * len(pair_of) + u, :, span] for u in pair_of], axis=0)
        rounded = (plain - update).astype(BF16)
        weighted = (rounded.astype(F32) * weight[:, span]).astype(BF16)
        return lax.dot_general(weighted, rounded, across, preferred_element_type=F32)

    def finish(product, g):
        kept = jnp.where(same, product, 0.0)
        top = kept.astype(BF16)
        rest = (kept - top.astype(F32)).astype(BF16)
        spread = jnp.dot(top, expand, preferred_element_type=F32) + jnp.dot(rest, expand, preferred_element_type=F32)
        result = jnp.zeros((GROUP, size), F32)
        for i in range(NPMAX):
            rows_of = [spread[u * part_size + i * SUB:u * part_size + (i + 1) * SUB, :] for u in pair_of]
            result = jnp.where(owner == i, jnp.concatenate(rows_of, axis=0), result)
        dens[pl.ds(pl.multiple_of(g * GROUP, GROUP), GROUP), :] = result

    cut = vec.shape[1] // 2
    first_half, second_half = slice(0, cut), slice(cut, 2 * cut)
    batch = max(d for d in (3, 2, 1) if (groups - 2) % d == 0)

    def tail_first(t, carry):
        for e in range(batch):
            g = 1 + t * batch + e
            full[g] = tail(first_half, g)
        return carry

    def tail_second(t, carry):
        products = [full[1 + t * batch + e] + tail(second_half, 1 + t * batch + e) for e in range(batch)]
        for e, product in enumerate(products):
            finish(product, 1 + t * batch + e)
        return carry

    for c in range(0, max(1, chunks // 2)):
        after_last(c)
    lax.fori_loop(0, (groups - 2) // batch, tail_first, 0)
    for c in range(max(1, chunks // 2), chunks):
        after_last(c)
    lax.fori_loop(0, (groups - 2) // batch, tail_second, 0)
    share = own_ref.shape[0]
    inside = share - GROUP

    def den_copy(start, count, slot):
        src = pl.ds(pl.multiple_of(start, GROUP), count)
        dst = pl.ds(pl.multiple_of(start - other * share, GROUP), count)
        return remote(dens.at[src], got_ref.at[dst], den_sems, (slot,), (row, other))

    sent = [den_copy(other * share + GROUP * col, inside, 0), den_copy(other * (atoms - GROUP), GROUP, 1)]
    sent[0].start()

    for copy in pan_halos:
        copy.wait_send()
    for copy in passed + vec_halos:
        copy.wait()
    for side, at in ((0, 0), (1, HALO + rows)):
        block = halo_ref[side].astype(F32)
        for c, span in enumerate(lanes):
            ext[c, at:at + HALO, :] = block[:, span]
        for which in (0, 1):
            pext[which, at:at + HALO, :] = pan_ref[which, at:at + HALO, :].astype(F32)
    late_gather = functools.partial(gather, which=1)
    lax.fori_loop(0, RIM // 2, late_gather, 0)
    lax.fori_loop((atoms + RIM) // 2, (atoms + 2 * RIM) // 2, late_gather, 0)

    every = slice(0, 2 * cut)
    project(other * (subs - 1))
    theirs, ours = other * (groups - 1), col * (groups - 1)
    product = tail(every, theirs)
    project(col * (subs - 1))
    finish(product, theirs)
    sent[1].start()
    finish(tail(every, ours), ours)
    own_ref[...] = dens[pl.ds(pl.multiple_of(col * share, share), share), :]

    for copy in sent:
        copy.wait()
    swap.wait_send()
    for copy in count_copies:
        copy.wait_send()
    for c in range(chunks):
        for step in first_steps(c):
            first_copy(c, step).wait_send()
            last_copy(c, step).wait_send()
        for turn in rounds(c):
            fold_copy(c, turn).wait_send()


def vector_kernel(vin_ref, pan_ref, mix_ref, own_ref, got_ref, vec_hbm, den_ref, done, sems):
    tiles = sems.shape[0]
    tile = vin_ref.shape[0] // tiles
    den_ref[...] = own_ref[...] + got_ref[...]
    copies = []
    for t in range(tiles):
        at = slice(t * tile, (t + 1) * tile)
        inside = slice(HALO + t * tile, HALO + (t + 1) * tile)
        panel = jnp.concatenate([pan_ref[0, inside, :], pan_ref[1, inside, :]], axis=1)
        update = lax.dot_general(panel, mix_ref[...], (((1,), (1,)), ((), ())), preferred_element_type=F32)
        done[at, :] = (vin_ref[at, :].astype(F32) - update).astype(BF16)
        copies.append(pltpu.make_async_copy(done.at[at], vec_hbm.at[at], sems.at[t]))
        copies[-1].start()
    for copy in copies:
        copy.wait()


def local(vectors_in, panel, factor, atom_basis, proj_count, coupling, block_present, occ_mask, occ_weight):
    n = lax.axis_size("row")
    rows, cols = vectors_in.shape
    half = panel.shape[1]
    npan = factor.shape[0]
    atoms = atom_basis.shape[1]
    groups = atoms // GROUP
    share = atoms // lax.axis_size("col")
    wide = coupling.shape[2]
    vmem = pl.BlockSpec(memory_space=pltpu.VMEM)
    hbm = pl.BlockSpec(memory_space=pl.ANY)
    plane = max(d for d in range(1, n + 1) if n % d == 0 and d * d <= n)
    most, least = max(plane, n // plane), min(plane, n // plane)
    chunks = max(1, cols // (n * 16))
    width = cols // chunks
    unit = width // n
    turns = most.bit_length() - 1
    ext_rows = rows + 2 * HALO
    subs = atoms // SUB
    pad_rows = (subs - 1) * SUB * BMAX + WIN
    dma = pltpu.SemaphoreType.DMA
    operands = (vectors_in, panel, jnp.swapaxes(coupling, 0, 1), factor, atom_basis, proj_count[None, :], block_present.T,
                occ_mask[None, :], occ_weight[None, :])
    operands = [pltpu.with_memory_space_constraint(x, pltpu.HBM) for x in operands]
    vin, pan, mix, own, got = pl.pallas_call(
        functools.partial(mix_kernel, n, plane),
        out_shape=(
            jax.ShapeDtypeStruct((rows, cols), BF16),
            jax.ShapeDtypeStruct((2, ext_rows, half), BF16),
            jax.ShapeDtypeStruct((cols, npan), BF16),
            jax.ShapeDtypeStruct((share, NPMAX * NPMAX), F32),
            jax.ShapeDtypeStruct((share, NPMAX * NPMAX), F32),
        ),
        in_specs=[hbm] * 9,
        out_specs=(vmem,) * 5,
        scratch_shapes=[
            *[pltpu.VMEM(x.shape, x.dtype) for x in operands[3:]],
            pltpu.VMEM((npan, rows), BF16),
            pltpu.VMEM((chunks, width, npan), BF16),
            pltpu.VMEM((chunks, most, width // least, npan), BF16),
            pltpu.VMEM((chunks, turns, width // least, npan), BF16),
            pltpu.VMEM((chunks, turns, width // least, npan), BF16),
            pltpu.VMEM((npan, npan), BF16),
            pltpu.VMEM((npan, npan), BF16),
            pltpu.VMEM((2, 1, atoms), jnp.int32),
            pltpu.VMEM((atoms, atoms), F32),
            pltpu.VMEM((K, atoms, wide), BF16),
            pltpu.VMEM((2, HALO, cols), BF16),
            pltpu.VMEM((GROUP // SUB, wide // 128, (2 * SUB + K - 2) * SUB, 128), F32),
            pltpu.VMEM((subs, SUB * NPMAX, WIN), BF16),
            pltpu.VMEM((2, 8, atoms), jnp.int32),
            pltpu.SMEM((2, 8, atoms), jnp.int32),
            pltpu.VMEM((cols // 128, ext_rows + BMAX, 128), F32),
            pltpu.VMEM((2, ext_rows + BMAX, half), F32),
            pltpu.VMEM((pad_rows, cols), BF16),
            pltpu.VMEM((pad_rows, npan), BF16),
            pltpu.VMEM((subs, SUB * NPMAX, cols), F32),
            pltpu.VMEM((subs, SUB * NPMAX, npan), BF16),
            pltpu.VMEM((groups, GROUP * NPMAX, GROUP * NPMAX), F32),
            pltpu.VMEM((atoms, NPMAX * NPMAX), F32),
            pltpu.VMEM((1, cols), F32),
            dma((2,)), dma((6,)), dma, dma, dma((2,)), dma((2, 5)), dma((2, 2, PIECES)), dma((2, 2)),
            dma((2, chunks, 2, most)), dma((2, chunks, turns)), dma((2, 2)),
        ],
        compiler_params=pltpu.CompilerParams(collective_id=0, has_side_effects=True, vmem_limit_bytes=48 << 20),
        cost_estimate=pl.CostEstimate(flops=8 * 10**9, bytes_accessed=10 << 20, transcendentals=0),
    )(*operands)

    return pl.pallas_call(
        vector_kernel,
        out_shape=(
            jax.ShapeDtypeStruct((rows, cols), BF16),
            jax.ShapeDtypeStruct((share, NPMAX * NPMAX), F32),
        ),
        in_specs=[vmem] * 5,
        out_specs=[hbm, vmem],
        scratch_shapes=[pltpu.VMEM((rows, cols), BF16), dma((8,))],
        compiler_params=pltpu.CompilerParams(vmem_limit_bytes=16 << 20),
        cost_estimate=pl.CostEstimate(flops=6 * 10**9, bytes_accessed=10 << 20, transcendentals=0),
    )(vin, pan, mix, own, got)


def solution(mesh):
    placed = (
        P("row", "col"),
        P("row", "col"),
        P(),
        P("row", None),
        P("row"),
        P("row", None, None),
        P("row", None),
        P("col"),
        P("col"),
    )
    return jax.shard_map(
        local,
        mesh=mesh,
        in_specs=placed,
        out_specs=(P("row", "col"), P(("row", "col"), None)),
        check_vma=False,
    )
```

```python
import functools

import jax
import jax.numpy as jnp
from jax import lax
from jax.experimental import pallas as pl
from jax.experimental.pallas import tpu as pltpu
from jax.sharding import PartitionSpec as P

NPMAX = 16
BMAX = 24
K = 9
RIM = (K - 1) // 2
HALO = RIM * BMAX
PIECES = 6
HALO_ORDER = (0, 6, 1, 7, 2, 8, 3, 9, 4, 5, 10, 11)
GROUP = 16
SUB = 8
WIN = -(-(SUB + K - 1) * BMAX // 128) * 128
REACH = SUB + K - 1
F32 = jnp.float32
BF16 = jnp.bfloat16
MESH = pl.DeviceIdType.MESH


def iota(rows, columns, axis):
    return lax.broadcasted_iota(jnp.int32, (rows, columns), axis)


def group_of(rows, columns, axis, size, most):
    small = (8, columns) if axis == 1 else (rows, 128)
    index = iota(*small, axis)
    group = jnp.zeros(small, jnp.int32)
    for edge in range(1, most):
        group = group + jnp.where(index >= edge * size, 1, 0)
    return jnp.tile(group, (rows // small[0], columns // small[1]))


def mix_kernel(n, plane, vec_hbm, panel_hbm, coupling_hbm, factor_hbm, basis_hbm, proj_hbm, present_hbm, mask_hbm, occ_hbm,
               vec, pan_ref, mix_ref, own_ref, got_ref,
               factor_ref, basis_ref, proj_ref, present_ref, mask_ref, occ_ref,
               pan_t, part, got_first, middle, got_second, factor_hi, factor_lo, counts, limit, cm_ref, halo_ref, skew, band,
               first_ref, starts, ext, pext, padded, ppadded, base, lean, full, dens, weight,
               load_sem, small_sem, own_sem, cm_sem, start_sem, pan_sems, halo_sems, count_sems, ring_sems, fold_sems, den_sems):
    row, col = lax.axis_index("row"), lax.axis_index("col")
    other = 1 - col
    up, down = lax.rem(row + 1, n), lax.rem(row + n - 1, n)
    rows, half = panel_hbm.shape
    chunks, wide_c, npan = part.shape
    unit = wide_c // n
    atoms, wide = cm_ref.shape[1:]
    groups = atoms // GROUP
    body = pl.ds(HALO, rows)
    q, p = n // plane, plane
    line, spot = lax.div(row, p), lax.rem(row, p)
    contract = (((0,), (0,)), ((), ()))
    across = (((1,), (1,)), ((), ()))

    def plane_peer(step):
        return line * p + lax.rem(spot + step, p)

    def line_peer(step):
        return lax.rem(line + step, q) * p + spot

    by_plane, by_line = (p, spot, plane_peer), (q, line, line_peer)
    ways = [(by_line, by_plane) if chunks == 4 and c == 2 else (by_plane, by_line) for c in range(chunks)]

    own = pltpu.make_async_copy(panel_hbm, pan_ref.at[col, body], own_sem)
    own.start()
    pieces = rows // load_sem.shape[0]
    loads = [pltpu.make_async_copy(vec_hbm.at[pl.ds(i * pieces, pieces)], vec.at[pl.ds(i * pieces, pieces)], load_sem.at[i])
             for i in range(load_sem.shape[0])]
    for load in loads:
        load.start()
    small = [pltpu.make_async_copy(src, dst, small_sem.at[i]) for i, (src, dst) in enumerate((
        (basis_hbm, basis_ref), (factor_hbm, factor_ref), (proj_hbm, proj_ref), (present_hbm, present_ref),
        (mask_hbm, mask_ref), (occ_hbm, occ_ref)))]
    for load in small:
        load.start()
    blocks = pltpu.make_async_copy(coupling_hbm, cm_ref, cm_sem)

    barrier = pltpu.get_barrier_semaphore()
    greeted = [(plane_peer(step), col) for step in range(1, p)] + [(line_peer(step), col) for step in range(1, q)]
    greeted += [(row, other)]
    for target in greeted:
        pl.semaphore_signal(barrier, inc=1, device_id=target, device_id_type=MESH)
    length = ext.shape[1]
    edge = rows + HALO
    ext[:, edge:, :] = jnp.zeros((ext.shape[0], length - edge, 128), F32)
    pext[:, edge:, :] = jnp.zeros((2, length - edge, half), F32)
    low = (SUB - 1) * SUB
    skew[:, :, 0:low, :] = jnp.zeros((*skew.shape[:2], low, 128), F32)
    skew[:, :, low + K * SUB:, :] = jnp.zeros((*skew.shape[:2], low, 128), F32)
    pl.semaphore_wait(barrier, len(greeted))

    def remote(src, dst, sems, slot, target):
        return pltpu.make_async_remote_copy(
            src_ref=src, dst_ref=dst, send_sem=sems.at[(0,) + slot], recv_sem=sems.at[(1,) + slot],
            device_id=target, device_id_type=MESH)

    swap = remote(panel_hbm, pan_ref.at[col, body], pan_sems, (0,), (row, other))
    swap.start()
    count_copies = [
        remote(basis_hbm, counts.at[side], count_sems, (side,), (target, col))
        for side, target in ((0, up), (1, down))
    ]
    pan_halos, passed, vec_halos = [], [], []
    for side, target in ((0, up), (1, down)):
        src_at = rows - HALO if side == 0 else 0
        dst_at = 0 if side == 0 else HALO + rows
        pan_halos.append(remote(panel_hbm.at[pl.ds(src_at, HALO)], pan_ref.at[col, pl.ds(dst_at, HALO)],
                                pan_sems, (1 + side,), (target, col)))
        ghost = pan_ref.at[col, pl.ds(dst_at, HALO)]
        passed.append(remote(ghost, ghost, pan_sems, (3 + side,), (row, other)))
    far = jnp.where(row == n - 1, 0, 1)
    for side in (far, 1 - far):
        target = jnp.where(side == 0, up, down)
        src_at = (rows - HALO) * (1 - side)
        for piece in range(PIECES):
            part_at = piece * (HALO // PIECES)
            src = pl.ds(pl.multiple_of(src_at + part_at, HALO // PIECES), HALO // PIECES)
            vec_halos.append(remote(vec_hbm.at[src], halo_ref.at[side, pl.ds(part_at, HALO // PIECES)],
                                    halo_sems, (side, piece), (target, col)))

    own.wait()
    pan_t[pl.ds(pl.multiple_of(col * half, half), half), :] = pan_ref[col, body, :].T
    for load in small:
        load.wait()
    high = factor_ref[...].astype(BF16)
    factor_hi[...] = high
    factor_lo[...] = (factor_ref[...] - high.astype(F32)).astype(BF16)
    weight[...] = mask_ref[...].astype(F32) * occ_ref[...] / (vec_hbm.shape[1] * lax.axis_size("col"))
    for load in loads:
        load.wait()
    blocks.start()

    swap.wait_recv()
    pan_t[pl.ds(pl.multiple_of(other * half, half), half), :] = pan_ref[other, body, :].T

    def span_of(c):
        return slice(c * wide_c, (c + 1) * wide_c)

    def first_copy(c, step):
        (size, at, peer), (size_s, _, _) = ways[c]
        length = size_s * unit
        src = pl.ds(pl.multiple_of(lax.rem(at + step, size) * length, unit), length)
        return remote(part.at[c, src], got_first.at[c, step, pl.ds(0, length)], ring_sems, (c, 0, step), (peer(step), col))

    def rounds(c):
        return range(ways[c][1][0].bit_length() - 1)

    def fold_copy(c, turn):
        _, (size, at, peer) = ways[c]
        reach = 1 << turn
        ahead = lax.rem(lax.div(at, reach), 2)
        step = reach + ahead * (size - 2 * reach)
        length = size * unit
        return remote(middle.at[c, turn, pl.ds(0, length)], got_second.at[c, turn, pl.ds(0, length)],
                      fold_sems, (c, turn), (peer(step), col))

    def own_block(c):
        (_, at, _), (size_s, _, _) = ways[c]
        return pl.multiple_of(c * wide_c + at * size_s * unit, unit)

    def last_copy(c, step):
        (_, _, peer), (size_s, _, _) = ways[c]
        mine = pl.ds(own_block(c), size_s * unit)
        return remote(mix_ref.at[mine], mix_ref.at[mine], ring_sems, (c, 1, step), (peer(step), col))

    def first_steps(c):
        return range(1, ways[c][0][0])

    def after_first(c):
        (_, at, _), (size_s, _, _) = ways[c]
        length = size_s * unit
        for step in first_steps(c):
            first_copy(c, step).wait_recv()
        total = part[c, pl.ds(pl.multiple_of(at * length, unit), length), :].astype(F32)
        for step in first_steps(c):
            total = total + got_first[c, step, 0:length, :].astype(F32)
        middle[c, 0, 0:length, :] = total.astype(BF16)
        fold_copy(c, 0).start()

    def after_fold(c, turn):
        length = ways[c][1][0] * unit
        fold_copy(c, turn).wait_recv()
        inner = middle[c, turn, 0:length, :].astype(F32) + got_second[c, turn, 0:length, :].astype(F32)
        top = inner.astype(BF16)
        if turn + 1 < len(rounds(c)):
            middle[c, turn + 1, 0:length, :] = top
            fold_copy(c, turn + 1).start()
            return
        rest = (inner - top.astype(F32)).astype(BF16)
        both = jnp.dot(jnp.concatenate([top, rest], axis=0), factor_hi[...], preferred_element_type=F32)
        mixed = both[0:length] + both[length:] + jnp.dot(top, factor_lo[...], preferred_element_type=F32)
        mix_ref[pl.ds(own_block(c), length), :] = mixed.astype(BF16)
        for step in first_steps(c):
            last_copy(c, step).start()

    def after_last(c):
        for step in first_steps(c):
            last_copy(c, step).wait_recv()

    def greet_neighbours():
        for copy in count_copies + pan_halos:
            copy.start()

    def pass_on():
        for copy in pan_halos:
            copy.wait_recv()
        for copy in passed:
            copy.start()

    def start_halos(*which):
        for piece in which:
            for copy in [vec_halos[i] for i in HALO_ORDER[2 * piece:2 * piece + 2]]:
                copy.start()

    for pair in ([(1, 2), (0, 3)] if chunks == 4 else [range(chunks)]):
        columns = jnp.concatenate([vec[:, span_of(c)] for c in pair], axis=1)
        inner = jnp.dot(pan_t[...], columns, preferred_element_type=F32).T.astype(BF16)
        for at, c in enumerate(pair):
            part[c] = inner[at * wide_c:(at + 1) * wide_c]
            for step in first_steps(c):
                first_copy(c, step).start()

    lanes = [slice(c * 128, (c + 1) * 128) for c in range(ext.shape[0])]
    chunk_rows = rows // 8

    def widen(t, carry):
        at = pl.multiple_of(t * chunk_rows, 16)
        block = vec[pl.ds(at, chunk_rows), :].astype(F32)
        for c, span in enumerate(lanes):
            ext[c, pl.ds(HALO + at, chunk_rows), :] = block[:, span]
        return carry

    lax.fori_loop(0, 8, widen, 0)

    for which in (0, 1):
        pext[which, HALO:HALO + rows, :] = pan_ref[which, body, :].astype(F32)
    here = basis_ref[...].astype(F32)
    lower = jnp.where(iota(atoms, atoms, 0) < iota(atoms, atoms, 1), 1.0, 0.0).astype(BF16)
    at = iota(1, atoms, 1)

    def tables(prev, post, which):
        table = jnp.concatenate([prev, here, post, jnp.zeros((5, atoms), F32)], axis=0).astype(BF16)
        first = jnp.dot(table, lower, preferred_element_type=F32).astype(jnp.int32)
        first_ref[which] = jnp.clip(first + (HALO - rows) + rows * iota(8, atoms, 0), 0, rows + 2 * HALO)
        copy = pltpu.make_async_copy(first_ref.at[which], starts.at[which], start_sem.at[which])
        copy.start()
        lines = []
        for k in range(K):
            d = k - RIM
            near = here
            if d != 0:
                turn = (-d) % atoms
                inside = (at + d >= 0) & (at + d < atoms)
                near = jnp.where(inside, pltpu.roll(here, turn, 1), pltpu.roll(prev if d < 0 else post, turn, 1))
            lines.append(jnp.where(present_ref[k:k + 1, :] > 0, near, 0.0))
        lines.append(proj_ref[...].astype(F32))
        lines.append(jnp.zeros((atoms - K - 1, atoms), F32))
        limit[...] = jnp.concatenate(lines, axis=0).T
        return copy

    none = jnp.zeros((1, atoms), F32)
    begin_copy = tables(none, none, 0)
    blocks.wait()

    in_i = group_of(SUB, wide, 1, BMAX, NPMAX)
    slot = (iota(SUB, wide, 1) - BMAX * in_i).astype(F32)
    in_i = in_i.astype(F32)
    lane = iota(8, 128, 1)

    def band_piece(u, i):
        tiles = []
        for tile in range(WIN // 128):
            acc = None
            for b in range(REACH):
                to, last = max(b * BMAX, tile * 128), min((b + 1) * BMAX, (tile + 1) * 128)
                while to < last:
                    source = i * BMAX + to - b * BMAX
                    count = min(last - to, 128 - source % 128)
                    piece = skew[u, source // 128, pl.ds((REACH - 1 - b) * SUB, SUB, stride=SUB + 1), :]
                    turn = (to - source) % 128
                    piece = piece if turn == 0 else pltpu.roll(piece, turn, 1)
                    acc = piece if acc is None else jnp.where(lane >= to % 128, piece, acc)
                    to += count
            tiles.append(acc)
        return jnp.concatenate(tiles, axis=1)

    def band_step(t, carry):
        chunk = pl.ds(pl.multiple_of(t * GROUP, GROUP), GROUP)
        bounds = limit[chunk, :]
        for u in range(GROUP // SUB):
            within = bounds[u * SUB:(u + 1) * SUB]
            valid = in_i < within[:, K:K + 1]
            for k in range(K):
                block = cm_ref[k, chunk, :].astype(F32)[u * SUB:(u + 1) * SUB]
                block = jnp.where(valid & (slot < within[:, k:k + 1]), block, 0.0)
                top = (REACH - 1 - k) * SUB
                for tile in range(wide // 128):
                    skew[u, tile, top:top + SUB, :] = block[:, tile * 128:(tile + 1) * 128]
        for u in range(GROUP // SUB):
            for i in range(0, NPMAX, 2):
                both = jnp.concatenate([band_piece(u, i), band_piece(u, i + 1)], axis=0)
                band[t * (GROUP // SUB) + u, i * SUB:(i + 2) * SUB, :] = both.astype(BF16)
        return carry

    def gather(t, carry, which=0):
        at = pl.multiple_of(2 * t * BMAX, 16)
        begins = []
        for e in (0, 1):
            flat = 2 * t + e + atoms - RIM
            begins.append(starts[which, lax.div(flat, atoms), lax.rem(flat, atoms)])
        for c, span in enumerate(lanes):
            both = [ext[c, pl.ds(begin, BMAX), :] for begin in begins]
            padded[pl.ds(at, 2 * BMAX), span] = jnp.concatenate(both, axis=0).astype(BF16)
        for c in (0, 1):
            both = [pext[c, pl.ds(begin, BMAX), :] for begin in begins]
            ppadded[pl.ds(at, 2 * BMAX), c * half:(c + 1) * half] = jnp.concatenate(both, axis=0).astype(BF16)
        return carry

    def project(s, carry=0):
        at = pl.ds(pl.multiple_of(s * SUB * BMAX, 16), WIN)
        base[s] = jnp.dot(band[s], padded[at, :], preferred_element_type=F32)
        lean[s] = jnp.dot(band[s], ppadded[at, :], preferred_element_type=F32).astype(BF16)
        return carry

    def bands(low, high):
        lax.fori_loop(low, high, band_step, 0)

    def gathers(low, high):
        lax.fori_loop(low, high, gather, 0)

    def projects(*which):
        for s in which:
            project(s)

    begin_copy.wait()
    inside_from, inside_to = RIM // 2, (atoms + RIM) // 2
    inside_mid = (inside_from + inside_to) // 2
    late_copy = []

    def outer_bands():
        for copy in count_copies:
            copy.wait_recv()
        late_copy.append(tables(counts[0].astype(F32), counts[1].astype(F32), 1))
        lax.fori_loop(0, 2, lambda t, carry: band_step(t * (groups - 1), carry), 0)

    third = (groups - 2) // 3
    works = [functools.partial(bands, 1 + t * third, 1 + (t + 1) * third) for t in range(3)]
    works += [functools.partial(gathers, inside_from, inside_mid), functools.partial(gathers, inside_mid, inside_to)]
    subs = atoms // SUB
    works += [functools.partial(projects, s, s + 1) for s in range(2, subs - 2, 2)]
    works += [outer_bands, functools.partial(projects, 1, subs - 2)]
    if chunks == 4:
        order = [
            [],
            [(after_first, 1), (greet_neighbours,), (start_halos, 0)],
            [(after_first, 0)],
            [(after_fold, 1, 0), (after_first, 2), (after_first, 3), (start_halos, 1, 2)],
            [(after_fold, 0, 0), (start_halos, 3)],
            [],
            [(after_fold, 2, 0)],
            [(after_fold, 1, 1), (after_fold, 3, 0)],
            [],
            [(after_fold, 0, 1)],
            [(after_fold, 2, 1), (after_fold, 3, 1), (start_halos, 4, 5), (pass_on,)],
            [],
            [],
        ]
    else:
        every = range(chunks)
        order = [[], [(after_first, c) for c in every] + [(greet_neighbours,), (start_halos, *range(PIECES))]]
        order += [[(after_fold, c, turn) for c in every] for turn in range(len(rounds(0)))]
        order += [[] for _ in works[len(order):-1]] + [[(pass_on,)]]
    for work, events in zip(works, order, strict=True):
        work()
        for event in events:
            event[0](*event[1:])

    size = GROUP * NPMAX
    part_size = SUB * NPMAX
    row_at, lane_at = iota(size, size, 0), iota(size, size, 1)
    same = ((row_at >= part_size) == (lane_at >= part_size)) & ((row_at & (SUB - 1)) == (lane_at & (SUB - 1)))
    expand = jnp.where(group_of(size, size, 0, SUB, size // SUB) - jnp.where(row_at >= part_size, NPMAX, 0)
                       == (lane_at & (NPMAX - 1)), 1.0, 0.0).astype(BF16)
    owner = group_of(GROUP, size, 1, NPMAX, NPMAX)
    pair_of = range(GROUP // SUB)

    def tail(span, g):
        lines = jnp.concatenate([lean[g * len(pair_of) + u] for u in pair_of], axis=0)
        update = lax.dot_general(lines, mix_ref[span, :], across, preferred_element_type=F32)
        plain = jnp.concatenate([base[g * len(pair_of) + u, :, span] for u in pair_of], axis=0)
        rounded = (plain - update).astype(BF16)
        weighted = (rounded.astype(F32) * weight[:, span]).astype(BF16)
        return lax.dot_general(weighted, rounded, across, preferred_element_type=F32)

    def finish(product, g):
        kept = jnp.where(same, product, 0.0)
        top = kept.astype(BF16)
        rest = (kept - top.astype(F32)).astype(BF16)
        spread = jnp.dot(top, expand, preferred_element_type=F32) + jnp.dot(rest, expand, preferred_element_type=F32)
        result = jnp.zeros((GROUP, size), F32)
        for i in range(NPMAX):
            rows_of = [spread[u * part_size + i * SUB:u * part_size + (i + 1) * SUB, :] for u in pair_of]
            result = jnp.where(owner == i, jnp.concatenate(rows_of, axis=0), result)
        dens[pl.ds(pl.multiple_of(g * GROUP, GROUP), GROUP), :] = result

    cut = vec.shape[1] // 2
    first_half, second_half = slice(0, cut), slice(cut, 2 * cut)
    batch = max(d for d in (6, 3, 2, 1) if (groups - 2) % d == 0)

    def tail_first(t, carry):
        for e in range(batch):
            g = 1 + t * batch + e
            full[g] = tail(first_half, g)
        return carry

    def tail_second(t, carry):
        products = [full[1 + t * batch + e] + tail(second_half, 1 + t * batch + e) for e in range(batch)]
        for e, product in enumerate(products):
            finish(product, 1 + t * batch + e)
        return carry

    for c in range(0, max(1, chunks // 2)):
        after_last(c)
    lax.fori_loop(0, (groups - 2) // batch, tail_first, 0)
    for c in range(max(1, chunks // 2), chunks):
        after_last(c)
    lax.fori_loop(0, (groups - 2) // batch, tail_second, 0)
    share = own_ref.shape[0]
    inside = share - GROUP

    def den_copy(start, count, slot):
        src = pl.ds(pl.multiple_of(start, GROUP), count)
        dst = pl.ds(pl.multiple_of(start - other * share, GROUP), count)
        return remote(dens.at[src], got_ref.at[dst], den_sems, (slot,), (row, other))

    sent = [den_copy(other * share + GROUP * col, inside, 0), den_copy(other * (atoms - GROUP), GROUP, 1)]
    sent[0].start()

    for copy in pan_halos:
        copy.wait_send()
    for copy in passed + vec_halos:
        copy.wait()
    for side, at in ((0, 0), (1, HALO + rows)):
        block = halo_ref[side].astype(F32)
        for c, span in enumerate(lanes):
            ext[c, at:at + HALO, :] = block[:, span]
        for which in (0, 1):
            pext[which, at:at + HALO, :] = pan_ref[which, at:at + HALO, :].astype(F32)
    late_copy[0].wait()
    late_gather = functools.partial(gather, which=1)
    lax.fori_loop(0, RIM // 2, late_gather, 0)
    lax.fori_loop((atoms + RIM) // 2, (atoms + 2 * RIM) // 2, late_gather, 0)

    every = slice(0, 2 * cut)
    project(other * (subs - 1))
    theirs, ours = other * (groups - 1), col * (groups - 1)
    product = tail(every, theirs)
    project(col * (subs - 1))
    finish(product, theirs)
    sent[1].start()
    finish(tail(every, ours), ours)
    own_ref[...] = dens[pl.ds(pl.multiple_of(col * share, share), share), :]

    for copy in sent:
        copy.wait()
    swap.wait_send()
    for copy in count_copies:
        copy.wait_send()
    for c in range(chunks):
        for step in first_steps(c):
            first_copy(c, step).wait_send()
            last_copy(c, step).wait_send()
        for turn in rounds(c):
            fold_copy(c, turn).wait_send()


def vector_kernel(vin_ref, pan_ref, mix_ref, own_ref, got_ref, vec_hbm, den_ref, done, sems):
    tiles = sems.shape[0]
    tile = vin_ref.shape[0] // tiles
    den_ref[...] = own_ref[...] + got_ref[...]
    copies = []
    for t in range(tiles):
        at = slice(t * tile, (t + 1) * tile)
        inside = slice(HALO + t * tile, HALO + (t + 1) * tile)
        panel = jnp.concatenate([pan_ref[0, inside, :], pan_ref[1, inside, :]], axis=1)
        update = lax.dot_general(panel, mix_ref[...], (((1,), (1,)), ((), ())), preferred_element_type=F32)
        done[at, :] = (vin_ref[at, :].astype(F32) - update).astype(BF16)
        copies.append(pltpu.make_async_copy(done.at[at], vec_hbm.at[at], sems.at[t]))
        copies[-1].start()
    for copy in copies:
        copy.wait()


def local(vectors_in, panel, factor, atom_basis, proj_count, coupling, block_present, occ_mask, occ_weight):
    n = lax.axis_size("row")
    rows, cols = vectors_in.shape
    half = panel.shape[1]
    npan = factor.shape[0]
    atoms = atom_basis.shape[1]
    groups = atoms // GROUP
    share = atoms // lax.axis_size("col")
    wide = coupling.shape[2]
    vmem = pl.BlockSpec(memory_space=pltpu.VMEM)
    hbm = pl.BlockSpec(memory_space=pl.ANY)
    plane = max(d for d in range(1, n + 1) if n % d == 0 and d * d <= n)
    most, least = max(plane, n // plane), min(plane, n // plane)
    chunks = max(1, cols // (n * 16))
    width = cols // chunks
    unit = width // n
    turns = most.bit_length() - 1
    ext_rows = rows + 2 * HALO
    subs = atoms // SUB
    pad_rows = (subs - 1) * SUB * BMAX + WIN
    dma = pltpu.SemaphoreType.DMA
    operands = (vectors_in, panel, jnp.swapaxes(coupling, 0, 1), factor, atom_basis, proj_count[None, :], block_present.T,
                occ_mask[None, :], occ_weight[None, :])
    operands = [pltpu.with_memory_space_constraint(x, pltpu.HBM) for x in operands]
    vin, pan, mix, own, got = pl.pallas_call(
        functools.partial(mix_kernel, n, plane),
        out_shape=(
            jax.ShapeDtypeStruct((rows, cols), BF16),
            jax.ShapeDtypeStruct((2, ext_rows, half), BF16),
            jax.ShapeDtypeStruct((cols, npan), BF16),
            jax.ShapeDtypeStruct((share, NPMAX * NPMAX), F32),
            jax.ShapeDtypeStruct((share, NPMAX * NPMAX), F32),
        ),
        in_specs=[hbm] * 9,
        out_specs=(vmem,) * 5,
        scratch_shapes=[
            *[pltpu.VMEM(x.shape, x.dtype) for x in operands[3:]],
            pltpu.VMEM((npan, rows), BF16),
            pltpu.VMEM((chunks, width, npan), BF16),
            pltpu.VMEM((chunks, most, width // least, npan), BF16),
            pltpu.VMEM((chunks, turns, width // least, npan), BF16),
            pltpu.VMEM((chunks, turns, width // least, npan), BF16),
            pltpu.VMEM((npan, npan), BF16),
            pltpu.VMEM((npan, npan), BF16),
            pltpu.VMEM((2, 1, atoms), jnp.int32),
            pltpu.VMEM((atoms, atoms), F32),
            pltpu.VMEM((K, atoms, wide), BF16),
            pltpu.VMEM((2, HALO, cols), BF16),
            pltpu.VMEM((GROUP // SUB, wide // 128, (2 * SUB + K - 2) * SUB, 128), F32),
            pltpu.VMEM((subs, SUB * NPMAX, WIN), BF16),
            pltpu.VMEM((2, 8, atoms), jnp.int32),
            pltpu.SMEM((2, 8, atoms), jnp.int32),
            pltpu.VMEM((cols // 128, ext_rows + BMAX, 128), F32),
            pltpu.VMEM((2, ext_rows + BMAX, half), F32),
            pltpu.VMEM((pad_rows, cols), BF16),
            pltpu.VMEM((pad_rows, npan), BF16),
            pltpu.VMEM((subs, SUB * NPMAX, cols), F32),
            pltpu.VMEM((subs, SUB * NPMAX, npan), BF16),
            pltpu.VMEM((groups, GROUP * NPMAX, GROUP * NPMAX), F32),
            pltpu.VMEM((atoms, NPMAX * NPMAX), F32),
            pltpu.VMEM((1, cols), F32),
            dma((2,)), dma((6,)), dma, dma, dma((2,)), dma((2, 5)), dma((2, 2, PIECES)), dma((2, 2)),
            dma((2, chunks, 2, most)), dma((2, chunks, turns)), dma((2, 2)),
        ],
        compiler_params=pltpu.CompilerParams(collective_id=0, has_side_effects=True, vmem_limit_bytes=48 << 20),
        cost_estimate=pl.CostEstimate(flops=8 * 10**9, bytes_accessed=10 << 20, transcendentals=0),
    )(*operands)

    return pl.pallas_call(
        vector_kernel,
        out_shape=(
            jax.ShapeDtypeStruct((rows, cols), BF16),
            jax.ShapeDtypeStruct((share, NPMAX * NPMAX), F32),
        ),
        in_specs=[vmem] * 5,
        out_specs=[hbm, vmem],
        scratch_shapes=[pltpu.VMEM((rows, cols), BF16), dma((8,))],
        compiler_params=pltpu.CompilerParams(vmem_limit_bytes=16 << 20),
        cost_estimate=pl.CostEstimate(flops=6 * 10**9, bytes_accessed=10 << 20, transcendentals=0),
    )(vin, pan, mix, own, got)


def solution(mesh):
    placed = (
        P("row", "col"),
        P("row", "col"),
        P(),
        P("row", None),
        P("row"),
        P("row", None, None),
        P("row", None),
        P("col"),
        P("col"),
    )
    return jax.shard_map(
        local,
        mesh=mesh,
        in_specs=placed,
        out_specs=(P("row", "col"), P(("row", "col"), None)),
        check_vma=False,
    )
```

```python
import functools

import jax
import jax.numpy as jnp
from jax import lax
from jax.experimental import pallas as pl
from jax.experimental.pallas import tpu as pltpu
from jax.sharding import PartitionSpec as P

NPMAX = 16
BMAX = 24
K = 9
RIM = (K - 1) // 2
HALO = RIM * BMAX
PIECES = 6
HALO_ORDER = (0, 6, 1, 7, 2, 8, 3, 9, 4, 5, 10, 11)
GROUP = 16
SUB = 8
WIN = -(-(SUB + K - 1) * BMAX // 128) * 128
REACH = SUB + K - 1
F32 = jnp.float32
BF16 = jnp.bfloat16
MESH = pl.DeviceIdType.MESH


def iota(rows, columns, axis):
    return lax.broadcasted_iota(jnp.int32, (rows, columns), axis)


def group_of(rows, columns, axis, size, most):
    small = (8, columns) if axis == 1 else (rows, 128)
    index = iota(*small, axis)
    group = jnp.zeros(small, jnp.int32)
    for edge in range(1, most):
        group = group + jnp.where(index >= edge * size, 1, 0)
    return jnp.tile(group, (rows // small[0], columns // small[1]))


def mix_kernel(n, plane, vec_hbm, panel_hbm, coupling_hbm, factor_hbm, basis_hbm, proj_hbm, present_hbm, mask_hbm, occ_hbm,
               vec, pan_ref, mix_ref, own_ref, got_ref,
               factor_ref, basis_ref, proj_ref, present_ref, mask_ref, occ_ref,
               pan_t, part, got_first, middle, got_second, factor_hi, factor_lo, counts, limit, cm_ref, halo_ref, skew, band,
               first_ref, starts, ext, pext, padded, ppadded, base, lean, full, dens, weight,
               load_sem, small_sem, own_sem, cm_sem, start_sem, pan_sems, halo_sems, count_sems, ring_sems, fold_sems, den_sems):
    row, col = lax.axis_index("row"), lax.axis_index("col")
    other = 1 - col
    up, down = lax.rem(row + 1, n), lax.rem(row + n - 1, n)
    rows, half = panel_hbm.shape
    chunks, wide_c, npan = part.shape
    unit = wide_c // n
    atoms, wide = cm_ref.shape[1:]
    groups = atoms // GROUP
    body = pl.ds(HALO, rows)
    q, p = n // plane, plane
    line, spot = lax.div(row, p), lax.rem(row, p)
    contract = (((0,), (0,)), ((), ()))
    across = (((1,), (1,)), ((), ()))

    def plane_peer(step):
        return line * p + lax.rem(spot + step, p)

    def line_peer(step):
        return lax.rem(line + step, q) * p + spot

    by_plane, by_line = (p, spot, plane_peer), (q, line, line_peer)
    ways = [(by_line, by_plane) if chunks == 4 and c == 2 else (by_plane, by_line) for c in range(chunks)]

    own = pltpu.make_async_copy(panel_hbm, pan_ref.at[col, body], own_sem)
    own.start()
    pieces = rows // load_sem.shape[0]
    loads = [pltpu.make_async_copy(vec_hbm.at[pl.ds(i * pieces, pieces)], vec.at[pl.ds(i * pieces, pieces)], load_sem.at[i])
             for i in range(load_sem.shape[0])]
    for load in loads:
        load.start()
    small = [pltpu.make_async_copy(src, dst, small_sem.at[i]) for i, (src, dst) in enumerate((
        (basis_hbm, basis_ref), (factor_hbm, factor_ref), (proj_hbm, proj_ref), (present_hbm, present_ref),
        (mask_hbm, mask_ref), (occ_hbm, occ_ref)))]
    for load in small:
        load.start()
    blocks = pltpu.make_async_copy(coupling_hbm, cm_ref, cm_sem)

    barrier = pltpu.get_barrier_semaphore()
    greeted = [(plane_peer(step), col) for step in range(1, p)] + [(line_peer(step), col) for step in range(1, q)]
    greeted += [(row, other)]
    for target in greeted:
        pl.semaphore_signal(barrier, inc=1, device_id=target, device_id_type=MESH)
    length = ext.shape[1]
    edge = rows + HALO
    ext[:, edge:, :] = jnp.zeros((ext.shape[0], length - edge, 128), F32)
    pext[:, edge:, :] = jnp.zeros((2, length - edge, half), F32)
    low = (SUB - 1) * SUB
    skew[:, :, 0:low, :] = jnp.zeros((*skew.shape[:2], low, 128), F32)
    skew[:, :, low + K * SUB:, :] = jnp.zeros((*skew.shape[:2], low, 128), F32)
    pl.semaphore_wait(barrier, len(greeted))

    def remote(src, dst, sems, slot, target):
        return pltpu.make_async_remote_copy(
            src_ref=src, dst_ref=dst, send_sem=sems.at[(0,) + slot], recv_sem=sems.at[(1,) + slot],
            device_id=target, device_id_type=MESH)

    swap = remote(panel_hbm, pan_ref.at[col, body], pan_sems, (0,), (row, other))
    swap.start()
    count_copies = [
        remote(basis_hbm, counts.at[side], count_sems, (side,), (target, col))
        for side, target in ((0, up), (1, down))
    ]
    pan_halos, passed, vec_halos = [], [], []
    for side, target in ((0, up), (1, down)):
        src_at = rows - HALO if side == 0 else 0
        dst_at = 0 if side == 0 else HALO + rows
        pan_halos.append(remote(panel_hbm.at[pl.ds(src_at, HALO)], pan_ref.at[col, pl.ds(dst_at, HALO)],
                                pan_sems, (1 + side,), (target, col)))
        ghost = pan_ref.at[col, pl.ds(dst_at, HALO)]
        passed.append(remote(ghost, ghost, pan_sems, (3 + side,), (row, other)))
    far = jnp.where(row == n - 1, 0, 1)
    for side in (far, 1 - far):
        target = jnp.where(side == 0, up, down)
        src_at = (rows - HALO) * (1 - side)
        for piece in range(PIECES):
            part_at = piece * (HALO // PIECES)
            src = pl.ds(pl.multiple_of(src_at + part_at, HALO // PIECES), HALO // PIECES)
            vec_halos.append(remote(vec_hbm.at[src], halo_ref.at[side, pl.ds(part_at, HALO // PIECES)],
                                    halo_sems, (side, piece), (target, col)))

    own.wait()
    pan_t[pl.ds(pl.multiple_of(col * half, half), half), :] = pan_ref[col, body, :].T
    for load in small:
        load.wait()
    high = factor_ref[...].astype(BF16)
    factor_hi[...] = high
    factor_lo[...] = (factor_ref[...] - high.astype(F32)).astype(BF16)
    weight[...] = mask_ref[...].astype(F32) * occ_ref[...] / (vec_hbm.shape[1] * lax.axis_size("col"))
    for load in loads:
        load.wait()
    blocks.start()

    def span_of(c):
        return slice(c * wide_c, (c + 1) * wide_c)

    pairs = [(1, 2), (0, 3)] if chunks == 4 else [range(chunks)]

    def products(pair, which):
        mine = pl.ds(pl.multiple_of(which * half, half), half)
        columns = jnp.concatenate([vec[:, span_of(c)] for c in pair], axis=1)
        inner = jnp.dot(pan_t[mine, :], columns, preferred_element_type=F32).T.astype(BF16)
        for at, c in enumerate(pair):
            part[c, :, mine] = inner[at * wide_c:(at + 1) * wide_c]

    for pair in pairs:
        products(pair, col)
    swap.wait_recv()
    pan_t[pl.ds(pl.multiple_of(other * half, half), half), :] = pan_ref[other, body, :].T

    def first_copy(c, step):
        (size, at, peer), (size_s, _, _) = ways[c]
        length = size_s * unit
        src = pl.ds(pl.multiple_of(lax.rem(at + step, size) * length, unit), length)
        return remote(part.at[c, src], got_first.at[c, step, pl.ds(0, length)], ring_sems, (c, 0, step), (peer(step), col))

    def rounds(c):
        return range(ways[c][1][0].bit_length() - 1)

    def fold_copy(c, turn):
        _, (size, at, peer) = ways[c]
        reach = 1 << turn
        ahead = lax.rem(lax.div(at, reach), 2)
        step = reach + ahead * (size - 2 * reach)
        length = size * unit
        return remote(middle.at[c, turn, pl.ds(0, length)], got_second.at[c, turn, pl.ds(0, length)],
                      fold_sems, (c, turn), (peer(step), col))

    def own_block(c):
        (_, at, _), (size_s, _, _) = ways[c]
        return pl.multiple_of(c * wide_c + at * size_s * unit, unit)

    def last_copy(c, step):
        (_, _, peer), (size_s, _, _) = ways[c]
        mine = pl.ds(own_block(c), size_s * unit)
        return remote(mix_ref.at[mine], mix_ref.at[mine], ring_sems, (c, 1, step), (peer(step), col))

    def first_steps(c):
        return range(1, ways[c][0][0])

    def after_first(c):
        (_, at, _), (size_s, _, _) = ways[c]
        length = size_s * unit
        for step in first_steps(c):
            first_copy(c, step).wait_recv()
        total = part[c, pl.ds(pl.multiple_of(at * length, unit), length), :].astype(F32)
        for step in first_steps(c):
            total = total + got_first[c, step, 0:length, :].astype(F32)
        middle[c, 0, 0:length, :] = total.astype(BF16)
        fold_copy(c, 0).start()

    def after_fold(c, turn):
        length = ways[c][1][0] * unit
        fold_copy(c, turn).wait_recv()
        inner = middle[c, turn, 0:length, :].astype(F32) + got_second[c, turn, 0:length, :].astype(F32)
        top = inner.astype(BF16)
        if turn + 1 < len(rounds(c)):
            middle[c, turn + 1, 0:length, :] = top
            fold_copy(c, turn + 1).start()
            return
        rest = (inner - top.astype(F32)).astype(BF16)
        both = jnp.dot(jnp.concatenate([top, rest], axis=0), factor_hi[...], preferred_element_type=F32)
        mixed = both[0:length] + both[length:] + jnp.dot(top, factor_lo[...], preferred_element_type=F32)
        mix_ref[pl.ds(own_block(c), length), :] = mixed.astype(BF16)
        for step in first_steps(c):
            last_copy(c, step).start()

    def after_last(c):
        for step in first_steps(c):
            last_copy(c, step).wait_recv()

    def greet_neighbours():
        for copy in count_copies + pan_halos:
            copy.start()

    def pass_on():
        for copy in pan_halos:
            copy.wait_recv()
        for copy in passed:
            copy.start()

    def start_halos(*which):
        for piece in which:
            for copy in [vec_halos[i] for i in HALO_ORDER[2 * piece:2 * piece + 2]]:
                copy.start()

    for pair in pairs:
        products(pair, other)
        for c in pair:
            for step in first_steps(c):
                first_copy(c, step).start()

    lanes = [slice(c * 128, (c + 1) * 128) for c in range(ext.shape[0])]
    chunk_rows = rows // 8

    def widen(t, carry):
        at = pl.multiple_of(t * chunk_rows, 16)
        block = vec[pl.ds(at, chunk_rows), :].astype(F32)
        for c, span in enumerate(lanes):
            ext[c, pl.ds(HALO + at, chunk_rows), :] = block[:, span]
        return carry

    lax.fori_loop(0, 8, widen, 0)

    for which in (0, 1):
        pext[which, HALO:HALO + rows, :] = pan_ref[which, body, :].astype(F32)
    here = basis_ref[...].astype(F32)
    lower = jnp.where(iota(atoms, atoms, 0) < iota(atoms, atoms, 1), 1.0, 0.0).astype(BF16)
    at = iota(1, atoms, 1)

    def tables(prev, post, which):
        table = jnp.concatenate([prev, here, post, jnp.zeros((5, atoms), F32)], axis=0).astype(BF16)
        first = jnp.dot(table, lower, preferred_element_type=F32).astype(jnp.int32)
        first_ref[which] = jnp.clip(first + (HALO - rows) + rows * iota(8, atoms, 0), 0, rows + 2 * HALO)
        copy = pltpu.make_async_copy(first_ref.at[which], starts.at[which], start_sem.at[which])
        copy.start()
        lines = []
        for k in range(K):
            d = k - RIM
            near = here
            if d != 0:
                turn = (-d) % atoms
                inside = (at + d >= 0) & (at + d < atoms)
                near = jnp.where(inside, pltpu.roll(here, turn, 1), pltpu.roll(prev if d < 0 else post, turn, 1))
            lines.append(jnp.where(present_ref[k:k + 1, :] > 0, near, 0.0))
        lines.append(proj_ref[...].astype(F32))
        lines.append(jnp.zeros((atoms - K - 1, atoms), F32))
        limit[...] = jnp.concatenate(lines, axis=0).T
        return copy

    none = jnp.zeros((1, atoms), F32)
    begin_copy = tables(none, none, 0)
    blocks.wait()

    in_i = group_of(SUB, wide, 1, BMAX, NPMAX)
    slot = (iota(SUB, wide, 1) - BMAX * in_i).astype(F32)
    in_i = in_i.astype(F32)
    lane = iota(8, 128, 1)

    def band_piece(u, i):
        tiles = []
        for tile in range(WIN // 128):
            acc = None
            for b in range(REACH):
                to, last = max(b * BMAX, tile * 128), min((b + 1) * BMAX, (tile + 1) * 128)
                while to < last:
                    source = i * BMAX + to - b * BMAX
                    count = min(last - to, 128 - source % 128)
                    piece = skew[u, source // 128, pl.ds((REACH - 1 - b) * SUB, SUB, stride=SUB + 1), :]
                    turn = (to - source) % 128
                    piece = piece if turn == 0 else pltpu.roll(piece, turn, 1)
                    acc = piece if acc is None else jnp.where(lane >= to % 128, piece, acc)
                    to += count
            tiles.append(acc)
        return jnp.concatenate(tiles, axis=1)

    def band_step(t, carry):
        chunk = pl.ds(pl.multiple_of(t * GROUP, GROUP), GROUP)
        bounds = limit[chunk, :]
        for u in range(GROUP // SUB):
            within = bounds[u * SUB:(u + 1) * SUB]
            valid = in_i < within[:, K:K + 1]
            for k in range(K):
                block = cm_ref[k, chunk, :].astype(F32)[u * SUB:(u + 1) * SUB]
                block = jnp.where(valid & (slot < within[:, k:k + 1]), block, 0.0)
                top = (REACH - 1 - k) * SUB
                for tile in range(wide // 128):
                    skew[u, tile, top:top + SUB, :] = block[:, tile * 128:(tile + 1) * 128]
        for u in range(GROUP // SUB):
            for i in range(0, NPMAX, 2):
                both = jnp.concatenate([band_piece(u, i), band_piece(u, i + 1)], axis=0)
                band[t * (GROUP // SUB) + u, i * SUB:(i + 2) * SUB, :] = both.astype(BF16)
        return carry

    def gather(t, carry, which=0):
        at = pl.multiple_of(2 * t * BMAX, 16)
        begins = []
        for e in (0, 1):
            flat = 2 * t + e + atoms - RIM
            begins.append(starts[which, lax.div(flat, atoms), lax.rem(flat, atoms)])
        for c, span in enumerate(lanes):
            both = [ext[c, pl.ds(begin, BMAX), :] for begin in begins]
            padded[pl.ds(at, 2 * BMAX), span] = jnp.concatenate(both, axis=0).astype(BF16)
        for c in (0, 1):
            both = [pext[c, pl.ds(begin, BMAX), :] for begin in begins]
            ppadded[pl.ds(at, 2 * BMAX), c * half:(c + 1) * half] = jnp.concatenate(both, axis=0).astype(BF16)
        return carry

    def project(s, carry=0):
        at = pl.ds(pl.multiple_of(s * SUB * BMAX, 16), WIN)
        base[s] = jnp.dot(band[s], padded[at, :], preferred_element_type=F32)
        lean[s] = jnp.dot(band[s], ppadded[at, :], preferred_element_type=F32).astype(BF16)
        return carry

    def bands(low, high):
        lax.fori_loop(low, high, band_step, 0)

    def gathers(low, high):
        lax.fori_loop(low, high, gather, 0)

    def projects(*which):
        for s in which:
            project(s)

    begin_copy.wait()
    inside_from, inside_to = RIM // 2, (atoms + RIM) // 2
    inside_mid = (inside_from + inside_to) // 2
    late_copy = []

    def outer_bands():
        for copy in count_copies:
            copy.wait_recv()
        late_copy.append(tables(counts[0].astype(F32), counts[1].astype(F32), 1))
        lax.fori_loop(0, 2, lambda t, carry: band_step(t * (groups - 1), carry), 0)

    third = (groups - 2) // 3
    works = [functools.partial(bands, 1 + t * third, 1 + (t + 1) * third) for t in range(3)]
    works += [functools.partial(gathers, inside_from, inside_mid), functools.partial(gathers, inside_mid, inside_to)]
    subs = atoms // SUB
    works += [functools.partial(projects, s, s + 1) for s in range(2, subs - 2, 2)]
    works += [outer_bands, functools.partial(projects, 1, subs - 2)]
    if chunks == 4:
        order = [
            [],
            [(after_first, 1), (greet_neighbours,), (start_halos, 0)],
            [(after_first, 0)],
            [(after_fold, 1, 0), (after_first, 2), (after_first, 3), (start_halos, 1, 2)],
            [(after_fold, 0, 0)],
            [],
            [(after_fold, 2, 0), (start_halos, 3)],
            [(after_fold, 1, 1), (after_fold, 3, 0)],
            [],
            [(after_fold, 0, 1)],
            [(after_fold, 2, 1), (after_fold, 3, 1), (start_halos, 4, 5), (pass_on,)],
            [],
            [],
        ]
    else:
        every = range(chunks)
        order = [[], [(after_first, c) for c in every] + [(greet_neighbours,), (start_halos, *range(PIECES))]]
        order += [[(after_fold, c, turn) for c in every] for turn in range(len(rounds(0)))]
        order += [[] for _ in works[len(order):-1]] + [[(pass_on,)]]
    for work, events in zip(works, order, strict=True):
        work()
        for event in events:
            event[0](*event[1:])

    size = GROUP * NPMAX
    part_size = SUB * NPMAX
    row_at, lane_at = iota(size, size, 0), iota(size, size, 1)
    same = ((row_at >= part_size) == (lane_at >= part_size)) & ((row_at & (SUB - 1)) == (lane_at & (SUB - 1)))
    expand = jnp.where(group_of(size, size, 0, SUB, size // SUB) - jnp.where(row_at >= part_size, NPMAX, 0)
                       == (lane_at & (NPMAX - 1)), 1.0, 0.0).astype(BF16)
    owner = group_of(GROUP, size, 1, NPMAX, NPMAX)
    pair_of = range(GROUP // SUB)

    def tail(span, g):
        lines = jnp.concatenate([lean[g * len(pair_of) + u] for u in pair_of], axis=0)
        update = lax.dot_general(lines, mix_ref[span, :], across, preferred_element_type=F32)
        plain = jnp.concatenate([base[g * len(pair_of) + u, :, span] for u in pair_of], axis=0)
        rounded = (plain - update).astype(BF16)
        weighted = (rounded.astype(F32) * weight[:, span]).astype(BF16)
        return lax.dot_general(weighted, rounded, across, preferred_element_type=F32)

    def finish(product, g):
        kept = jnp.where(same, product, 0.0)
        top = kept.astype(BF16)
        rest = (kept - top.astype(F32)).astype(BF16)
        spread = jnp.dot(top, expand, preferred_element_type=F32) + jnp.dot(rest, expand, preferred_element_type=F32)
        result = jnp.zeros((GROUP, size), F32)
        for i in range(NPMAX):
            rows_of = [spread[u * part_size + i * SUB:u * part_size + (i + 1) * SUB, :] for u in pair_of]
            result = jnp.where(owner == i, jnp.concatenate(rows_of, axis=0), result)
        dens[pl.ds(pl.multiple_of(g * GROUP, GROUP), GROUP), :] = result

    cut = vec.shape[1] // 2
    first_half, second_half = slice(0, cut), slice(cut, 2 * cut)
    batch = max(d for d in (6, 3, 2, 1) if (groups - 2) % d == 0)

    def tail_first(span, t, carry, fresh=True):
        for e in range(batch):
            g = 1 + t * batch + e
            product = tail(span, g)
            full[g] = product if fresh else full[g] + product
        return carry

    def tail_second(t, carry):
        products = [full[1 + t * batch + e] + tail(second_half, 1 + t * batch + e) for e in range(batch)]
        for e, product in enumerate(products):
            finish(product, 1 + t * batch + e)
        return carry

    for c in (1, 0) if chunks == 4 else (0,):
        after_last(c)
        span = span_of(c) if chunks == 4 else first_half
        lax.fori_loop(0, (groups - 2) // batch, functools.partial(tail_first, span, fresh=c == 1 or chunks != 4), 0)
    for c in range(max(1, chunks // 2), chunks):
        after_last(c)
    lax.fori_loop(0, (groups - 2) // batch, tail_second, 0)
    share = own_ref.shape[0]
    inside = share - GROUP

    def den_copy(start, count, slot):
        src = pl.ds(pl.multiple_of(start, GROUP), count)
        dst = pl.ds(pl.multiple_of(start - other * share, GROUP), count)
        return remote(dens.at[src], got_ref.at[dst], den_sems, (slot,), (row, other))

    sent = [den_copy(other * share + GROUP * col, inside, 0), den_copy(other * (atoms - GROUP), GROUP, 1)]
    sent[0].start()

    for copy in pan_halos:
        copy.wait_send()
    for copy in passed + vec_halos:
        copy.wait()
    for side, at in ((0, 0), (1, HALO + rows)):
        block = halo_ref[side].astype(F32)
        for c, span in enumerate(lanes):
            ext[c, at:at + HALO, :] = block[:, span]
        for which in (0, 1):
            pext[which, at:at + HALO, :] = pan_ref[which, at:at + HALO, :].astype(F32)
    late_copy[0].wait()
    late_gather = functools.partial(gather, which=1)
    lax.fori_loop(0, RIM // 2, late_gather, 0)
    lax.fori_loop((atoms + RIM) // 2, (atoms + 2 * RIM) // 2, late_gather, 0)

    every = slice(0, 2 * cut)
    project(other * (subs - 1))
    theirs, ours = other * (groups - 1), col * (groups - 1)
    product = tail(every, theirs)
    project(col * (subs - 1))
    finish(product, theirs)
    sent[1].start()
    finish(tail(every, ours), ours)
    own_ref[...] = dens[pl.ds(pl.multiple_of(col * share, share), share), :]

    for copy in sent:
        copy.wait()
    swap.wait_send()
    for copy in count_copies:
        copy.wait_send()
    for c in range(chunks):
        for step in first_steps(c):
            first_copy(c, step).wait_send()
            last_copy(c, step).wait_send()
        for turn in rounds(c):
            fold_copy(c, turn).wait_send()


def vector_kernel(vin_ref, pan_ref, mix_ref, own_ref, got_ref, vec_hbm, den_ref, done, sems):
    tiles = sems.shape[0]
    tile = vin_ref.shape[0] // tiles
    den_ref[...] = own_ref[...] + got_ref[...]
    copies = []
    for t in range(tiles):
        at = slice(t * tile, (t + 1) * tile)
        inside = slice(HALO + t * tile, HALO + (t + 1) * tile)
        panel = jnp.concatenate([pan_ref[0, inside, :], pan_ref[1, inside, :]], axis=1)
        update = lax.dot_general(panel, mix_ref[...], (((1,), (1,)), ((), ())), preferred_element_type=F32)
        done[at, :] = (vin_ref[at, :].astype(F32) - update).astype(BF16)
        copies.append(pltpu.make_async_copy(done.at[at], vec_hbm.at[at], sems.at[t]))
        copies[-1].start()
    for copy in copies:
        copy.wait()


def local(vectors_in, panel, factor, atom_basis, proj_count, coupling, block_present, occ_mask, occ_weight):
    n = lax.axis_size("row")
    rows, cols = vectors_in.shape
    half = panel.shape[1]
    npan = factor.shape[0]
    atoms = atom_basis.shape[1]
    groups = atoms // GROUP
    share = atoms // lax.axis_size("col")
    wide = coupling.shape[2]
    vmem = pl.BlockSpec(memory_space=pltpu.VMEM)
    hbm = pl.BlockSpec(memory_space=pl.ANY)
    plane = max(d for d in range(1, n + 1) if n % d == 0 and d * d <= n)
    most, least = max(plane, n // plane), min(plane, n // plane)
    chunks = max(1, cols // (n * 16))
    width = cols // chunks
    unit = width // n
    turns = most.bit_length() - 1
    ext_rows = rows + 2 * HALO
    subs = atoms // SUB
    pad_rows = (subs - 1) * SUB * BMAX + WIN
    dma = pltpu.SemaphoreType.DMA
    operands = (vectors_in, panel, jnp.swapaxes(coupling, 0, 1), factor, atom_basis, proj_count[None, :], block_present.T,
                occ_mask[None, :], occ_weight[None, :])
    operands = [pltpu.with_memory_space_constraint(x, pltpu.HBM) for x in operands]
    vin, pan, mix, own, got = pl.pallas_call(
        functools.partial(mix_kernel, n, plane),
        out_shape=(
            jax.ShapeDtypeStruct((rows, cols), BF16),
            jax.ShapeDtypeStruct((2, ext_rows, half), BF16),
            jax.ShapeDtypeStruct((cols, npan), BF16),
            jax.ShapeDtypeStruct((share, NPMAX * NPMAX), F32),
            jax.ShapeDtypeStruct((share, NPMAX * NPMAX), F32),
        ),
        in_specs=[hbm] * 9,
        out_specs=(vmem,) * 5,
        scratch_shapes=[
            *[pltpu.VMEM(x.shape, x.dtype) for x in operands[3:]],
            pltpu.VMEM((npan, rows), BF16),
            pltpu.VMEM((chunks, width, npan), BF16),
            pltpu.VMEM((chunks, most, width // least, npan), BF16),
            pltpu.VMEM((chunks, turns, width // least, npan), BF16),
            pltpu.VMEM((chunks, turns, width // least, npan), BF16),
            pltpu.VMEM((npan, npan), BF16),
            pltpu.VMEM((npan, npan), BF16),
            pltpu.VMEM((2, 1, atoms), jnp.int32),
            pltpu.VMEM((atoms, atoms), F32),
            pltpu.VMEM((K, atoms, wide), BF16),
            pltpu.VMEM((2, HALO, cols), BF16),
            pltpu.VMEM((GROUP // SUB, wide // 128, (2 * SUB + K - 2) * SUB, 128), F32),
            pltpu.VMEM((subs, SUB * NPMAX, WIN), BF16),
            pltpu.VMEM((2, 8, atoms), jnp.int32),
            pltpu.SMEM((2, 8, atoms), jnp.int32),
            pltpu.VMEM((cols // 128, ext_rows + BMAX, 128), F32),
            pltpu.VMEM((2, ext_rows + BMAX, half), F32),
            pltpu.VMEM((pad_rows, cols), BF16),
            pltpu.VMEM((pad_rows, npan), BF16),
            pltpu.VMEM((subs, SUB * NPMAX, cols), F32),
            pltpu.VMEM((subs, SUB * NPMAX, npan), BF16),
            pltpu.VMEM((groups, GROUP * NPMAX, GROUP * NPMAX), F32),
            pltpu.VMEM((atoms, NPMAX * NPMAX), F32),
            pltpu.VMEM((1, cols), F32),
            dma((2,)), dma((6,)), dma, dma, dma((2,)), dma((2, 5)), dma((2, 2, PIECES)), dma((2, 2)),
            dma((2, chunks, 2, most)), dma((2, chunks, turns)), dma((2, 2)),
        ],
        compiler_params=pltpu.CompilerParams(collective_id=0, has_side_effects=True, vmem_limit_bytes=48 << 20),
        cost_estimate=pl.CostEstimate(flops=8 * 10**9, bytes_accessed=10 << 20, transcendentals=0),
    )(*operands)

    return pl.pallas_call(
        vector_kernel,
        out_shape=(
            jax.ShapeDtypeStruct((rows, cols), BF16),
            jax.ShapeDtypeStruct((share, NPMAX * NPMAX), F32),
        ),
        in_specs=[vmem] * 5,
        out_specs=[hbm, vmem],
        scratch_shapes=[pltpu.VMEM((rows, cols), BF16), dma((8,))],
        compiler_params=pltpu.CompilerParams(vmem_limit_bytes=16 << 20),
        cost_estimate=pl.CostEstimate(flops=6 * 10**9, bytes_accessed=10 << 20, transcendentals=0),
    )(vin, pan, mix, own, got)


def solution(mesh):
    placed = (
        P("row", "col"),
        P("row", "col"),
        P(),
        P("row", None),
        P("row"),
        P("row", None, None),
        P("row", None),
        P("col"),
        P("col"),
    )
    return jax.shard_map(
        local,
        mesh=mesh,
        in_specs=placed,
        out_specs=(P("row", "col"), P(("row", "col"), None)),
        check_vma=False,
    )
```

```python
import functools

import jax
import jax.numpy as jnp
from jax import lax
from jax.experimental import pallas as pl
from jax.experimental.pallas import tpu as pltpu
from jax.sharding import PartitionSpec as P

NPMAX = 16
BMAX = 24
K = 9
RIM = (K - 1) // 2
HALO = RIM * BMAX
PIECES = 6
HALO_ORDER = (0, 6, 1, 7, 2, 8, 3, 9, 4, 5, 10, 11)
GROUP = 16
SUB = 8
WIN = -(-(SUB + K - 1) * BMAX // 128) * 128
REACH = SUB + K - 1
F32 = jnp.float32
BF16 = jnp.bfloat16
MESH = pl.DeviceIdType.MESH


def iota(rows, columns, axis):
    return lax.broadcasted_iota(jnp.int32, (rows, columns), axis)


def group_of(rows, columns, axis, size, most):
    small = (8, columns) if axis == 1 else (rows, 128)
    index = iota(*small, axis)
    group = jnp.zeros(small, jnp.int32)
    for edge in range(1, most):
        group = group + jnp.where(index >= edge * size, 1, 0)
    return jnp.tile(group, (rows // small[0], columns // small[1]))


def mix_kernel(n, plane, vec_hbm, panel_hbm, coupling_hbm, factor_hbm, basis_hbm, proj_hbm, present_hbm, mask_hbm, occ_hbm,
               vec, pan_ref, mix_ref, own_ref, got_ref,
               factor_ref, basis_ref, proj_ref, present_ref, mask_ref, occ_ref,
               pan_t, part, got_first, middle, got_second, factor_hi, factor_lo, counts, limit, cm_ref, halo_ref, skew, band,
               first_ref, starts, ext, pext, padded, ppadded, base, lean, full, dens, weight,
               load_sem, small_sem, own_sem, cm_sem, start_sem, pan_sems, halo_sems, count_sems, ring_sems, fold_sems, den_sems):
    row, col = lax.axis_index("row"), lax.axis_index("col")
    other = 1 - col
    up, down = lax.rem(row + 1, n), lax.rem(row + n - 1, n)
    rows, half = panel_hbm.shape
    chunks, wide_c, npan = part.shape
    unit = wide_c // n
    atoms, wide = cm_ref.shape[1:]
    groups = atoms // GROUP
    body = pl.ds(HALO, rows)
    q, p = n // plane, plane
    line, spot = lax.div(row, p), lax.rem(row, p)
    contract = (((0,), (0,)), ((), ()))
    across = (((1,), (1,)), ((), ()))

    def plane_peer(step):
        return line * p + lax.rem(spot + step, p)

    def line_peer(step):
        return lax.rem(line + step, q) * p + spot

    by_plane, by_line = (p, spot, plane_peer), (q, line, line_peer)
    ways = [(by_line, by_plane) if chunks == 4 and c == 2 else (by_plane, by_line) for c in range(chunks)]

    own = pltpu.make_async_copy(panel_hbm, pan_ref.at[col, body], own_sem)
    own.start()
    pieces = rows // load_sem.shape[0]
    loads = [pltpu.make_async_copy(vec_hbm.at[pl.ds(i * pieces, pieces)], vec.at[pl.ds(i * pieces, pieces)], load_sem.at[i])
             for i in range(load_sem.shape[0])]
    for load in loads:
        load.start()
    small = [pltpu.make_async_copy(src, dst, small_sem.at[i]) for i, (src, dst) in enumerate((
        (basis_hbm, basis_ref), (factor_hbm, factor_ref), (proj_hbm, proj_ref), (present_hbm, present_ref),
        (mask_hbm, mask_ref), (occ_hbm, occ_ref)))]
    for load in small:
        load.start()
    blocks = pltpu.make_async_copy(coupling_hbm, cm_ref, cm_sem)

    barrier = pltpu.get_barrier_semaphore()
    greeted = [(plane_peer(step), col) for step in range(1, p)] + [(line_peer(step), col) for step in range(1, q)]
    greeted += [(row, other)]
    for target in greeted:
        pl.semaphore_signal(barrier, inc=1, device_id=target, device_id_type=MESH)
    length = ext.shape[1]
    edge = rows + HALO
    ext[:, edge:, :] = jnp.zeros((ext.shape[0], length - edge, 128), F32)
    pext[:, edge:, :] = jnp.zeros((2, length - edge, half), F32)
    low = (SUB - 1) * SUB
    skew[:, :, 0:low, :] = jnp.zeros((*skew.shape[:2], low, 128), F32)
    skew[:, :, low + K * SUB:, :] = jnp.zeros((*skew.shape[:2], low, 128), F32)
    pl.semaphore_wait(barrier, len(greeted))

    def remote(src, dst, sems, slot, target):
        return pltpu.make_async_remote_copy(
            src_ref=src, dst_ref=dst, send_sem=sems.at[(0,) + slot], recv_sem=sems.at[(1,) + slot],
            device_id=target, device_id_type=MESH)

    swap = remote(panel_hbm, pan_ref.at[col, body], pan_sems, (0,), (row, other))
    swap.start()
    count_copies = [
        remote(basis_hbm, counts.at[side], count_sems, (side,), (target, col))
        for side, target in ((0, up), (1, down))
    ]
    pan_halos, passed, vec_halos = [], [], []
    for side, target in ((0, up), (1, down)):
        src_at = rows - HALO if side == 0 else 0
        dst_at = 0 if side == 0 else HALO + rows
        pan_halos.append(remote(panel_hbm.at[pl.ds(src_at, HALO)], pan_ref.at[col, pl.ds(dst_at, HALO)],
                                pan_sems, (1 + side,), (target, col)))
        ghost = pan_ref.at[col, pl.ds(dst_at, HALO)]
        passed.append(remote(ghost, ghost, pan_sems, (3 + side,), (row, other)))
    far = jnp.where(row == n - 1, 0, 1)
    for side in (far, 1 - far):
        target = jnp.where(side == 0, up, down)
        src_at = (rows - HALO) * (1 - side)
        for piece in range(PIECES):
            part_at = piece * (HALO // PIECES)
            src = pl.ds(pl.multiple_of(src_at + part_at, HALO // PIECES), HALO // PIECES)
            vec_halos.append(remote(vec_hbm.at[src], halo_ref.at[side, pl.ds(part_at, HALO // PIECES)],
                                    halo_sems, (side, piece), (target, col)))

    own.wait()
    pan_t[pl.ds(pl.multiple_of(col * half, half), half), :] = pan_ref[col, body, :].T
    for load in small:
        load.wait()
    high = factor_ref[...].astype(BF16)
    factor_hi[...] = high
    factor_lo[...] = (factor_ref[...] - high.astype(F32)).astype(BF16)
    weight[...] = mask_ref[...].astype(F32) * occ_ref[...] / (vec_hbm.shape[1] * lax.axis_size("col"))
    for load in loads:
        load.wait()
    blocks.start()

    def span_of(c):
        return slice(c * wide_c, (c + 1) * wide_c)

    pairs = [(1, 2), (0, 3)] if chunks == 4 else [range(chunks)]

    def products(pair, which):
        mine = pl.ds(pl.multiple_of(which * half, half), half)
        columns = jnp.concatenate([vec[:, span_of(c)] for c in pair], axis=1)
        inner = jnp.dot(pan_t[mine, :], columns, preferred_element_type=F32).T.astype(BF16)
        for at, c in enumerate(pair):
            part[c, :, mine] = inner[at * wide_c:(at + 1) * wide_c]

    for pair in pairs:
        products(pair, col)
    swap.wait_recv()
    pan_t[pl.ds(pl.multiple_of(other * half, half), half), :] = pan_ref[other, body, :].T

    def first_copy(c, step):
        (size, at, peer), (size_s, _, _) = ways[c]
        length = size_s * unit
        src = pl.ds(pl.multiple_of(lax.rem(at + step, size) * length, unit), length)
        return remote(part.at[c, src], got_first.at[c, step, pl.ds(0, length)], ring_sems, (c, 0, step), (peer(step), col))

    def rounds(c):
        return range(ways[c][1][0].bit_length() - 1)

    def fold_copy(c, turn):
        _, (size, at, peer) = ways[c]
        reach = 1 << turn
        ahead = lax.rem(lax.div(at, reach), 2)
        step = reach + ahead * (size - 2 * reach)
        length = size * unit
        return remote(middle.at[c, turn, pl.ds(0, length)], got_second.at[c, turn, pl.ds(0, length)],
                      fold_sems, (c, turn), (peer(step), col))

    def own_block(c):
        (_, at, _), (size_s, _, _) = ways[c]
        return pl.multiple_of(c * wide_c + at * size_s * unit, unit)

    def last_copy(c, step):
        (_, _, peer), (size_s, _, _) = ways[c]
        mine = pl.ds(own_block(c), size_s * unit)
        return remote(mix_ref.at[mine], mix_ref.at[mine], ring_sems, (c, 1, step), (peer(step), col))

    def first_steps(c):
        return range(1, ways[c][0][0])

    def after_first(c):
        (_, at, _), (size_s, _, _) = ways[c]
        length = size_s * unit
        for step in first_steps(c):
            first_copy(c, step).wait_recv()
        total = part[c, pl.ds(pl.multiple_of(at * length, unit), length), :].astype(F32)
        for step in first_steps(c):
            total = total + got_first[c, step, 0:length, :].astype(F32)
        middle[c, 0, 0:length, :] = total.astype(BF16)
        fold_copy(c, 0).start()

    def after_fold(c, turn):
        length = ways[c][1][0] * unit
        fold_copy(c, turn).wait_recv()
        inner = middle[c, turn, 0:length, :].astype(F32) + got_second[c, turn, 0:length, :].astype(F32)
        top = inner.astype(BF16)
        if turn + 1 < len(rounds(c)):
            middle[c, turn + 1, 0:length, :] = top
            fold_copy(c, turn + 1).start()
            return
        rest = (inner - top.astype(F32)).astype(BF16)
        both = jnp.dot(jnp.concatenate([top, rest], axis=0), factor_hi[...], preferred_element_type=F32)
        mixed = both[0:length] + both[length:] + jnp.dot(top, factor_lo[...], preferred_element_type=F32)
        mix_ref[pl.ds(own_block(c), length), :] = mixed.astype(BF16)
        for step in first_steps(c):
            last_copy(c, step).start()

    def after_last(c):
        for step in first_steps(c):
            last_copy(c, step).wait_recv()

    def greet_neighbours():
        for copy in count_copies + pan_halos:
            copy.start()

    def pass_on():
        for copy in pan_halos:
            copy.wait_recv()
        for copy in passed:
            copy.start()

    def slow_halos(*which):
        pl.when(col == 0)(lambda: start_halos(*which))

    def fast_halos(*which):
        pl.when(col == 1)(lambda: start_halos(*which))

    def start_halos(*which):
        for piece in which:
            for copy in [vec_halos[i] for i in HALO_ORDER[2 * piece:2 * piece + 2]]:
                copy.start()

    for pair in pairs:
        products(pair, other)
        for c in pair:
            for step in first_steps(c):
                first_copy(c, step).start()

    lanes = [slice(c * 128, (c + 1) * 128) for c in range(ext.shape[0])]
    chunk_rows = rows // 8

    def widen(t, carry):
        at = pl.multiple_of(t * chunk_rows, 16)
        block = vec[pl.ds(at, chunk_rows), :].astype(F32)
        for c, span in enumerate(lanes):
            ext[c, pl.ds(HALO + at, chunk_rows), :] = block[:, span]
        return carry

    lax.fori_loop(0, 8, widen, 0)

    for which in (0, 1):
        pext[which, HALO:HALO + rows, :] = pan_ref[which, body, :].astype(F32)
    here = basis_ref[...].astype(F32)
    lower = jnp.where(iota(atoms, atoms, 0) < iota(atoms, atoms, 1), 1.0, 0.0).astype(BF16)
    at = iota(1, atoms, 1)

    def tables(prev, post, which):
        table = jnp.concatenate([prev, here, post, jnp.zeros((5, atoms), F32)], axis=0).astype(BF16)
        first = jnp.dot(table, lower, preferred_element_type=F32).astype(jnp.int32)
        first_ref[which] = jnp.clip(first + (HALO - rows) + rows * iota(8, atoms, 0), 0, rows + 2 * HALO)
        copy = pltpu.make_async_copy(first_ref.at[which], starts.at[which], start_sem.at[which])
        copy.start()
        lines = []
        for k in range(K):
            d = k - RIM
            near = here
            if d != 0:
                turn = (-d) % atoms
                inside = (at + d >= 0) & (at + d < atoms)
                near = jnp.where(inside, pltpu.roll(here, turn, 1), pltpu.roll(prev if d < 0 else post, turn, 1))
            lines.append(jnp.where(present_ref[k:k + 1, :] > 0, near, 0.0))
        lines.append(proj_ref[...].astype(F32))
        lines.append(jnp.zeros((atoms - K - 1, atoms), F32))
        limit[...] = jnp.concatenate(lines, axis=0).T
        return copy

    none = jnp.zeros((1, atoms), F32)
    begin_copy = tables(none, none, 0)
    blocks.wait()

    in_i = group_of(SUB, wide, 1, BMAX, NPMAX)
    slot = (iota(SUB, wide, 1) - BMAX * in_i).astype(F32)
    in_i = in_i.astype(F32)
    lane = iota(8, 128, 1)

    def band_piece(u, i):
        tiles = []
        for tile in range(WIN // 128):
            acc = None
            for b in range(REACH):
                to, last = max(b * BMAX, tile * 128), min((b + 1) * BMAX, (tile + 1) * 128)
                while to < last:
                    source = i * BMAX + to - b * BMAX
                    count = min(last - to, 128 - source % 128)
                    piece = skew[u, source // 128, pl.ds((REACH - 1 - b) * SUB, SUB, stride=SUB + 1), :]
                    turn = (to - source) % 128
                    piece = piece if turn == 0 else pltpu.roll(piece, turn, 1)
                    acc = piece if acc is None else jnp.where(lane >= to % 128, piece, acc)
                    to += count
            tiles.append(acc)
        return jnp.concatenate(tiles, axis=1)

    def band_step(t, carry):
        chunk = pl.ds(pl.multiple_of(t * GROUP, GROUP), GROUP)
        bounds = limit[chunk, :]
        for u in range(GROUP // SUB):
            within = bounds[u * SUB:(u + 1) * SUB]
            valid = in_i < within[:, K:K + 1]
            for k in range(K):
                block = cm_ref[k, chunk, :].astype(F32)[u * SUB:(u + 1) * SUB]
                block = jnp.where(valid & (slot < within[:, k:k + 1]), block, 0.0)
                top = (REACH - 1 - k) * SUB
                for tile in range(wide // 128):
                    skew[u, tile, top:top + SUB, :] = block[:, tile * 128:(tile + 1) * 128]
        for u in range(GROUP // SUB):
            for i in range(0, NPMAX, 2):
                both = jnp.concatenate([band_piece(u, i), band_piece(u, i + 1)], axis=0)
                band[t * (GROUP // SUB) + u, i * SUB:(i + 2) * SUB, :] = both.astype(BF16)
        return carry

    def gather(t, carry, which=0):
        at = pl.multiple_of(2 * t * BMAX, 16)
        begins = []
        for e in (0, 1):
            flat = 2 * t + e + atoms - RIM
            begins.append(starts[which, lax.div(flat, atoms), lax.rem(flat, atoms)])
        for c, span in enumerate(lanes):
            both = [ext[c, pl.ds(begin, BMAX), :] for begin in begins]
            padded[pl.ds(at, 2 * BMAX), span] = jnp.concatenate(both, axis=0).astype(BF16)
        for c in (0, 1):
            both = [pext[c, pl.ds(begin, BMAX), :] for begin in begins]
            ppadded[pl.ds(at, 2 * BMAX), c * half:(c + 1) * half] = jnp.concatenate(both, axis=0).astype(BF16)
        return carry

    def project(s, carry=0):
        at = pl.ds(pl.multiple_of(s * SUB * BMAX, 16), WIN)
        base[s] = jnp.dot(band[s], padded[at, :], preferred_element_type=F32)
        lean[s] = jnp.dot(band[s], ppadded[at, :], preferred_element_type=F32).astype(BF16)
        return carry

    def bands(low, high):
        lax.fori_loop(low, high, band_step, 0)

    def gathers(low, high):
        lax.fori_loop(low, high, gather, 0)

    def projects(*which):
        for s in which:
            project(s)

    begin_copy.wait()
    inside_from, inside_to = RIM // 2, (atoms + RIM) // 2
    inside_mid = (inside_from + inside_to) // 2
    late_copy = []

    def outer_bands():
        for copy in count_copies:
            copy.wait_recv()
        late_copy.append(tables(counts[0].astype(F32), counts[1].astype(F32), 1))
        lax.fori_loop(0, 2, lambda t, carry: band_step(t * (groups - 1), carry), 0)

    third = (groups - 2) // 3
    works = [functools.partial(bands, 1 + t * third, 1 + (t + 1) * third) for t in range(3)]
    works += [functools.partial(gathers, inside_from, inside_mid), functools.partial(gathers, inside_mid, inside_to)]
    subs = atoms // SUB
    works += [functools.partial(projects, s, s + 1) for s in range(2, subs - 2, 2)]
    works += [outer_bands, functools.partial(projects, 1, subs - 2)]
    if chunks == 4:
        order = [
            [],
            [(after_first, 1), (greet_neighbours,), (start_halos, 0)],
            [(after_first, 0)],
            [(after_fold, 1, 0), (after_first, 2), (after_first, 3), (start_halos, 1, 2)],
            [(after_fold, 0, 0)],
            [],
            [(after_fold, 2, 0), (start_halos, 3)],
            [(after_fold, 1, 1), (after_fold, 3, 0)],
            [],
            [(after_fold, 0, 1)],
            [(after_fold, 2, 1), (after_fold, 3, 1), (slow_halos, 4, 5), (pass_on,)],
            [(fast_halos, 4, 5)],
            [],
        ]
    else:
        every = range(chunks)
        order = [[], [(after_first, c) for c in every] + [(greet_neighbours,), (start_halos, *range(PIECES))]]
        order += [[(after_fold, c, turn) for c in every] for turn in range(len(rounds(0)))]
        order += [[] for _ in works[len(order):-1]] + [[(pass_on,)]]
    for work, events in zip(works, order, strict=True):
        work()
        for event in events:
            event[0](*event[1:])

    size = GROUP * NPMAX
    part_size = SUB * NPMAX
    row_at, lane_at = iota(size, size, 0), iota(size, size, 1)
    same = ((row_at >= part_size) == (lane_at >= part_size)) & ((row_at & (SUB - 1)) == (lane_at & (SUB - 1)))
    expand = jnp.where(group_of(size, size, 0, SUB, size // SUB) - jnp.where(row_at >= part_size, NPMAX, 0)
                       == (lane_at & (NPMAX - 1)), 1.0, 0.0).astype(BF16)
    owner = group_of(GROUP, size, 1, NPMAX, NPMAX)
    pair_of = range(GROUP // SUB)

    def tail(span, g):
        lines = jnp.concatenate([lean[g * len(pair_of) + u] for u in pair_of], axis=0)
        update = lax.dot_general(lines, mix_ref[span, :], across, preferred_element_type=F32)
        plain = jnp.concatenate([base[g * len(pair_of) + u, :, span] for u in pair_of], axis=0)
        rounded = (plain - update).astype(BF16)
        weighted = (rounded.astype(F32) * weight[:, span]).astype(BF16)
        return lax.dot_general(weighted, rounded, across, preferred_element_type=F32)

    def finish(product, g):
        kept = jnp.where(same, product, 0.0)
        top = kept.astype(BF16)
        rest = (kept - top.astype(F32)).astype(BF16)
        spread = jnp.dot(top, expand, preferred_element_type=F32) + jnp.dot(rest, expand, preferred_element_type=F32)
        result = jnp.zeros((GROUP, size), F32)
        for i in range(NPMAX):
            rows_of = [spread[u * part_size + i * SUB:u * part_size + (i + 1) * SUB, :] for u in pair_of]
            result = jnp.where(owner == i, jnp.concatenate(rows_of, axis=0), result)
        dens[pl.ds(pl.multiple_of(g * GROUP, GROUP), GROUP), :] = result

    cut = vec.shape[1] // 2
    first_half, second_half = slice(0, cut), slice(cut, 2 * cut)
    batch = max(d for d in (6, 3, 2, 1) if (groups - 2) % d == 0)

    def tail_first(span, t, carry, fresh=True):
        for e in range(batch):
            g = 1 + t * batch + e
            product = tail(span, g)
            full[g] = product if fresh else full[g] + product
        return carry

    def tail_second(t, carry):
        products = [full[1 + t * batch + e] + tail(second_half, 1 + t * batch + e) for e in range(batch)]
        for e, product in enumerate(products):
            finish(product, 1 + t * batch + e)
        return carry

    for c in (1, 0) if chunks == 4 else (0,):
        after_last(c)
        span = span_of(c) if chunks == 4 else first_half
        lax.fori_loop(0, (groups - 2) // batch, functools.partial(tail_first, span, fresh=c == 1 or chunks != 4), 0)
    for c in range(max(1, chunks // 2), chunks):
        after_last(c)
    lax.fori_loop(0, (groups - 2) // batch, tail_second, 0)
    share = own_ref.shape[0]
    inside = share - GROUP

    def den_copy(start, count, slot):
        src = pl.ds(pl.multiple_of(start, GROUP), count)
        dst = pl.ds(pl.multiple_of(start - other * share, GROUP), count)
        return remote(dens.at[src], got_ref.at[dst], den_sems, (slot,), (row, other))

    sent = [den_copy(other * share + GROUP * col, inside, 0), den_copy(other * (atoms - GROUP), GROUP, 1)]
    sent[0].start()

    for copy in pan_halos:
        copy.wait_send()
    for copy in passed + vec_halos:
        copy.wait()
    for side, at in ((0, 0), (1, HALO + rows)):
        block = halo_ref[side].astype(F32)
        for c, span in enumerate(lanes):
            ext[c, at:at + HALO, :] = block[:, span]
        for which in (0, 1):
            pext[which, at:at + HALO, :] = pan_ref[which, at:at + HALO, :].astype(F32)
    late_copy[0].wait()
    late_gather = functools.partial(gather, which=1)
    lax.fori_loop(0, RIM // 2, late_gather, 0)
    lax.fori_loop((atoms + RIM) // 2, (atoms + 2 * RIM) // 2, late_gather, 0)

    every = slice(0, 2 * cut)
    project(other * (subs - 1))
    theirs, ours = other * (groups - 1), col * (groups - 1)
    product = tail(every, theirs)
    project(col * (subs - 1))
    finish(product, theirs)
    sent[1].start()
    finish(tail(every, ours), ours)
    own_ref[...] = dens[pl.ds(pl.multiple_of(col * share, share), share), :]

    for copy in sent:
        copy.wait()
    swap.wait_send()
    for copy in count_copies:
        copy.wait_send()
    for c in range(chunks):
        for step in first_steps(c):
            first_copy(c, step).wait_send()
            last_copy(c, step).wait_send()
        for turn in rounds(c):
            fold_copy(c, turn).wait_send()


def vector_kernel(vin_ref, pan_ref, mix_ref, own_ref, got_ref, vec_hbm, den_ref, done, sems):
    tiles = sems.shape[0]
    tile = vin_ref.shape[0] // tiles
    den_ref[...] = own_ref[...] + got_ref[...]
    copies = []
    for t in range(tiles):
        at = slice(t * tile, (t + 1) * tile)
        inside = slice(HALO + t * tile, HALO + (t + 1) * tile)
        panel = jnp.concatenate([pan_ref[0, inside, :], pan_ref[1, inside, :]], axis=1)
        update = lax.dot_general(panel, mix_ref[...], (((1,), (1,)), ((), ())), preferred_element_type=F32)
        done[at, :] = (vin_ref[at, :].astype(F32) - update).astype(BF16)
        copies.append(pltpu.make_async_copy(done.at[at], vec_hbm.at[at], sems.at[t]))
        copies[-1].start()
    for copy in copies:
        copy.wait()


def local(vectors_in, panel, factor, atom_basis, proj_count, coupling, block_present, occ_mask, occ_weight):
    n = lax.axis_size("row")
    rows, cols = vectors_in.shape
    half = panel.shape[1]
    npan = factor.shape[0]
    atoms = atom_basis.shape[1]
    groups = atoms // GROUP
    share = atoms // lax.axis_size("col")
    wide = coupling.shape[2]
    vmem = pl.BlockSpec(memory_space=pltpu.VMEM)
    hbm = pl.BlockSpec(memory_space=pl.ANY)
    plane = max(d for d in range(1, n + 1) if n % d == 0 and d * d <= n)
    most, least = max(plane, n // plane), min(plane, n // plane)
    chunks = max(1, cols // (n * 16))
    width = cols // chunks
    unit = width // n
    turns = most.bit_length() - 1
    ext_rows = rows + 2 * HALO
    subs = atoms // SUB
    pad_rows = (subs - 1) * SUB * BMAX + WIN
    dma = pltpu.SemaphoreType.DMA
    operands = (vectors_in, panel, jnp.swapaxes(coupling, 0, 1), factor, atom_basis, proj_count[None, :], block_present.T,
                occ_mask[None, :], occ_weight[None, :])
    operands = [pltpu.with_memory_space_constraint(x, pltpu.HBM) for x in operands]
    vin, pan, mix, own, got = pl.pallas_call(
        functools.partial(mix_kernel, n, plane),
        out_shape=(
            jax.ShapeDtypeStruct((rows, cols), BF16),
            jax.ShapeDtypeStruct((2, ext_rows, half), BF16),
            jax.ShapeDtypeStruct((cols, npan), BF16),
            jax.ShapeDtypeStruct((share, NPMAX * NPMAX), F32),
            jax.ShapeDtypeStruct((share, NPMAX * NPMAX), F32),
        ),
        in_specs=[hbm] * 9,
        out_specs=(vmem,) * 5,
        scratch_shapes=[
            *[pltpu.VMEM(x.shape, x.dtype) for x in operands[3:]],
            pltpu.VMEM((npan, rows), BF16),
            pltpu.VMEM((chunks, width, npan), BF16),
            pltpu.VMEM((chunks, most, width // least, npan), BF16),
            pltpu.VMEM((chunks, turns, width // least, npan), BF16),
            pltpu.VMEM((chunks, turns, width // least, npan), BF16),
            pltpu.VMEM((npan, npan), BF16),
            pltpu.VMEM((npan, npan), BF16),
            pltpu.VMEM((2, 1, atoms), jnp.int32),
            pltpu.VMEM((atoms, atoms), F32),
            pltpu.VMEM((K, atoms, wide), BF16),
            pltpu.VMEM((2, HALO, cols), BF16),
            pltpu.VMEM((GROUP // SUB, wide // 128, (2 * SUB + K - 2) * SUB, 128), F32),
            pltpu.VMEM((subs, SUB * NPMAX, WIN), BF16),
            pltpu.VMEM((2, 8, atoms), jnp.int32),
            pltpu.SMEM((2, 8, atoms), jnp.int32),
            pltpu.VMEM((cols // 128, ext_rows + BMAX, 128), F32),
            pltpu.VMEM((2, ext_rows + BMAX, half), F32),
            pltpu.VMEM((pad_rows, cols), BF16),
            pltpu.VMEM((pad_rows, npan), BF16),
            pltpu.VMEM((subs, SUB * NPMAX, cols), F32),
            pltpu.VMEM((subs, SUB * NPMAX, npan), BF16),
            pltpu.VMEM((groups, GROUP * NPMAX, GROUP * NPMAX), F32),
            pltpu.VMEM((atoms, NPMAX * NPMAX), F32),
            pltpu.VMEM((1, cols), F32),
            dma((2,)), dma((6,)), dma, dma, dma((2,)), dma((2, 5)), dma((2, 2, PIECES)), dma((2, 2)),
            dma((2, chunks, 2, most)), dma((2, chunks, turns)), dma((2, 2)),
        ],
        compiler_params=pltpu.CompilerParams(collective_id=0, has_side_effects=True, vmem_limit_bytes=48 << 20),
        cost_estimate=pl.CostEstimate(flops=8 * 10**9, bytes_accessed=10 << 20, transcendentals=0),
    )(*operands)

    return pl.pallas_call(
        vector_kernel,
        out_shape=(
            jax.ShapeDtypeStruct((rows, cols), BF16),
            jax.ShapeDtypeStruct((share, NPMAX * NPMAX), F32),
        ),
        in_specs=[vmem] * 5,
        out_specs=[hbm, vmem],
        scratch_shapes=[pltpu.VMEM((rows, cols), BF16), dma((8,))],
        compiler_params=pltpu.CompilerParams(vmem_limit_bytes=16 << 20),
        cost_estimate=pl.CostEstimate(flops=6 * 10**9, bytes_accessed=10 << 20, transcendentals=0),
    )(vin, pan, mix, own, got)


def solution(mesh):
    placed = (
        P("row", "col"),
        P("row", "col"),
        P(),
        P("row", None),
        P("row"),
        P("row", None, None),
        P("row", None),
        P("col"),
        P("col"),
    )
    return jax.shard_map(
        local,
        mesh=mesh,
        in_specs=placed,
        out_specs=(P("row", "col"), P(("row", "col"), None)),
        check_vma=False,
    )
```

```python
import functools

import jax
import jax.numpy as jnp
from jax import lax
from jax.experimental import pallas as pl
from jax.experimental.pallas import tpu as pltpu
from jax.sharding import PartitionSpec as P

NPMAX = 16
BMAX = 24
K = 9
RIM = (K - 1) // 2
HALO = RIM * BMAX
PIECES = 6
HALO_ORDER = (0, 6, 1, 7, 2, 8, 3, 9, 4, 5, 10, 11)
GROUP = 16
SUB = 8
WIN = -(-(SUB + K - 1) * BMAX // 128) * 128
REACH = SUB + K - 1
F32 = jnp.float32
BF16 = jnp.bfloat16
MESH = pl.DeviceIdType.MESH


def iota(rows, columns, axis):
    return lax.broadcasted_iota(jnp.int32, (rows, columns), axis)


def group_of(rows, columns, axis, size, most):
    small = (8, columns) if axis == 1 else (rows, 128)
    index = iota(*small, axis)
    group = jnp.zeros(small, jnp.int32)
    for edge in range(1, most):
        group = group + jnp.where(index >= edge * size, 1, 0)
    return jnp.tile(group, (rows // small[0], columns // small[1]))


def mix_kernel(n, plane, vec_hbm, panel_hbm, coupling_hbm, factor_hbm, basis_hbm, proj_hbm, present_hbm, mask_hbm, occ_hbm,
               vec, pan_ref, mix_ref, own_ref, got_ref,
               factor_ref, basis_ref, proj_ref, present_ref, mask_ref, occ_ref,
               pan_t, part, got_first, middle, got_second, factor_hi, factor_lo, counts, limit, cm_ref, halo_ref, skew, band,
               first_ref, starts, ext, pext, padded, ppadded, base, lean, full, dens, weight,
               load_sem, small_sem, own_sem, cm_sem, start_sem, pan_sems, halo_sems, count_sems, ring_sems, fold_sems, den_sems):
    row, col = lax.axis_index("row"), lax.axis_index("col")
    other = 1 - col
    up, down = lax.rem(row + 1, n), lax.rem(row + n - 1, n)
    rows, half = panel_hbm.shape
    chunks, wide_c, npan = part.shape
    unit = wide_c // n
    atoms, wide = cm_ref.shape[1:]
    groups = atoms // GROUP
    body = pl.ds(HALO, rows)
    q, p = n // plane, plane
    line, spot = lax.div(row, p), lax.rem(row, p)
    contract = (((0,), (0,)), ((), ()))
    across = (((1,), (1,)), ((), ()))

    def plane_peer(step):
        return line * p + lax.rem(spot + step, p)

    def line_peer(step):
        return lax.rem(line + step, q) * p + spot

    by_plane, by_line = (p, spot, plane_peer), (q, line, line_peer)
    ways = [(by_line, by_plane) if chunks == 4 and c == 2 else (by_plane, by_line) for c in range(chunks)]

    own = pltpu.make_async_copy(panel_hbm, pan_ref.at[col, body], own_sem)
    own.start()
    pieces = rows // load_sem.shape[0]
    loads = [pltpu.make_async_copy(vec_hbm.at[pl.ds(i * pieces, pieces)], vec.at[pl.ds(i * pieces, pieces)], load_sem.at[i])
             for i in range(load_sem.shape[0])]
    for load in loads:
        load.start()
    small = [pltpu.make_async_copy(src, dst, small_sem.at[i]) for i, (src, dst) in enumerate((
        (basis_hbm, basis_ref), (factor_hbm, factor_ref), (proj_hbm, proj_ref), (present_hbm, present_ref),
        (mask_hbm, mask_ref), (occ_hbm, occ_ref)))]
    for load in small:
        load.start()
    blocks = pltpu.make_async_copy(coupling_hbm, cm_ref, cm_sem)

    barrier = pltpu.get_barrier_semaphore()
    greeted = [(plane_peer(step), col) for step in range(1, p)] + [(line_peer(step), col) for step in range(1, q)]
    greeted += [(row, other)]
    for target in greeted:
        pl.semaphore_signal(barrier, inc=1, device_id=target, device_id_type=MESH)
    length = ext.shape[1]
    edge = rows + HALO
    ext[:, edge:, :] = jnp.zeros((ext.shape[0], length - edge, 128), F32)
    pext[:, edge:, :] = jnp.zeros((2, length - edge, half), F32)
    low = (SUB - 1) * SUB
    skew[:, :, 0:low, :] = jnp.zeros((*skew.shape[:2], low, 128), F32)
    skew[:, :, low + K * SUB:, :] = jnp.zeros((*skew.shape[:2], low, 128), F32)
    pl.semaphore_wait(barrier, len(greeted))

    def remote(src, dst, sems, slot, target):
        return pltpu.make_async_remote_copy(
            src_ref=src, dst_ref=dst, send_sem=sems.at[(0,) + slot], recv_sem=sems.at[(1,) + slot],
            device_id=target, device_id_type=MESH)

    swap = remote(panel_hbm, pan_ref.at[col, body], pan_sems, (0,), (row, other))
    swap.start()
    count_copies = [
        remote(basis_hbm, counts.at[side], count_sems, (side,), (target, col))
        for side, target in ((0, up), (1, down))
    ]
    pan_halos, passed, vec_halos = [], [], []
    for side, target in ((0, up), (1, down)):
        src_at = rows - HALO if side == 0 else 0
        dst_at = 0 if side == 0 else HALO + rows
        pan_halos.append(remote(panel_hbm.at[pl.ds(src_at, HALO)], pan_ref.at[col, pl.ds(dst_at, HALO)],
                                pan_sems, (1 + side,), (target, col)))
        ghost = pan_ref.at[col, pl.ds(dst_at, HALO)]
        passed.append(remote(ghost, ghost, pan_sems, (3 + side,), (row, other)))
    far = jnp.where(row == n - 1, 0, 1)
    for side in (far, 1 - far):
        target = jnp.where(side == 0, up, down)
        src_at = (rows - HALO) * (1 - side)
        for piece in range(PIECES):
            part_at = piece * (HALO // PIECES)
            src = pl.ds(pl.multiple_of(src_at + part_at, HALO // PIECES), HALO // PIECES)
            vec_halos.append(remote(vec_hbm.at[src], halo_ref.at[side, pl.ds(part_at, HALO // PIECES)],
                                    halo_sems, (side, piece), (target, col)))

    own.wait()
    pan_t[pl.ds(pl.multiple_of(col * half, half), half), :] = pan_ref[col, body, :].T
    for load in small:
        load.wait()
    high = factor_ref[...].astype(BF16)
    factor_hi[...] = high
    factor_lo[...] = (factor_ref[...] - high.astype(F32)).astype(BF16)
    weight[...] = mask_ref[...].astype(F32) * occ_ref[...] / (vec_hbm.shape[1] * lax.axis_size("col"))
    for load in loads:
        load.wait()
    blocks.start()

    def span_of(c):
        return slice(c * wide_c, (c + 1) * wide_c)

    pairs = [(1, 2), (0, 3)] if chunks == 4 else [range(chunks)]

    def products(pair, which):
        mine = pl.ds(pl.multiple_of(which * half, half), half)
        columns = jnp.concatenate([vec[:, span_of(c)] for c in pair], axis=1)
        inner = jnp.dot(pan_t[mine, :], columns, preferred_element_type=F32).T.astype(BF16)
        for at, c in enumerate(pair):
            part[c, :, mine] = inner[at * wide_c:(at + 1) * wide_c]

    for pair in pairs:
        products(pair, col)
    swap.wait_recv()
    pan_t[pl.ds(pl.multiple_of(other * half, half), half), :] = pan_ref[other, body, :].T

    def first_copy(c, step):
        (size, at, peer), (size_s, _, _) = ways[c]
        length = size_s * unit
        src = pl.ds(pl.multiple_of(lax.rem(at + step, size) * length, unit), length)
        return remote(part.at[c, src], got_first.at[c, step, pl.ds(0, length)], ring_sems, (c, 0, step), (peer(step), col))

    def rounds(c):
        return range(ways[c][1][0].bit_length() - 1)

    def fold_copy(c, turn):
        _, (size, at, peer) = ways[c]
        reach = 1 << turn
        ahead = lax.rem(lax.div(at, reach), 2)
        step = reach + ahead * (size - 2 * reach)
        length = size * unit
        return remote(middle.at[c, turn, pl.ds(0, length)], got_second.at[c, turn, pl.ds(0, length)],
                      fold_sems, (c, turn), (peer(step), col))

    def own_block(c):
        (_, at, _), (size_s, _, _) = ways[c]
        return pl.multiple_of(c * wide_c + at * size_s * unit, unit)

    def last_copy(c, step):
        (_, _, peer), (size_s, _, _) = ways[c]
        mine = pl.ds(own_block(c), size_s * unit)
        return remote(mix_ref.at[mine], mix_ref.at[mine], ring_sems, (c, 1, step), (peer(step), col))

    def first_steps(c):
        return range(1, ways[c][0][0])

    def after_first(c):
        (_, at, _), (size_s, _, _) = ways[c]
        length = size_s * unit
        for step in first_steps(c):
            first_copy(c, step).wait_recv()
        total = part[c, pl.ds(pl.multiple_of(at * length, unit), length), :].astype(F32)
        for step in first_steps(c):
            total = total + got_first[c, step, 0:length, :].astype(F32)
        middle[c, 0, 0:length, :] = total.astype(BF16)
        fold_copy(c, 0).start()

    def after_fold(c, turn):
        length = ways[c][1][0] * unit
        fold_copy(c, turn).wait_recv()
        inner = middle[c, turn, 0:length, :].astype(F32) + got_second[c, turn, 0:length, :].astype(F32)
        top = inner.astype(BF16)
        if turn + 1 < len(rounds(c)):
            middle[c, turn + 1, 0:length, :] = top
            fold_copy(c, turn + 1).start()
            return
        rest = (inner - top.astype(F32)).astype(BF16)
        both = jnp.dot(jnp.concatenate([top, rest], axis=0), factor_hi[...], preferred_element_type=F32)
        mixed = both[0:length] + both[length:] + jnp.dot(top, factor_lo[...], preferred_element_type=F32)
        mix_ref[pl.ds(own_block(c), length), :] = mixed.astype(BF16)
        for step in first_steps(c):
            last_copy(c, step).start()

    def after_last(c):
        for step in first_steps(c):
            last_copy(c, step).wait_recv()

    def greet_neighbours():
        for copy in count_copies + pan_halos:
            copy.start()

    def pass_on():
        for copy in pan_halos:
            copy.wait_recv()
        for copy in passed:
            copy.start()

    def slow_halos(*which):
        pl.when(col == 0)(lambda: start_halos(*which))

    def fast_halos(*which):
        pl.when(col == 1)(lambda: start_halos(*which))

    def start_halos(*which):
        for piece in which:
            for copy in [vec_halos[i] for i in HALO_ORDER[2 * piece:2 * piece + 2]]:
                copy.start()

    for pair in pairs:
        products(pair, other)
        for c in pair:
            for step in first_steps(c):
                first_copy(c, step).start()

    lanes = [slice(c * 128, (c + 1) * 128) for c in range(ext.shape[0])]
    chunk_rows = rows // 8

    def widen(t, carry):
        at = pl.multiple_of(t * chunk_rows, 16)
        block = vec[pl.ds(at, chunk_rows), :].astype(F32)
        for c, span in enumerate(lanes):
            ext[c, pl.ds(HALO + at, chunk_rows), :] = block[:, span]
        return carry

    lax.fori_loop(0, 8, widen, 0)

    for which in (0, 1):
        pext[which, HALO:HALO + rows, :] = pan_ref[which, body, :].astype(F32)
    here = basis_ref[...].astype(F32)
    lower = jnp.where(iota(atoms, atoms, 0) < iota(atoms, atoms, 1), 1.0, 0.0).astype(BF16)
    at = iota(1, atoms, 1)

    def tables(prev, post, which):
        table = jnp.concatenate([prev, here, post, jnp.zeros((5, atoms), F32)], axis=0).astype(BF16)
        first = jnp.dot(table, lower, preferred_element_type=F32).astype(jnp.int32)
        first_ref[which] = jnp.clip(first + (HALO - rows) + rows * iota(8, atoms, 0), 0, rows + 2 * HALO)
        copy = pltpu.make_async_copy(first_ref.at[which], starts.at[which], start_sem.at[which])
        copy.start()
        lines = []
        for k in range(K):
            d = k - RIM
            near = here
            if d != 0:
                turn = (-d) % atoms
                inside = (at + d >= 0) & (at + d < atoms)
                near = jnp.where(inside, pltpu.roll(here, turn, 1), pltpu.roll(prev if d < 0 else post, turn, 1))
            lines.append(jnp.where(present_ref[k:k + 1, :] > 0, near, 0.0))
        lines.append(proj_ref[...].astype(F32))
        lines.append(jnp.zeros((atoms - K - 1, atoms), F32))
        limit[...] = jnp.concatenate(lines, axis=0).T
        return copy

    none = jnp.zeros((1, atoms), F32)
    begin_copy = tables(none, none, 0)
    blocks.wait()

    in_i = group_of(SUB, wide, 1, BMAX, NPMAX)
    slot = (iota(SUB, wide, 1) - BMAX * in_i).astype(F32)
    in_i = in_i.astype(F32)
    lane = iota(8, 128, 1)

    def band_piece(u, i):
        tiles = []
        for tile in range(WIN // 128):
            acc = None
            for b in range(REACH):
                to, last = max(b * BMAX, tile * 128), min((b + 1) * BMAX, (tile + 1) * 128)
                while to < last:
                    source = i * BMAX + to - b * BMAX
                    count = min(last - to, 128 - source % 128)
                    piece = skew[u, source // 128, pl.ds((REACH - 1 - b) * SUB, SUB, stride=SUB + 1), :]
                    turn = (to - source) % 128
                    piece = piece if turn == 0 else pltpu.roll(piece, turn, 1)
                    acc = piece if acc is None else jnp.where(lane >= to % 128, piece, acc)
                    to += count
            tiles.append(acc)
        return jnp.concatenate(tiles, axis=1)

    def band_step(t, carry):
        chunk = pl.ds(pl.multiple_of(t * GROUP, GROUP), GROUP)
        bounds = limit[chunk, :]
        for u in range(GROUP // SUB):
            within = bounds[u * SUB:(u + 1) * SUB]
            valid = in_i < within[:, K:K + 1]
            for k in range(K):
                block = cm_ref[k, chunk, :].astype(F32)[u * SUB:(u + 1) * SUB]
                block = jnp.where(valid & (slot < within[:, k:k + 1]), block, 0.0)
                top = (REACH - 1 - k) * SUB
                for tile in range(wide // 128):
                    skew[u, tile, top:top + SUB, :] = block[:, tile * 128:(tile + 1) * 128]
        for u in range(GROUP // SUB):
            for i in range(0, NPMAX, 2):
                both = jnp.concatenate([band_piece(u, i), band_piece(u, i + 1)], axis=0)
                band[t * (GROUP // SUB) + u, i * SUB:(i + 2) * SUB, :] = both.astype(BF16)
        return carry

    def gather(t, carry, which=0):
        at = pl.multiple_of(2 * t * BMAX, 16)
        begins = []
        for e in (0, 1):
            flat = 2 * t + e + atoms - RIM
            begins.append(starts[which, lax.div(flat, atoms), lax.rem(flat, atoms)])
        for c, span in enumerate(lanes):
            both = [ext[c, pl.ds(begin, BMAX), :] for begin in begins]
            padded[pl.ds(at, 2 * BMAX), span] = jnp.concatenate(both, axis=0).astype(BF16)
        for c in (0, 1):
            both = [pext[c, pl.ds(begin, BMAX), :] for begin in begins]
            ppadded[pl.ds(at, 2 * BMAX), c * half:(c + 1) * half] = jnp.concatenate(both, axis=0).astype(BF16)
        return carry

    def project(s, carry=0):
        at = pl.ds(pl.multiple_of(s * SUB * BMAX, 16), WIN)
        base[s] = jnp.dot(band[s], padded[at, :], preferred_element_type=F32)
        lean[s] = jnp.dot(band[s], ppadded[at, :], preferred_element_type=F32).astype(BF16)
        return carry

    def bands(low, high):
        lax.fori_loop(low, high, band_step, 0)

    def gathers(low, high):
        lax.fori_loop(low, high, gather, 0)

    def projects(*which):
        for s in which:
            project(s)

    begin_copy.wait()
    inside_from, inside_to = RIM // 2, (atoms + RIM) // 2
    inside_mid = (inside_from + inside_to) // 2
    late_copy = []

    def outer_bands():
        for copy in count_copies:
            copy.wait_recv()
        late_copy.append(tables(counts[0].astype(F32), counts[1].astype(F32), 1))
        lax.fori_loop(0, 2, lambda t, carry: band_step(t * (groups - 1), carry), 0)

    third = (groups - 2) // 3
    works = [functools.partial(bands, 1 + t * third, 1 + (t + 1) * third) for t in range(3)]
    works += [functools.partial(gathers, inside_from, inside_mid), functools.partial(gathers, inside_mid, inside_to)]
    subs = atoms // SUB
    works += [functools.partial(projects, s, s + 1) for s in range(2, subs - 2, 2)]
    works += [outer_bands, functools.partial(projects, 1, subs - 2)]
    if chunks == 4:
        order = [
            [],
            [(after_first, 1), (greet_neighbours,), (start_halos, 0)],
            [(after_first, 0)],
            [(after_fold, 1, 0), (after_first, 2), (after_first, 3), (start_halos, 1, 2)],
            [(after_fold, 0, 0)],
            [],
            [(after_fold, 2, 0), (start_halos, 3)],
            [(after_fold, 1, 1), (after_fold, 3, 0)],
            [],
            [(after_fold, 0, 1)],
            [(after_fold, 2, 1), (after_fold, 3, 1), (slow_halos, 4, 5), (pass_on,)],
            [],
            [(fast_halos, 4, 5)],
        ]
    else:
        every = range(chunks)
        order = [[], [(after_first, c) for c in every] + [(greet_neighbours,), (start_halos, *range(PIECES))]]
        order += [[(after_fold, c, turn) for c in every] for turn in range(len(rounds(0)))]
        order += [[] for _ in works[len(order):-1]] + [[(pass_on,)]]
    for work, events in zip(works, order, strict=True):
        work()
        for event in events:
            event[0](*event[1:])

    size = GROUP * NPMAX
    part_size = SUB * NPMAX
    row_at, lane_at = iota(size, size, 0), iota(size, size, 1)
    same = ((row_at >= part_size) == (lane_at >= part_size)) & ((row_at & (SUB - 1)) == (lane_at & (SUB - 1)))
    expand = jnp.where(group_of(size, size, 0, SUB, size // SUB) - jnp.where(row_at >= part_size, NPMAX, 0)
                       == (lane_at & (NPMAX - 1)), 1.0, 0.0).astype(BF16)
    owner = group_of(GROUP, size, 1, NPMAX, NPMAX)
    pair_of = range(GROUP // SUB)

    def tail(span, g):
        lines = jnp.concatenate([lean[g * len(pair_of) + u] for u in pair_of], axis=0)
        update = lax.dot_general(lines, mix_ref[span, :], across, preferred_element_type=F32)
        plain = jnp.concatenate([base[g * len(pair_of) + u, :, span] for u in pair_of], axis=0)
        rounded = (plain - update).astype(BF16)
        weighted = (rounded.astype(F32) * weight[:, span]).astype(BF16)
        return lax.dot_general(weighted, rounded, across, preferred_element_type=F32)

    def finish(product, g):
        kept = jnp.where(same, product, 0.0)
        top = kept.astype(BF16)
        rest = (kept - top.astype(F32)).astype(BF16)
        spread = jnp.dot(top, expand, preferred_element_type=F32) + jnp.dot(rest, expand, preferred_element_type=F32)
        result = jnp.zeros((GROUP, size), F32)
        for i in range(NPMAX):
            rows_of = [spread[u * part_size + i * SUB:u * part_size + (i + 1) * SUB, :] for u in pair_of]
            result = jnp.where(owner == i, jnp.concatenate(rows_of, axis=0), result)
        dens[pl.ds(pl.multiple_of(g * GROUP, GROUP), GROUP), :] = result

    cut = vec.shape[1] // 2
    first_half, second_half = slice(0, cut), slice(cut, 2 * cut)
    batch = max(d for d in (6, 3, 2, 1) if (groups - 2) % d == 0)

    def tail_first(span, t, carry, fresh=True):
        for e in range(batch):
            g = 1 + t * batch + e
            product = tail(span, g)
            full[g] = product if fresh else full[g] + product
        return carry

    def tail_second(t, carry):
        products = [full[1 + t * batch + e] + tail(second_half, 1 + t * batch + e) for e in range(batch)]
        for e, product in enumerate(products):
            finish(product, 1 + t * batch + e)
        return carry

    for c in (1, 0) if chunks == 4 else (0,):
        after_last(c)
        span = span_of(c) if chunks == 4 else first_half
        lax.fori_loop(0, (groups - 2) // batch, functools.partial(tail_first, span, fresh=c == 1 or chunks != 4), 0)
    for c in range(max(1, chunks // 2), chunks):
        after_last(c)
    lax.fori_loop(0, (groups - 2) // batch, tail_second, 0)
    share = own_ref.shape[0]
    inside = share - GROUP

    def den_copy(start, count, slot):
        src = pl.ds(pl.multiple_of(start, GROUP), count)
        dst = pl.ds(pl.multiple_of(start - other * share, GROUP), count)
        return remote(dens.at[src], got_ref.at[dst], den_sems, (slot,), (row, other))

    sent = [den_copy(other * share + GROUP * col, inside, 0), den_copy(other * (atoms - GROUP), GROUP, 1)]
    sent[0].start()

    for copy in pan_halos:
        copy.wait_send()
    for copy in passed + vec_halos:
        copy.wait()
    for side, at in ((0, 0), (1, HALO + rows)):
        block = halo_ref[side].astype(F32)
        for c, span in enumerate(lanes):
            ext[c, at:at + HALO, :] = block[:, span]
        for which in (0, 1):
            pext[which, at:at + HALO, :] = pan_ref[which, at:at + HALO, :].astype(F32)
    late_copy[0].wait()
    late_gather = functools.partial(gather, which=1)
    lax.fori_loop(0, RIM // 2, late_gather, 0)
    lax.fori_loop((atoms + RIM) // 2, (atoms + 2 * RIM) // 2, late_gather, 0)

    every = slice(0, 2 * cut)
    project(other * (subs - 1))
    theirs, ours = other * (groups - 1), col * (groups - 1)
    product = tail(every, theirs)
    project(col * (subs - 1))
    finish(product, theirs)
    sent[1].start()
    finish(tail(every, ours), ours)
    own_ref[...] = dens[pl.ds(pl.multiple_of(col * share, share), share), :]

    for copy in sent:
        copy.wait()
    swap.wait_send()
    for copy in count_copies:
        copy.wait_send()
    for c in range(chunks):
        for step in first_steps(c):
            first_copy(c, step).wait_send()
            last_copy(c, step).wait_send()
        for turn in rounds(c):
            fold_copy(c, turn).wait_send()


def vector_kernel(vin_ref, pan_ref, mix_ref, own_ref, got_ref, vec_hbm, den_ref, done, sems):
    tiles = sems.shape[0]
    tile = vin_ref.shape[0] // tiles
    den_ref[...] = own_ref[...] + got_ref[...]
    copies = []
    for t in range(tiles):
        at = slice(t * tile, (t + 1) * tile)
        inside = slice(HALO + t * tile, HALO + (t + 1) * tile)
        panel = jnp.concatenate([pan_ref[0, inside, :], pan_ref[1, inside, :]], axis=1)
        update = lax.dot_general(panel, mix_ref[...], (((1,), (1,)), ((), ())), preferred_element_type=F32)
        done[at, :] = (vin_ref[at, :].astype(F32) - update).astype(BF16)
        copies.append(pltpu.make_async_copy(done.at[at], vec_hbm.at[at], sems.at[t]))
        copies[-1].start()
    for copy in copies:
        copy.wait()


def local(vectors_in, panel, factor, atom_basis, proj_count, coupling, block_present, occ_mask, occ_weight):
    n = lax.axis_size("row")
    rows, cols = vectors_in.shape
    half = panel.shape[1]
    npan = factor.shape[0]
    atoms = atom_basis.shape[1]
    groups = atoms // GROUP
    share = atoms // lax.axis_size("col")
    wide = coupling.shape[2]
    vmem = pl.BlockSpec(memory_space=pltpu.VMEM)
    hbm = pl.BlockSpec(memory_space=pl.ANY)
    plane = max(d for d in range(1, n + 1) if n % d == 0 and d * d <= n)
    most, least = max(plane, n // plane), min(plane, n // plane)
    chunks = max(1, cols // (n * 16))
    width = cols // chunks
    unit = width // n
    turns = most.bit_length() - 1
    ext_rows = rows + 2 * HALO
    subs = atoms // SUB
    pad_rows = (subs - 1) * SUB * BMAX + WIN
    dma = pltpu.SemaphoreType.DMA
    operands = (vectors_in, panel, jnp.swapaxes(coupling, 0, 1), factor, atom_basis, proj_count[None, :], block_present.T,
                occ_mask[None, :], occ_weight[None, :])
    operands = [pltpu.with_memory_space_constraint(x, pltpu.HBM) for x in operands]
    vin, pan, mix, own, got = pl.pallas_call(
        functools.partial(mix_kernel, n, plane),
        out_shape=(
            jax.ShapeDtypeStruct((rows, cols), BF16),
            jax.ShapeDtypeStruct((2, ext_rows, half), BF16),
            jax.ShapeDtypeStruct((cols, npan), BF16),
            jax.ShapeDtypeStruct((share, NPMAX * NPMAX), F32),
            jax.ShapeDtypeStruct((share, NPMAX * NPMAX), F32),
        ),
        in_specs=[hbm] * 9,
        out_specs=(vmem,) * 5,
        scratch_shapes=[
            *[pltpu.VMEM(x.shape, x.dtype) for x in operands[3:]],
            pltpu.VMEM((npan, rows), BF16),
            pltpu.VMEM((chunks, width, npan), BF16),
            pltpu.VMEM((chunks, most, width // least, npan), BF16),
            pltpu.VMEM((chunks, turns, width // least, npan), BF16),
            pltpu.VMEM((chunks, turns, width // least, npan), BF16),
            pltpu.VMEM((npan, npan), BF16),
            pltpu.VMEM((npan, npan), BF16),
            pltpu.VMEM((2, 1, atoms), jnp.int32),
            pltpu.VMEM((atoms, atoms), F32),
            pltpu.VMEM((K, atoms, wide), BF16),
            pltpu.VMEM((2, HALO, cols), BF16),
            pltpu.VMEM((GROUP // SUB, wide // 128, (2 * SUB + K - 2) * SUB, 128), F32),
            pltpu.VMEM((subs, SUB * NPMAX, WIN), BF16),
            pltpu.VMEM((2, 8, atoms), jnp.int32),
            pltpu.SMEM((2, 8, atoms), jnp.int32),
            pltpu.VMEM((cols // 128, ext_rows + BMAX, 128), F32),
            pltpu.VMEM((2, ext_rows + BMAX, half), F32),
            pltpu.VMEM((pad_rows, cols), BF16),
            pltpu.VMEM((pad_rows, npan), BF16),
            pltpu.VMEM((subs, SUB * NPMAX, cols), F32),
            pltpu.VMEM((subs, SUB * NPMAX, npan), BF16),
            pltpu.VMEM((groups, GROUP * NPMAX, GROUP * NPMAX), F32),
            pltpu.VMEM((atoms, NPMAX * NPMAX), F32),
            pltpu.VMEM((1, cols), F32),
            dma((2,)), dma((6,)), dma, dma, dma((2,)), dma((2, 5)), dma((2, 2, PIECES)), dma((2, 2)),
            dma((2, chunks, 2, most)), dma((2, chunks, turns)), dma((2, 2)),
        ],
        compiler_params=pltpu.CompilerParams(collective_id=0, has_side_effects=True, vmem_limit_bytes=48 << 20),
        cost_estimate=pl.CostEstimate(flops=8 * 10**9, bytes_accessed=10 << 20, transcendentals=0),
    )(*operands)

    return pl.pallas_call(
        vector_kernel,
        out_shape=(
            jax.ShapeDtypeStruct((rows, cols), BF16),
            jax.ShapeDtypeStruct((share, NPMAX * NPMAX), F32),
        ),
        in_specs=[vmem] * 5,
        out_specs=[hbm, vmem],
        scratch_shapes=[pltpu.VMEM((rows, cols), BF16), dma((8,))],
        compiler_params=pltpu.CompilerParams(vmem_limit_bytes=16 << 20),
        cost_estimate=pl.CostEstimate(flops=6 * 10**9, bytes_accessed=10 << 20, transcendentals=0),
    )(vin, pan, mix, own, got)


def solution(mesh):
    placed = (
        P("row", "col"),
        P("row", "col"),
        P(),
        P("row", None),
        P("row"),
        P("row", None, None),
        P("row", None),
        P("col"),
        P("col"),
    )
    return jax.shard_map(
        local,
        mesh=mesh,
        in_specs=placed,
        out_specs=(P("row", "col"), P(("row", "col"), None)),
        check_vma=False,
    )
```
